32 devices in a mesh: dp: 8 (over z, y), seq: 4 (over x, core).
Axes of the slice: x: 2, y: 2, z: 4, core: 2. Of those that a mesh axis runs over, the one named last changes fastest.
Arguments:
- block_in: bfloat16 [16, 1024, 512], P('dp', 'seq'), may hold values from -6 to 6
- cotangent: bfloat16 [16, 1024, 512], P('dp', 'seq'), may hold values from -6 to 6
- ln_gain: float32 [512], P('dp'), may hold values from 0.5 to 1.5
- ln_bias: float32 [512], P('dp'), may hold values from -3 to 3
- lambda_log: float32 [64], P('dp'), may hold values from -1 to 0.3
- lambda_imag: float32 [64], P('dp'), may hold values from -30 to 30
- dss_weight: float32 [2, 64, 512], P(None, None, 'dp'), may hold values from -1.5 to 1.5
- log_step: float32 [512], P('dp'), may hold values from -8 to -2
- skip_gain: float32 [512], P('dp'), may hold values from -4 to 4
- lin_weight: bfloat16 [512, 1024], P(None, 'dp'), may hold values from -0.5 to 0.5
- lin_bias: float32 [1024], P('dp'), may hold values from -3 to 3
- doc_lengths: int32 [16, 4], P('dp'), may hold values from 1 to 800, 1024 in all within a row
Outputs:
- block_out: bfloat16 [16, 1024, 512], P('dp', 'seq')
- grad_block_in: bfloat16 [16, 1024, 512], P('dp', 'seq')
- grad_ln_gain: float32 [512], P('dp')
- grad_ln_bias: float32 [512], P('dp')
- grad_lambda_log: float32 [64], P('dp')
- grad_lambda_imag: float32 [64], P('dp')
- grad_dss_weight: float32 [2, 64, 512], P(None, None, 'dp')
- grad_log_step: float32 [512], P('dp')
- grad_skip_gain: float32 [512], P('dp')
- grad_lin_weight: float32 [512, 1024], P(None, 'dp')
- grad_lin_bias: float32 [1024], P('dp')
The draws below stay inside these ranges and needn't reach their ends.
Inputs may be any that keep to these rules, and one draw needn't show every extreme that they name: `doc_lengths`: each row sums to 1024.
All inputs are finite; a program needn't handle non-finite values.
Results may differ from the reference program's by a relative error of at most 0.0076.
Values may be sent and summed in bfloat16 or wider, within the bound.
No kernel may reach another device: no remote copies, remote signals or barrier semaphores. Data moves between devices by JAX's collectives and lax.ppermute only.
A program may use at most 448 MiB of HBM per device.

```python
import math
import jax
import jax.numpy as jnp
import numpy as np
from jax import lax

D = 512
N = 64
LEN = 1024
DOCS = 4
DOCMAX = 800
SEQS = 16


def draw_log_step(key, part):
    return jax.random.uniform(key, (D,), jnp.float32, -8.0, -2.0)


def steps_of(key, shape, pieces, least, high):
    factor_of, own = 1.0, jax.random.fold_in(key, 6)
    for dim, shards_of in pieces:
        draws = jnp.exp(jax.random.uniform(jax.random.fold_in(own, dim), (shards_of,), jnp.float32, least / len(pieces), high / len(pieces)))
        factor_of = factor_of * jnp.repeat(draws, shape[dim] // shards_of).reshape([-1 if axis == dim else 1 for axis in range(len(shape))])
    return factor_of


def length_profile(amount, total, reach, lean):
    portions = [(1 << 20) // math.isqrt(standing ** lean) + 1 for standing in range(2, amount + 1)]
    spare, given = total - reach - (amount - 1), [1] * (amount - 1)
    while spare > 0:
        candidates = [i for i in range(amount - 1) if given[i] < reach]
        mass, left = sum([portions[i] for i in candidates]), spare
        for i in candidates:
            more = min(reach - given[i], max(1, left * portions[i] // mass), spare)
            given[i] = given[i] + more
            spare = spare - more
    return np.array([reach] + given)


def ragged_sizes(rng, number_of, total, limit, skew):
    if number_of == 2:
        one = jax.random.randint(rng, (), max(1, total - limit), min(limit, total - 1) + 1)
        return jnp.stack([one, total - one])
    sizes = jnp.asarray(length_profile(number_of, total, limit, skew), jnp.int32)
    twos = (number_of - 1) // 2
    giver, taker = sizes[1:1 + 2 * twos:2], sizes[2:2 + 2 * twos:2]
    room = jnp.minimum(giver - 1, limit - taker)
    moved = jax.random.randint(jax.random.fold_in(rng, 1), (twos,), 0, 1 << 20) % (room + 1)
    sizes = sizes.at[1:1 + 2 * twos:2].set(giver - moved).at[2:2 + 2 * twos:2].set(taker + moved)
    return sizes[jax.random.permutation(jax.random.fold_in(rng, 2), number_of)]


def normal_values(key, shape, width, most, pieces=(), kind=jnp.bfloat16):
    gain = steps_of(key, shape, pieces, -0.22, 0.18) if pieces else 1.0
    values = jax.random.normal(key, shape, jnp.float32) * width * gain
    return jnp.minimum(jnp.maximum(values, -most), most).astype(kind)


def setup_inputs(seed: int = 0) -> dict:
    key_of = jax.random.split(jax.random.key(seed), 13)
    return {
        "block_in": normal_values(key_of[0], (SEQS, LEN, D), 1.0, 6.0, ((0, 8), (1, 4))),
        "cotangent": normal_values(key_of[1], (SEQS, LEN, D), 1.0, 6.0, ((0, 8), (1, 4))),
        "ln_gain": jnp.clip(1.0 + 0.1 * jax.random.normal(key_of[2], (D,), jnp.float32), 0.5, 1.5),
        "ln_bias": normal_values(key_of[3], (D,), 0.5, 3.0, ((0, 8),), jnp.float32),
        "lambda_log": jnp.clip(-1.0 + 1.3 * jax.random.uniform(key_of[4], (N,), jnp.float32) ** steps_of(key_of[4], (N,), ((0, 8),), -0.2, 0.2), -1.0, 0.3),
        "lambda_imag": jnp.clip(jax.random.uniform(key_of[5], (N,), jnp.float32, -30.0, 30.0) * steps_of(key_of[5], (N,), ((0, 8),), -0.4, 0.0), -30.0, 30.0),
        "dss_weight": normal_values(key_of[6], (2, N, D), 0.25, 1.5, ((2, 8),), jnp.float32),
        "log_step": draw_log_step(jax.random.fold_in(key_of[12], 71), 0),
        "skip_gain": normal_values(key_of[8], (D,), 1.0, 4.0, ((0, 8),), jnp.float32),
        "lin_weight": normal_values(key_of[9], (D, 2 * D), (D // 4) ** -0.5, 0.5, ((1, 8),)),
        "lin_bias": normal_values(key_of[10], (2 * D,), 0.5, 3.0, ((0, 8),), jnp.float32),
        "doc_lengths": jax.vmap(lambda own: ragged_sizes(own, DOCS, LEN, DOCMAX, 1))(jax.random.split(key_of[11], SEQS)).reshape((SEQS, DOCS)).astype(jnp.int32),
    }


@jax.custom_vjp
def low(v):
    return lax.optimization_barrier(v.astype(jnp.bfloat16)).astype(jnp.float32)

@jax.custom_vjp
def low_back(v):
    return v

def low_keep(v):
    return (low(v), None)

def low_pass(kept, grad):
    return (grad,)

def back_keep(v):
    return (v, None)

def back_low(kept, grad):
    return (low(grad),)
low.defvjp(low_keep, low_pass)
low_back.defvjp(back_keep, back_low)
ln_eps = 1e-05

def layer_norm(values, gain_vec, bias_vec):
    centre = values - lax.optimization_barrier(jnp.mean(values, axis=-1, keepdims=True))
    spread = lax.optimization_barrier(jnp.mean(centre * centre, axis=-1, keepdims=True))
    return centre * lax.rsqrt(spread + ln_eps) * gain_vec + bias_vec

def power_pair(real_rate, imag_rate, exponent):
    magnitude = jnp.exp(exponent * real_rate)
    phase_val = exponent * imag_rate
    return (magnitude * jnp.cos(phase_val), magnitude * jnp.sin(phase_val))

def state_rates(rate_log, freq_imag, step_log):
    step_size = jnp.exp(step_log)
    real_rate = -jnp.exp(rate_log)[:, None] * step_size[None, :]
    imag_rate = freq_imag[:, None] * step_size[None, :]
    return (real_rate, imag_rate)

def output_coeffs(state_weight, real_rate, imag_rate, length):
    half_sine = jnp.sin(0.5 * imag_rate)
    one_re = 2.0 * half_sine * half_sine - jnp.expm1(real_rate) * jnp.cos(imag_rate)
    one_im = -jnp.exp(real_rate) * jnp.sin(imag_rate)
    far_re, far_im = power_pair(real_rate, imag_rate, float(length))
    den_re = 1.0 - far_re
    den_im = -far_im
    num_re = state_weight[0] * one_re - state_weight[1] * one_im
    num_im = state_weight[0] * one_im + state_weight[1] * one_re
    norm_sq = den_re * den_re + den_im * den_im
    coef_re = (num_re * den_re + num_im * den_im) / norm_sq
    coef_im = (num_im * den_re - num_re * den_im) / norm_sq
    return (coef_re, coef_im)

def kernel_fn(lambda_log, lambda_imag, dss_weight, log_step):
    real_rate, imag_rate = state_rates(lambda_log, lambda_imag, log_step)
    coef_re, coef_im = output_coeffs(dss_weight, real_rate, imag_rate, LEN)
    span = math.gcd(LEN, 128)

    def one_block(start_at):
        lags = (start_at + jnp.arange(span, dtype=jnp.int32)).astype(jnp.float32)[:, None, None]
        pow_re, pow_im = power_pair(real_rate, imag_rate, lags)
        return lax.optimization_barrier(jnp.sum(coef_re * pow_re - coef_im * pow_im, axis=1))
    starts = (jnp.arange(LEN // span, dtype=jnp.int32) * span).astype(jnp.int32)
    blocks = lax.map(jax.checkpoint(one_block), starts)
    return blocks.reshape(LEN, D)

def doc_conv(normed, kernel, lengths):
    ends = jnp.cumsum(lengths).astype(jnp.int32)
    begins = (ends - lengths).astype(jnp.int32)
    places = jnp.arange(LEN, dtype=jnp.int32)
    member = ((places[None, :] >= begins[:, None]) & (places[None, :] < ends[:, None])).astype(jnp.float32)
    spectrum_k = jnp.fft.rfft(kernel, n=2 * LEN, axis=0)
    masked = member[:, :, None] * normed[None]
    spectrum_u = jnp.fft.rfft(masked, n=2 * LEN, axis=1)
    mixed = jnp.fft.irfft(spectrum_u * spectrum_k[None], n=2 * LEN, axis=1)[:, :LEN]
    return lax.optimization_barrier(jnp.sum(member[:, :, None] * mixed, axis=0))

def sequence_forward(x_seq, ln_gain, ln_bias, kernel, skip_gain, lin_weight, lin_bias, lengths):
    normed = layer_norm(x_seq, ln_gain, ln_bias)
    conv = doc_conv(normed, kernel, lengths) + skip_gain * normed
    act = low(jax.nn.gelu(conv, approximate=False))
    pre = low_back(jnp.dot(act, lin_weight, precision=lax.Precision.HIGHEST) + lin_bias)
    return x_seq + pre[:, :D] * jax.nn.sigmoid(pre[:, D:])

def reference(block_in, cotangent, ln_gain, ln_bias, lambda_log, lambda_imag, dss_weight, log_step, skip_gain, lin_weight, lin_bias, doc_lengths):
    kernel, kernel_back = jax.vjp(kernel_fn, lambda_log, lambda_imag, dss_weight, log_step)
    weight_full = lin_weight.astype(jnp.float32)

    def one_seq(totals, items):
        x_seq, cot_seq, lengths = items

        def seq_only(x_part, gain_part, bias_part, kernel_part, skip_part, weight_part, lbias_part):
            return sequence_forward(x_part, gain_part, bias_part, kernel_part, skip_part, weight_part, lbias_part, lengths)
        outputs, back_fn = jax.vjp(seq_only, x_seq, ln_gain, ln_bias, kernel, skip_gain, weight_full, lin_bias)
        grads = back_fn(cot_seq)
        new_totals = tuple((total + grad for total, grad in zip(totals, grads[1:])))
        return (new_totals, (outputs.astype(jnp.bfloat16), grads[0].astype(jnp.bfloat16)))
    start_totals = (jnp.zeros((D,), jnp.float32), jnp.zeros((D,), jnp.float32), jnp.zeros((LEN, D), jnp.float32), jnp.zeros((D,), jnp.float32), jnp.zeros((D, 2 * D), jnp.float32), jnp.zeros((2 * D,), jnp.float32))
    totals, (block_out, grad_in) = lax.scan(one_seq, start_totals, (block_in.astype(jnp.float32), cotangent.astype(jnp.float32), doc_lengths))
    grad_rate, grad_freq, grad_state, grad_step = kernel_back(totals[2])
    return (block_out, grad_in, totals[0], totals[1], grad_rate, grad_freq, grad_state, grad_step, totals[3], totals[4], totals[5])
```

```python
from functools import partial

import jax
import jax.numpy as jnp
import numpy as np
from jax import lax
from jax.experimental import pallas as pl
from jax.experimental.pallas import tpu as pltpu
from jax.sharding import PartitionSpec as P

f32, bf16, i32 = jnp.float32, jnp.bfloat16, jnp.int32
ln_eps = 1e-05
DOCMAX = 800
FINE = 8
COARSE = 10
LANES = 128
NN = (((1,), (0,)), ((), ()))
NT = (((1,), (1,)), ((), ()))
TN = (((0,), (0,)), ((), ()))
VM = pl.BlockSpec(memory_space=pltpu.VMEM)
SM = pl.BlockSpec(memory_space=pltpu.SMEM)


def dot(a, b, dims=NN):
    return lax.dot_general(a, b, dims, preferred_element_type=f32)


def exact_dot(a, b, dims=NN):
    return lax.dot_general(a, b, dims, precision=lax.Precision.HIGHEST, preferred_element_type=f32)


def shape(dims, dtype=f32):
    return jax.ShapeDtypeStruct(dims, dtype)


def call(body, out, specs, scratch=(), name=None, mib=8):
    return pl.pallas_call(
        body,
        out_shape=out,
        in_specs=specs,
        scratch_shapes=list(scratch),
        cost_estimate=pl.CostEstimate(flops=1000, bytes_accessed=1000, transcendentals=0),
        compiler_params=pltpu.CompilerParams(vmem_limit_bytes=mib * 2**20),
        name=name,
    )


def dft_tables(block):
    k = np.arange(block)[:, None]
    j = np.arange(block)[None, :]
    theta = np.pi * (((2 * k + 1) * j) % (4 * block)) / (2 * block)
    full = np.concatenate([np.cos(theta), -np.sin(theta)], axis=0)
    high = full.astype(jnp.bfloat16)
    low = (full - high.astype(np.float64)).astype(jnp.bfloat16)
    return high, low, np.ascontiguousarray(high.T), np.ascontiguousarray(low.T)


def channel_order(width, ndp, nseq):
    sub = width // ndp // nseq
    return np.arange(width).reshape(ndp, nseq, sub).transpose(1, 0, 2).reshape(-1)


def iota(dims, axis):
    return lax.broadcasted_iota(i32, dims, axis)


def cmul(ar, ai, br, bi):
    return ar * br - ai * bi, ar * bi + ai * br


def small_expm1(a):
    poly = jnp.full_like(a, 1.0)
    for k in range(9, 1, -1):
        poly = 1.0 + poly * a * (1.0 / k)
    return jnp.where(jnp.abs(a) < 0.5, a * poly, jnp.exp(a) - 1.0)


def state_terms(rate_log, freq, step_log, length):
    step = jnp.exp(step_log)
    a = -jnp.exp(rate_log) * step
    b = freq * step
    half = jnp.sin(0.5 * b)
    cos_b, sin_b, mag = jnp.cos(b), jnp.sin(b), jnp.exp(a)
    one_re = 2.0 * half * half - small_expm1(a) * cos_b
    one_im = -mag * sin_b
    far = jnp.exp(length * a)
    far_re, far_im = far * jnp.cos(length * b), far * jnp.sin(length * b)
    den_re, den_im = 1.0 - far_re, -far_im
    inv = 1.0 / (den_re * den_re + den_im * den_im)
    g_re = (one_re * den_re + one_im * den_im) * inv
    g_im = (one_im * den_re - one_re * den_im) * inv
    return a, b, mag * cos_b, mag * sin_b, one_re, one_im, far_re, far_im, den_re, den_im, inv, g_re, g_im


TERMS = 13


def rows8(zr, zi):
    dims = (8, zr.shape[-1])
    at = iota(dims, 0)
    r1, i1 = jnp.broadcast_to(zr, dims), jnp.broadcast_to(zi, dims)
    r2, i2 = cmul(r1, i1, r1, i1)
    r4, i4 = cmul(r2, i2, r2, i2)
    p = (jnp.where(at & 1 > 0, r1, 1.0), jnp.where(at & 1 > 0, i1, 0.0))
    p = cmul(*p, jnp.where(at & 2 > 0, r2, 1.0), jnp.where(at & 2 > 0, i2, 0.0))
    p = cmul(*p, jnp.where(at & 4 > 0, r4, 1.0), jnp.where(at & 4 > 0, i4, 0.0))
    return p, cmul(r4, i4, r4, i4)


def powers(wr, wi):
    pows = [None, (wr, wi)]
    for v in range(2, COARSE + 1):
        pows.append(cmul(*pows[v // 2], *pows[v - v // 2]))
    return pows


def halves(x):
    hi = x.astype(bf16)
    return hi, (x - hi.astype(f32)).astype(bf16)


def split3(hi_ref, lo_ref, x):
    x_hi, x_lo = halves(x)
    return dot(hi_ref[...], x_hi) + (dot(hi_ref[...], x_lo) + dot(lo_ref[...], x_hi))


def signs(block, lanes):
    return jnp.where(iota((block, lanes), 0) & 1 > 0, -1.0, 1.0)


def moved(x, by):
    return x if by % LANES == 0 else pltpu.roll(x, by % LANES, 1)


def pack_kernel(sub, me_ref, w_ref, step_ref, skip_ref, gain_ref, bias_ref, lam_ref, imag_ref, lb_ref, o_ref):
    own, per, cols = step_ref.shape[1], lam_ref.shape[1], lb_ref.shape[1]
    groups = LANES // sub
    height = w_ref.shape[0] // groups
    pick = (iota((own, LANES), 0) == me_ref[0] * sub + iota((own, LANES), 1) % sub).astype(f32)
    w = exact_dot(w_ref[...], pick)
    vec = exact_dot(jnp.concatenate([step_ref[...], skip_ref[...], gain_ref[...], bias_ref[...]] * 2, axis=0), pick)
    group = iota((1, LANES), 1) // sub
    main = jnp.zeros((height, LANES), f32)
    row = jnp.zeros((1, LANES), f32)
    for u in range(groups):
        main = jnp.where(group == u, w[u * height : (u + 1) * height], main)
        if u < 4:
            row = jnp.where(group == u, vec[u : u + 1], row)
    spot, lane = iota((per, LANES), 0), iota((per, LANES), 1)
    rates = exact_dot(jnp.broadcast_to(lam_ref[...], (8, per)), (lane == spot).astype(f32)) + exact_dot(
        jnp.broadcast_to(imag_ref[...], (8, per)), (lane == spot + per).astype(f32)
    )
    o_ref[0] = jnp.zeros(o_ref.shape[1:], f32)
    o_ref[0, 0:height] = main
    o_ref[0, height : height + 1] = row
    o_ref[0, height + 1 : height + 2] = rates[0:1]
    o_ref[0, height + 2 : height + 3, 0:cols] = lb_ref[...]
    for i in range(1, o_ref.shape[0]):
        o_ref[i] = o_ref[0]


def lag_kernel(sub, length, shared_ref, f_ref, fl_ref, kh_ref, w_ref, vec_ref, term_ref, k_scr, z_scr, kf_scr):
    ndp = shared_ref.shape[0]
    n_w, lanes = w_ref.shape
    nstate = n_w // 2
    per = nstate // ndp
    groups = LANES // sub
    height = n_w // groups
    block = f_ref.shape[1]
    group = iota((1, LANES), 1) // sub
    for u in range(groups):
        acc = jnp.zeros(shared_ref.shape[1:], f32)
        for i in range(ndp):
            acc = jnp.where(group == i, moved(shared_ref[i], (i - u) * sub), acc)
        w_ref[u * height : (u + 1) * height] = acc[0:height]
        if u < 4:
            vec_ref[u : u + 1] = acc[height : height + 1]
    vec_ref[4:8] = jnp.zeros((4, lanes), f32)
    rows = jnp.concatenate([shared_ref[i, height + 1 : height + 2] for i in range(ndp)], axis=0)
    spread = exact_dot((iota((nstate, ndp), 0) // per == iota((nstate, ndp), 1)).astype(f32), rows)
    lane, state = iota((nstate, lanes), 1), iota((nstate, lanes), 0)
    lam = jnp.sum(jnp.where(lane == state % per, spread, 0.0), axis=1, keepdims=True)
    imag = jnp.sum(jnp.where(lane == state % per + per, spread, 0.0), axis=1, keepdims=True)
    terms = state_terms(lam, imag, vec_ref[0:1], float(length))
    for slot, value in enumerate(terms):
        term_ref[slot] = value
    z_scr[0], z_scr[1] = cmul(w_ref[0:nstate], w_ref[nstate:], terms[11], terms[12])
    k_scr[...] = jnp.zeros_like(k_scr)

    def pair(m, _):
        ready = []
        for n in (2 * m, 2 * m + 1):
            (fr, fi), w = rows8(term_ref[2, pl.ds(n, 1), :], term_ref[3, pl.ds(n, 1), :])
            cr = jnp.broadcast_to(z_scr[0, pl.ds(n, 1), :], (8, lanes))
            ci = jnp.broadcast_to(z_scr[1, pl.ds(n, 1), :], (8, lanes))
            ready.append([cmul(fr, fi, cr, ci), powers(*w)])
        for u in range(DOCMAX // FINE // COARSE):
            for v in range(COARSE):
                at = (u * COARSE + v) * FINE
                total = k_scr[at : at + FINE]
                for (xr, xi), pows in ready:
                    total = total + (xr * pows[v][0] - xi * pows[v][1] if v else xr)
                k_scr[at : at + FINE] = total
            for one in ready:
                one[0] = cmul(*one[0], *one[1][COARSE])
        return 0

    lax.fori_loop(0, nstate // 2, pair, 0)
    k_scr[0:1] += vec_ref[1:2]
    parts = length // block
    for p in range(parts):
        kf_scr[p] = split3(f_ref, fl_ref, k_scr[p * block : (p + 1) * block])
    sign = signs(block, lanes)
    for p in range(parts):
        re, im = kf_scr[p, :block], kf_scr[p, block:]
        if p:
            re = re - sign * kf_scr[p - 1, block:]
            im = im + sign * kf_scr[p - 1, :block]
        kh_ref[p, :block] = re * (1.0 / block)
        kh_ref[p, block:] = im * (1.0 / block)


def ln_kernel(me_ref, x_ref, p_ref, *o_refs):
    count, block, width = x_ref.shape
    wide = o_refs[0].shape[-1]
    x = x_ref[...].astype(f32).reshape(count * block, width)
    centre = x - jnp.mean(x, axis=-1, keepdims=True)
    spread = jnp.mean(centre * centre, axis=-1, keepdims=True)
    hi, lo = halves(centre * lax.rsqrt(spread + ln_eps))
    for d, o_ref in enumerate(o_refs):
        c = me_ref[0] ^ d
        cols = p_ref[:, pl.ds(pl.multiple_of(c * wide, wide), wide)]
        o_ref[...] = (dot(hi, cols) + dot(lo, cols)).reshape(count, block, wide)


def ln_back_kernel(me_ref, g0, g1, g2, g3, x_ref, c_ref, p_ref, o_ref):
    count, block, width = x_ref.shape
    wide = g0.shape[-1]
    tokens = count * block
    g = jnp.zeros((tokens, width), f32)
    for d, g_ref in enumerate((g0, g1, g2, g3)):
        c = me_ref[0] ^ d
        cols = p_ref[:, pl.ds(pl.multiple_of(c * wide, wide), wide)]
        g = g + dot(g_ref[...].reshape(tokens, wide), cols, NT)
    x = x_ref[...].astype(f32).reshape(tokens, width)
    centre = x - jnp.mean(x, axis=-1, keepdims=True)
    inv = lax.rsqrt(jnp.mean(centre * centre, axis=-1, keepdims=True) + ln_eps)
    hat = centre * inv
    mean_g = jnp.mean(g, axis=-1, keepdims=True)
    mean_gx = jnp.mean(g * hat, axis=-1, keepdims=True)
    cot = c_ref[...].astype(f32).reshape(tokens, width)
    o_ref[...] = (cot + inv * (g - mean_g - hat * mean_gx)).astype(bf16).reshape(o_ref.shape)


def doc_ends(len_ref, s):
    ends = []
    for d in range(len_ref.shape[1]):
        ends.append(len_ref[s, d] + (ends[-1] if ends else 0))
    return ends


def places(len_ref, s, b, block, parts):
    lo, hi = b * block, b * block + block
    ends = doc_ends(len_ref, s)
    h_start, t_start, h_end, t_end = 0, 0, parts * block, parts * block
    for end in ends:
        h_start = jnp.maximum(h_start, jnp.where(end <= lo, end, 0))
        t_start = jnp.maximum(t_start, jnp.where(end < hi, end, 0))
        h_end = jnp.minimum(h_end, jnp.where(end > lo, end, parts * block))
        t_end = jnp.minimum(t_end, jnp.where(end >= hi, end, parts * block))
    head = jnp.minimum(h_end, hi) - lo
    tail = jnp.maximum(t_start, lo) - lo
    return head, tail, h_start // block, (t_end - 1) // block


def middles(len_ref, count, block, body):
    docs = len_ref.shape[1]
    if docs < 3:
        return

    def one(item, _):
        s, d = item // (docs - 2), item % (docs - 2) + 1
        start = 0
        for e in range(docs):
            start = start + jnp.where(e < d, len_ref[s, e], 0)
        end = start + len_ref[s, d]
        b = start // block

        @pl.when((start > b * block) & (end < (b + 1) * block))
        def _():
            body(s, b, start - b * block, end - b * block)

        return 0

    lax.fori_loop(0, count * (docs - 2), one, 0)


def spectra(head, tail, x, f_ref, fl_ref, exact=False):
    rows = iota(x.shape, 0)
    both = jnp.concatenate([jnp.where(rows < head, x, 0.0), jnp.where(rows >= tail, x, 0.0)], axis=1)
    if exact:
        both = both.astype(bf16)
        return dot(f_ref[...], both) + dot(fl_ref[...], both)
    return split3(f_ref, fl_ref, both)


def conv_kernel(me_ref, len_ref, x0, x1, x2, x3, vec_ref, kh_ref, f_ref, fl_ref, ft_ref, ftl_ref,
                o0, o1, o2, o3, s_ref, u_scr, y_scr, out_scr):
    count, block, lanes = x0.shape
    parts = kh_ref.shape[0]
    gain, bias = vec_ref[2:3], vec_ref[3:4]
    for d, x_ref in enumerate((x0, x1, x2, x3)):
        for s in range(count):
            u_scr[s, me_ref[0] ^ d] = x_ref[s] * gain + bias

    def forward(item, _):
        s, b = item // parts, item % parts
        head, tail, _, _ = places(len_ref, s, b, block, parts)
        s_ref[item] = spectra(head, tail, u_scr[s, b], f_ref, fl_ref)
        return 0

    lax.fori_loop(0, count * parts, forward, 0)

    def output(item, _):
        s, b = item // parts, item % parts
        head, tail, first, _ = places(len_ref, s, b, block, parts)
        kr, ki = kh_ref[0, :block], kh_ref[0, block:]
        for cols in (slice(0, lanes), slice(lanes, 2 * lanes)):
            sr, si = s_ref[item, :block, cols], s_ref[item, block:, cols]
            y_scr[:block, cols], y_scr[block:, cols] = cmul(kr, ki, sr, si)

        def add(e, _):
            p = b - e
            sr, si = s_ref[item - p, :block, lanes:], s_ref[item - p, block:, lanes:]
            re, im = cmul(kh_ref[p, :block], kh_ref[p, block:], sr, si)
            y_scr[:block, :lanes] += re
            y_scr[block:, :lanes] += im
            return 0

        lax.fori_loop(first, b, add, 0)
        y = split3(ft_ref, ftl_ref, y_scr[...])
        rows = iota((block, lanes), 0)
        out_scr[s, b] = jnp.where(rows < head, y[:, :lanes], jnp.where(rows >= tail, y[:, lanes:], 0.0))
        return 0

    lax.fori_loop(0, count * parts, output, 0)

    def middle(s, b, start, end):
        rows = iota((block, lanes), 0)
        keep = (rows >= start) & (rows < end)
        spec = split3(f_ref, fl_ref, jnp.where(keep, u_scr[s, b], 0.0))
        re, im = cmul(kh_ref[0, :block], kh_ref[0, block:], spec[:block], spec[block:])
        y = split3(ft_ref, ftl_ref, jnp.concatenate([re, im], axis=0))
        out_scr[s, b] = jnp.where(keep, y, out_scr[s, b])

    middles(len_ref, count, block, middle)
    for d, o_ref in enumerate((o0, o1, o2, o3)):
        for s in range(count):
            o_ref[s] = out_scr[s, me_ref[0] ^ d].astype(bf16)


def back_kernel(me_ref, len_ref, x0, x1, x2, x3, c0, c1, c2, c3, s_ref, vec_ref, kh_ref,
                f_ref, fl_ref, ft_ref, ftl_ref, g0, g1, g2, g3, dkh_ref, dvec_ref,
                v_scr, sv_scr, y_scr, du_scr):
    count, block, lanes = x0.shape
    parts = kh_ref.shape[0]
    gain, bias = vec_ref[2:3], vec_ref[3:4]
    for d, c_ref in enumerate((c0, c1, c2, c3)):
        for s in range(count):
            v_scr[s, me_ref[0] ^ d] = c_ref[s].astype(f32)
    dkh_ref[...] = jnp.zeros_like(dkh_ref)

    def forward(item, _):
        s, b = item // parts, item % parts
        head, tail, _, _ = places(len_ref, s, b, block, parts)
        sv_scr[item] = spectra(head, tail, v_scr[s, b], f_ref, fl_ref, exact=True)
        return 0

    lax.fori_loop(0, count * parts, forward, 0)

    def source(item, _):
        s, b = item // parts, item % parts
        head, tail, _, last = places(len_ref, s, b, block, parts)
        kr, ki = kh_ref[0, :block], kh_ref[0, block:]
        two = jnp.where(tail > 0, 1.0, 0.0)
        for side in (0, 1):
            cols = slice(side * lanes, (side + 1) * lanes)
            vr, vi = sv_scr[item, :block, cols], sv_scr[item, block:, cols]
            y_scr[:block, cols], y_scr[block:, cols] = cmul(kr, -ki, vr, vi)
            re, im = cmul(vr, vi, s_ref[item, :block, cols], -s_ref[item, block:, cols])
            dkh_ref[0, :block] += re * two if side else re
            dkh_ref[0, block:] += im * two if side else im

        def add(e, _):
            p = e - b
            vr, vi = sv_scr[item + p, :block, :lanes], sv_scr[item + p, block:, :lanes]
            re, im = cmul(kh_ref[p, :block], -kh_ref[p, block:], vr, vi)
            y_scr[:block, lanes:] += re
            y_scr[block:, lanes:] += im
            re, im = cmul(vr, vi, s_ref[item, :block, lanes:], -s_ref[item, block:, lanes:])
            dkh_ref[p, :block] += re
            dkh_ref[p, block:] += im
            return 0

        lax.fori_loop(b + 1, last + 1, add, 0)
        y = split3(ft_ref, ftl_ref, y_scr[...])
        rows = iota((block, lanes), 0)
        du_scr[s, b] = jnp.where(rows >= tail, y[:, lanes:], jnp.where(rows < head, y[:, :lanes], 0.0))
        return 0

    lax.fori_loop(0, count * parts, source, 0)

    def middle(s, b, start, end):
        rows = iota((block, lanes), 0)
        keep = (rows >= start) & (rows < end)
        v = jnp.where(keep, v_scr[s, b], 0.0).astype(bf16)
        sv = dot(f_ref[...], v) + dot(fl_ref[...], v)
        u = jnp.zeros((block, lanes), f32)
        for d, x_ref in enumerate((x0, x1, x2, x3)):
            u = jnp.where(b == me_ref[0] ^ d, x_ref[s], u)
        su = split3(f_ref, fl_ref, jnp.where(keep, u * gain + bias, 0.0))
        re, im = cmul(sv[:block], sv[block:], su[:block], -su[block:])
        dkh_ref[0, :block] += re
        dkh_ref[0, block:] += im
        re, im = cmul(kh_ref[0, :block], -kh_ref[0, block:], sv[:block], sv[block:])
        y = split3(ft_ref, ftl_ref, jnp.concatenate([re, im], axis=0))
        du_scr[s, b] = jnp.where(keep, y, du_scr[s, b])

    middles(len_ref, count, block, middle)
    d_gain = jnp.zeros((1, lanes), f32)
    d_bias = jnp.zeros((1, lanes), f32)
    for d, (x_ref, g_ref) in enumerate(zip((x0, x1, x2, x3), (g0, g1, g2, g3))):
        for s in range(count):
            du = du_scr[s, me_ref[0] ^ d]
            d_bias += jnp.sum(du, axis=0, keepdims=True)
            d_gain += jnp.sum(du * x_ref[s], axis=0, keepdims=True)
            g_ref[s] = (du * gain).astype(bf16)
    dvec_ref[0:1] = d_gain
    dvec_ref[1:2] = d_bias


def dense_kernel(me_ref, q0, q1, q2, q3, x_ref, c_ref, w_ref, lb_ref,
                 out_ref, act_ref, dpre_ref, dlb_ref, d0, d1, d2, d3, slope_scr, dact_scr):
    count, block, wide = q0.shape
    tokens, width = act_ref.shape
    for d, q_ref in enumerate((q0, q1, q2, q3)):
        cols = pl.ds(pl.multiple_of((me_ref[0] ^ d) * wide, wide), wide)
        v = q_ref[...].reshape(tokens, wide).astype(f32)
        cdf = 0.5 * (1.0 + lax.erf(v * np.float32(1.0 / np.sqrt(2.0))))
        act_ref[:, cols] = (v * cdf).astype(bf16)
        slope_scr[:, cols] = cdf + v * (jnp.exp(-0.5 * v * v) * np.float32(1.0 / np.sqrt(2.0 * np.pi)))
    pre = dot(act_ref[...], w_ref[...]) + lb_ref[...]
    first = pre[:, :width]
    gate = 1.0 / (1.0 + jnp.exp(-pre[:, width:]))
    x = x_ref[...].reshape(tokens, width).astype(f32)
    out_ref[...] = (x + first * gate).astype(bf16).reshape(out_ref.shape)
    cot = c_ref[...].reshape(tokens, width).astype(f32)
    d_first = cot * gate
    d_second = d_first * first * (1.0 - gate)
    d_pre = jnp.concatenate([d_first, d_second], axis=1).astype(bf16)
    dpre_ref[...] = d_pre
    dlb_ref[...] = jnp.sum(d_pre.astype(f32), axis=0, keepdims=True)
    dact_scr[...] = dot(d_pre, w_ref[...], NT)
    for d, o_ref in enumerate((d0, d1, d2, d3)):
        cols = pl.ds(pl.multiple_of((me_ref[0] ^ d) * wide, wide), wide)
        o_ref[...] = (dact_scr[:, cols] * slope_scr[:, cols]).astype(bf16).reshape(o_ref.shape)


def weight_kernel(act_ref, dpre_ref, dw_ref):
    part = dw_ref.shape[-1]
    full = dot(act_ref[...], dpre_ref[...], TN)
    for i in range(dw_ref.shape[0]):
        dw_ref[i] = full[:, i * part : (i + 1) * part].astype(bf16)


def state_grad_kernel(sub, length, w_ref, term_ref, dkh_ref, dvec_ref, dlb_ref, ft_ref, ftl_ref, o_ref,
                      dk_scr, f_scr, dw_scr):
    ndp = o_ref.shape[0]
    n_w, lanes = w_ref.shape
    nstate = n_w // 2
    per = nstate // ndp
    groups = LANES // sub
    height = n_w // groups
    parts, twice, _ = dkh_ref.shape
    block = twice // 2
    sign = signs(block, lanes)
    for p in range(parts):
        re, im = dkh_ref[p, :block], dkh_ref[p, block:]
        if p + 1 < parts:
            re = re + sign * dkh_ref[p + 1, block:]
            im = im - sign * dkh_ref[p + 1, :block]
        dk_scr[p * block : (p + 1) * block] = split3(
            ft_ref, ftl_ref, jnp.concatenate([re, im], axis=0)
        ) * (1.0 / block)
    at8 = iota((8, lanes), 0).astype(f32)

    def one(n, _):
        (fr, fi), w = rows8(term_ref[2, pl.ds(n, 1), :], term_ref[3, pl.ds(n, 1), :])
        pows = powers(*w)
        zero = jnp.zeros((8, lanes), f32)
        s_re, s_im, e_re, e_im, h_re, h_im = (zero,) * 6
        for u in range(DOCMAX // FINE // COARSE - 1, -1, -1):
            t_re, t_im, o_re, o_im = (zero,) * 4
            for v in range(COARSE - 1, 0, -1):
                at = (u * COARSE + v) * FINE
                dk = dk_scr[at : at + FINE]
                t_re = t_re + dk * pows[v][0]
                t_im = t_im + dk * pows[v][1]
                o_re = o_re + t_re
                o_im = o_im + t_im
            t_re = t_re + dk_scr[u * COARSE * FINE : u * COARSE * FINE + FINE]
            e_re, e_im = cmul(e_re, e_im, *pows[COARSE])
            s_re, s_im = cmul(s_re, s_im, *pows[COARSE])
            h_re, h_im = cmul(h_re, h_im, *pows[COARSE])
            e_re, e_im = e_re + s_re, e_im + s_im
            s_re, s_im = s_re + t_re, s_im + t_im
            h_re, h_im = h_re + o_re, h_im + o_im
        m_re = (FINE * COARSE) * e_re + FINE * h_re + at8 * s_re
        m_im = (FINE * COARSE) * e_im + FINE * h_im + at8 * s_im
        s_re, s_im = cmul(s_re, s_im, fr, fi)
        m_re, m_im = cmul(m_re, m_im, fr, fi)
        for slot, value in enumerate((s_re, s_im, m_re, m_im)):
            f_scr[slot, pl.ds(n, 1), :] = jnp.sum(value, axis=0, keepdims=True)
        return 0

    lax.fori_loop(0, nstate, one, 0)
    a, b, z_re, z_im, one_re, one_im, far_re, far_im, den_re, den_im, inv, g_re, g_im = (
        term_ref[slot] for slot in range(TERMS)
    )
    f0, f1 = (f_scr[0], f_scr[1]), (f_scr[2], f_scr[3])
    gf_re, gf_im = cmul(g_re, g_im, *f0)
    dw_scr[0:nstate] = gf_re
    dw_scr[nstate:] = -gf_im
    inv_one = 1.0 / (one_re * one_re + one_im * one_im)
    near_re, near_im = cmul(z_re, z_im, one_re * inv_one, -one_im * inv_one)
    far_re, far_im = cmul(far_re, far_im, den_re * inv, -den_im * inv)
    q_re, q_im = cmul(length * far_re - near_re, length * far_im - near_im, *f0)
    c_re, c_im = cmul(w_ref[0:nstate], w_ref[nstate:], g_re, g_im)
    y_re, y_im = cmul(c_re, c_im, q_re + f1[0], q_im + f1[1])
    by_a = a * y_re
    by_step = by_a - b * y_im
    step = jnp.exp(dvec_ref[2:3])
    by_imag = -step * y_im
    d_step = jnp.sum(by_step, axis=0, keepdims=True)
    lane, state = iota((nstate, lanes), 1), iota((nstate, lanes), 0)
    col_a = jnp.sum(by_a, axis=1, keepdims=True)
    col_b = jnp.sum(by_imag, axis=1, keepdims=True)
    grid = jnp.where(lane == state % per, col_a, jnp.where(lane == state % per + per, col_b, 0.0))
    rates = exact_dot((iota((ndp, nstate), 0) == iota((ndp, nstate), 1) // per).astype(f32), grid)
    vecs = (d_step, dk_scr[0:1], dvec_ref[0:1], dvec_ref[1:2])
    group = iota((1, LANES), 1) // sub
    cols = dlb_ref.shape[1] // ndp
    for i in range(ndp):
        main = jnp.zeros((height, LANES), f32)
        row = jnp.zeros((1, LANES), f32)
        for u in range(groups):
            main = jnp.where(group == u, moved(dw_scr[u * height : (u + 1) * height], (u - i) * sub), main)
            if u < 4:
                row = jnp.where(group == u, moved(jnp.broadcast_to(vecs[u], (8, LANES)), (u - i) * sub)[0:1], row)
        o_ref[i] = jnp.zeros(o_ref.shape[1:], f32)
        o_ref[i, 0:height] = main
        o_ref[i, height : height + 1] = row
        o_ref[i, height + 1 : height + 2] = rates[i : i + 1]
        o_ref[i, height + 2 : height + 3, 0:cols] = dlb_ref[:, i * cols : (i + 1) * cols]


def sum_kernel(x_ref, o_ref):
    total = x_ref[0].astype(f32)
    for i in range(1, x_ref.shape[0]):
        total = total + x_ref[i].astype(f32)
    o_ref[...] = total


def last_kernel(sub, me_ref, m0, m1, m2, m3, w0, w1, w2, w3, w_ref, step_ref, skip_ref, gain_ref, bias_ref,
                lam_ref, imag_ref, lb_ref, dw_ref):
    n_w, own = w_ref.shape
    groups = LANES // sub
    height = n_w // groups
    per, cols = lam_ref.shape[1], lb_ref.shape[1]
    group = iota((1, LANES), 1) // sub
    parts = (m0, m1, m2, m3)
    for u in range(groups):
        acc = jnp.zeros(m0.shape, f32)
        for d, m_ref in enumerate(parts):
            c = me_ref[0] ^ d
            acc = jnp.where(group == c, pltpu.roll(m_ref[...], (c - u) * sub + LANES, 1), acc)
        w_ref[u * height : (u + 1) * height] = acc[0:height, 0:own]
        if u < 4:
            (step_ref, skip_ref, gain_ref, bias_ref)[u][...] = acc[height : height + 1, 0:own]
    total = m0[...] + m1[...] + m2[...] + m3[...]
    lam_ref[...] = total[height + 1 : height + 2, 0:per]
    imag_ref[...] = pltpu.roll(total, LANES - per, 1)[height + 1 : height + 2, 0:per]
    lb_ref[...] = total[height + 2 : height + 3, 0:cols]
    nseq = len(parts)
    width = w0.shape[0]
    span = width // nseq
    for c in range(nseq):
        rows = slice(c * span, (c + 1) * span)
        whole = w0[rows].astype(f32) + w1[rows].astype(f32) + w2[rows].astype(f32) + w3[rows].astype(f32)
        for i in range(span // sub):
            at = (i * nseq + c) * sub
            dw_ref[at : at + sub] = whole[i * sub : (i + 1) * sub]


def trade(parts, axis):
    n = len(parts)
    return [parts[0]] + [lax.ppermute(parts[d], axis, [(i, i ^ d) for i in range(n)]) for d in range(1, n)]


def after(values, first):
    tied = lax.optimization_barrier((tuple(values), first))
    return list(tied[0])


def on_device(block_in, cotangent, ln_gain, ln_bias, lambda_log, lambda_imag, dss_weight, log_step, skip_gain,
              lin_weight, lin_bias, doc_lengths):
    ndp, nseq = lax.axis_size("dp"), lax.axis_size("seq")
    count, block, width = block_in.shape
    length = block * nseq
    own = ln_gain.shape[0]
    sub = own // nseq
    wide = width // nseq
    per = lambda_log.shape[0]
    nstate = per * ndp
    n_w = 2 * nstate
    cols = lin_weight.shape[1]
    tokens = count * block
    me = jnp.reshape(lax.axis_index("seq"), (1,)).astype(i32)
    perm = np.zeros((width, width), np.float32)
    perm[channel_order(width, ndp, nseq), np.arange(width)] = 1.0
    perm = jnp.asarray(perm, bf16)
    f_hi, f_lo, ft_hi, ft_lo = (jnp.asarray(t) for t in dft_tables(block))
    rows = -(-(n_w * sub // LANES + 3) // 8) * 8

    def row(v):
        return v.reshape(1, -1)

    packed = call(partial(pack_kernel, sub), shape((ndp, rows, LANES)), [SM] + [VM] * 8, name="pack")(
        me, dss_weight.reshape(n_w, own), row(log_step), row(skip_gain), row(ln_gain), row(ln_bias),
        row(lambda_log), row(lambda_imag), row(lin_bias)
    )
    shared = lax.all_to_all(packed, "dp", 0, 0, tiled=True)

    piece, piece32 = shape((count, block, wide), bf16), shape((count, block, wide))
    hats = call(ln_kernel, [piece32] * nseq, [SM, VM, VM], name="layer_norm")(me, block_in, perm)
    hats = trade(hats, "seq")

    (lin_late,) = after([lin_weight], shared[0, 0, 0])
    w_lin = lax.all_to_all(jnp.broadcast_to(lin_late[None], (ndp, width, cols)), "dp", 0, 0, tiled=True)
    w_lin = w_lin.reshape(ndp, ndp, nseq, sub, cols).transpose(2, 1, 3, 0, 4).reshape(width, 2 * width)
    bias_full = shared[:, n_w * sub // LANES + 2, :cols].reshape(1, 2 * width)

    spec = (nseq, 2 * block, wide)
    kh, w_all, vec, terms = call(
        partial(lag_kernel, sub, length), [shape(spec), shape((n_w, wide)), shape((8, wide)), shape((TERMS, nstate, wide))],
        [VM] * 3, scratch=[pltpu.VMEM((length, wide), f32), pltpu.VMEM((2, nstate, wide), f32), pltpu.VMEM(spec, f32)],
        name="lag_kernel",
    )(shared, f_hi, f_lo)

    blocks4 = (count, nseq, block, wide)
    sides = (count * nseq, 2 * block, 2 * wide)
    out = call(
        conv_kernel, [piece] * nseq + [shape(sides)], [SM, SM] + [VM] * (nseq + 6),
        scratch=[pltpu.VMEM(blocks4, f32), pltpu.VMEM(sides[1:], f32), pltpu.VMEM(blocks4, f32)],
        name="doc_conv", mib=16,
    )(me, doc_lengths, *hats, vec, kh, f_hi, f_lo, ft_hi, ft_lo)
    convs, spectra_u = trade(out[:nseq], "seq"), out[nseq]

    out = call(
        dense_kernel,
        [shape((count, block, width), bf16), shape((tokens, width), bf16), shape((tokens, 2 * width), bf16),
         shape((1, 2 * width))] + [piece] * nseq,
        [SM] + [VM] * (nseq + 4),
        scratch=[pltpu.VMEM((tokens, width), f32), pltpu.VMEM((tokens, width), f32)],
        name="gated_linear", mib=20,
    )(me, *convs, block_in, cotangent, w_lin, bias_full)
    block_out, act, d_pre, d_lin_bias = out[:4]
    d_convs = trade(out[4:], "seq")

    dw_parts = call(weight_kernel, shape((ndp, width, cols), bf16), [VM, VM], name="weight_grad")(act, d_pre)
    dw_parts = lax.all_to_all(dw_parts, "dp", 0, 0, tiled=True)

    out = call(
        back_kernel, [piece] * nseq + [shape(spec), shape((2, wide))],
        [SM, SM] + [VM] * (2 * nseq + 7),
        scratch=[pltpu.VMEM(blocks4, f32), pltpu.VMEM(sides, f32), pltpu.VMEM(sides[1:], f32), pltpu.VMEM(blocks4, f32)],
        name="doc_conv_grad", mib=24,
    )(me, doc_lengths, *hats, *d_convs, spectra_u, vec, kh, f_hi, f_lo, ft_hi, ft_lo)
    g_own, dkh, d_norm = out[:nseq], out[nseq], out[nseq + 1]
    gs = trade(g_own, "seq")

    small = call(
        partial(state_grad_kernel, sub, length), shape((ndp, rows, LANES)), [VM] * 7,
        scratch=[pltpu.VMEM((length, wide), f32), pltpu.VMEM((4, nstate, wide), f32), pltpu.VMEM((n_w, wide), f32)],
        name="state_grad",
    )(w_all, terms, dkh, jnp.concatenate([d_norm, vec[0:1]], axis=0), d_lin_bias, ft_hi, ft_lo)
    small, dw_parts = lax.optimization_barrier((small, dw_parts))
    small = lax.all_to_all(small, "dp", 0, 0, tiled=True)

    grad_in = call(
        ln_back_kernel, shape((count, block, width), bf16), [SM] + [VM] * (nseq + 3), name="layer_norm_grad", mib=12,
    )(me, *gs, block_in, cotangent, perm)

    dw_own = call(sum_kernel, shape((width, cols)), [VM], name="weight_sum")(dw_parts)
    dws = trade([dw_own] * nseq, "seq")
    small = call(sum_kernel, shape((rows, LANES)), [VM], name="small_sum")(small)
    smalls = trade([small] * nseq, "seq")
    d_w, d_step, d_skip, d_gain, d_bias, d_lam, d_imag, d_lb, dw = call(
        partial(last_kernel, sub),
        [shape((n_w, own))] + [shape((1, own))] * 4 + [shape((1, per))] * 2 + [shape((1, cols)), shape((width, cols))],
        [SM] + [VM] * (2 * nseq), name="last",
    )(me, *smalls, *dws)
    return (
        block_out, grad_in, d_gain.reshape(own), d_bias.reshape(own), d_lam.reshape(per), d_imag.reshape(per),
        d_w.reshape(2, nstate, own), d_step.reshape(own), d_skip.reshape(own), dw, d_lb.reshape(cols),
    )


def solution(mesh):
    placed = (
        P("dp", "seq", None), P("dp", "seq", None), P("dp"), P("dp"), P("dp"), P("dp"),
        P(None, None, "dp"), P("dp"), P("dp"), P(None, "dp"), P("dp"), P("dp", None),
    )
    return jax.shard_map(
        on_device,
        mesh=mesh,
        in_specs=placed,
        out_specs=(
            P("dp", "seq", None), P("dp", "seq", None), P("dp"), P("dp"), P("dp"), P("dp"),
            P(None, None, "dp"), P("dp"), P("dp"), P(None, "dp"), P("dp"),
        ),
        check_vma=False,
    )
```

```python
from functools import partial

import jax
import jax.numpy as jnp
import numpy as np
from jax import lax
from jax.experimental import pallas as pl
from jax.experimental.pallas import tpu as pltpu
from jax.sharding import PartitionSpec as P

f32, bf16, i32 = jnp.float32, jnp.bfloat16, jnp.int32
ln_eps = 1e-05
DOCMAX = 800
FINE = 8
COARSE = 10
LANES = 128
NN = (((1,), (0,)), ((), ()))
NT = (((1,), (1,)), ((), ()))
TN = (((0,), (0,)), ((), ()))
VM = pl.BlockSpec(memory_space=pltpu.VMEM)
AN = pl.BlockSpec(memory_space=pl.ANY)
DMA = pltpu.SemaphoreType.DMA


def dot(a, b, dims=NN):
    return lax.dot_general(a, b, dims, preferred_element_type=f32)


def exact_dot(a, b, dims=NN):
    return lax.dot_general(a, b, dims, precision=lax.Precision.HIGHEST, preferred_element_type=f32)


def shape(dims, dtype=f32):
    return jax.ShapeDtypeStruct(dims, dtype)


def call(body, out, specs, scratch=(), name=None, mib=8, outs=None, us=0, keep=()):
    inputs, kept = len(specs), len(keep)

    def whole(*refs):
        body(*refs[:inputs], *refs[inputs + kept :])

    kernel = pl.pallas_call(
        whole,
        out_shape=out,
        in_specs=list(specs) + [AN] * kept,
        out_specs=outs if outs is not None else jax.tree.map(lambda _: VM, out),
        scratch_shapes=list(scratch),
        cost_estimate=pl.CostEstimate(flops=int(us * 1.15e9), bytes_accessed=1000, transcendentals=0),
        compiler_params=pltpu.CompilerParams(vmem_limit_bytes=mib * 2**20),
        name=name,
    )
    return lambda *args: kernel(*args, *keep)


def iota(dims, axis):
    return lax.broadcasted_iota(i32, dims, axis)


def cmul(ar, ai, br, bi):
    return ar * br - ai * bi, ar * bi + ai * br


def small_expm1(a):
    poly = jnp.full_like(a, 1.0)
    for k in range(9, 1, -1):
        poly = 1.0 + poly * a * (1.0 / k)
    return jnp.where(jnp.abs(a) < 0.5, a * poly, jnp.exp(a) - 1.0)


def state_terms(rate_log, freq, step_log, length):
    step = jnp.exp(step_log)
    a = -jnp.exp(rate_log) * step
    b = freq * step
    half = jnp.sin(0.5 * b)
    cos_b, sin_b, mag = jnp.cos(b), jnp.sin(b), jnp.exp(a)
    one_re = 2.0 * half * half - small_expm1(a) * cos_b
    one_im = -mag * sin_b
    far = jnp.exp(length * a)
    far_re, far_im = far * jnp.cos(length * b), far * jnp.sin(length * b)
    den_re, den_im = 1.0 - far_re, -far_im
    inv = 1.0 / (den_re * den_re + den_im * den_im)
    g_re = (one_re * den_re + one_im * den_im) * inv
    g_im = (one_im * den_re - one_re * den_im) * inv
    return a, b, mag * cos_b, mag * sin_b, one_re, one_im, far_re, far_im, den_re, den_im, inv, g_re, g_im


TERMS = 13


def rows8(zr, zi):
    dims = (8, zr.shape[-1])
    at = iota(dims, 0)
    r1, i1 = jnp.broadcast_to(zr, dims), jnp.broadcast_to(zi, dims)
    r2, i2 = cmul(r1, i1, r1, i1)
    r4, i4 = cmul(r2, i2, r2, i2)
    p = (jnp.where(at & 1 > 0, r1, 1.0), jnp.where(at & 1 > 0, i1, 0.0))
    p = cmul(*p, jnp.where(at & 2 > 0, r2, 1.0), jnp.where(at & 2 > 0, i2, 0.0))
    p = cmul(*p, jnp.where(at & 4 > 0, r4, 1.0), jnp.where(at & 4 > 0, i4, 0.0))
    return p, cmul(r4, i4, r4, i4)


def powers(wr, wi):
    pows = [None, (wr, wi)]
    for v in range(2, COARSE + 1):
        pows.append(cmul(*pows[v // 2], *pows[v - v // 2]))
    return pows


def halves(x):
    hi = x.astype(bf16)
    return hi, (x - hi.astype(f32)).astype(bf16)


def stack3(ref, cols, x):
    height = x.shape[0]
    hi, lo = halves(x)
    ref[0:height, cols] = hi
    ref[height : 2 * height, cols] = lo
    ref[2 * height : 3 * height, cols] = hi


def signs(block, lanes):
    return jnp.where(iota((block, lanes), 0) & 1 > 0, -1.0, 1.0)


def table_kernel(f_ref, ft_ref):
    block = ft_ref.shape[0]
    for ref, flip in ((f_ref, 0), (ft_ref, 1)):
        k, j = iota((block, block), flip), iota((block, block), 1 - flip)
        theta = (((2 * k + 1) * j) % (4 * block)).astype(f32) * np.float32(np.pi / (2 * block))
        for half, value in ((0, jnp.cos(theta)), (1, -jnp.sin(theta))):
            hi, lo = halves(value)
            for third, part in enumerate((hi, hi, lo)):
                if flip:
                    at = (2 * third + half) * block
                    ref[:, at : at + block] = part
                else:
                    ref[half * block : (half + 1) * block, third * block : (third + 1) * block] = part


def moved(x, by):
    return x if by % LANES == 0 else pltpu.roll(x, by % LANES, 1)


def pack_kernel(sub, w_ref, step_ref, skip_ref, gain_ref, bias_ref, lam_ref, imag_ref, lb_ref, o_ref):
    own, per, cols = step_ref.shape[1], lam_ref.shape[1], lb_ref.shape[1]
    groups = LANES // sub
    height = w_ref.shape[0] // groups
    pick = (iota((own, LANES), 0) == lax.axis_index("seq") * sub + iota((own, LANES), 1) % sub).astype(f32)
    w = exact_dot(w_ref[...], pick)
    vec = exact_dot(jnp.concatenate([step_ref[...], skip_ref[...], gain_ref[...], bias_ref[...]] * 2, axis=0), pick)
    group = iota((1, LANES), 1) // sub
    main = jnp.zeros((height, LANES), f32)
    row = jnp.zeros((1, LANES), f32)
    for u in range(groups):
        main = jnp.where(group == u, w[u * height : (u + 1) * height], main)
        if u < 4:
            row = jnp.where(group == u, vec[u : u + 1], row)
    spot, lane = iota((per, LANES), 0), iota((per, LANES), 1)
    rates = exact_dot(jnp.broadcast_to(lam_ref[...], (8, per)), (lane == spot).astype(f32)) + exact_dot(
        jnp.broadcast_to(imag_ref[...], (8, per)), (lane == spot + per).astype(f32)
    )
    o_ref[...] = jnp.zeros(o_ref.shape, f32)
    o_ref[0, 0:height] = main
    o_ref[0, height : height + 1] = row
    o_ref[0, height + 1 : height + 2] = rates[0:1]
    o_ref[0, height + 2 : height + 3, 0:cols] = lb_ref[...]


def lag_kernel(sub, length, masks, n_parts, *refs):
    pieces, refs = refs[:n_parts], refs[n_parts:]
    f_ref, kh_ref, vec_ref, w_out, term_out, w_ref, term_ref, k_scr, z_scr, rhs_scr, kf_scr, sems = refs
    slots = [piece.at[t] for piece in pieces for t in range(piece.shape[0])]
    ndp = len(slots)
    me = lax.axis_index("dp")
    n_w, lanes = w_ref.shape
    nstate = n_w // 2
    per = nstate // ndp
    groups = LANES // sub
    height = n_w // groups
    block = f_ref.shape[0] // 2
    group = iota((1, LANES), 1) // sub
    for u in range(groups):
        acc = jnp.zeros(slots[0].shape, f32)
        for t in range(ndp):
            i = me ^ masks[t]
            acc = jnp.where(group == i, pltpu.roll(slots[t][...], (i - u) * sub + LANES * ndp, 1), acc)
        w_ref[u * height : (u + 1) * height] = acc[0:height]
        if u < 4:
            vec_ref[u : u + 1] = acc[height : height + 1]
    vec_ref[4:8] = jnp.zeros((4, lanes), f32)
    rows = jnp.concatenate([slot[height + 1 : height + 2] for slot in slots], axis=0)
    source = jnp.zeros((nstate, ndp), i32)
    for t in range(ndp):
        source = jnp.where(iota((nstate, ndp), 1) == t, me ^ masks[t], source)
    spread = exact_dot((iota((nstate, ndp), 0) // per == source).astype(f32), rows)
    lane, state = iota((nstate, lanes), 1), iota((nstate, lanes), 0)
    lam = jnp.sum(jnp.where(lane == state % per, spread, 0.0), axis=1, keepdims=True)
    imag = jnp.sum(jnp.where(lane == state % per + per, spread, 0.0), axis=1, keepdims=True)
    terms = state_terms(lam, imag, vec_ref[0:1], float(length))
    for slot, value in enumerate(terms):
        term_ref[slot] = value
    saves = [pltpu.make_async_copy(w_ref, w_out, sems.at[0]), pltpu.make_async_copy(term_ref, term_out, sems.at[1])]
    for save in saves:
        save.start()
    z_scr[0], z_scr[1] = cmul(w_ref[0:nstate], w_ref[nstate:], terms[11], terms[12])
    k_scr[...] = jnp.zeros_like(k_scr)

    def pair(m, _):
        ready = []
        for n in (2 * m, 2 * m + 1):
            (fr, fi), w = rows8(term_ref[2, pl.ds(n, 1), :], term_ref[3, pl.ds(n, 1), :])
            cr = jnp.broadcast_to(z_scr[0, pl.ds(n, 1), :], (8, lanes))
            ci = jnp.broadcast_to(z_scr[1, pl.ds(n, 1), :], (8, lanes))
            ready.append([cmul(fr, fi, cr, ci), powers(*w)])
        for u in range(DOCMAX // FINE // COARSE):
            for v in range(COARSE):
                at = (u * COARSE + v) * FINE
                total = k_scr[at : at + FINE]
                for (xr, xi), pows in ready:
                    total = total + (xr * pows[v][0] - xi * pows[v][1] if v else xr)
                k_scr[at : at + FINE] = total
            for one in ready:
                one[0] = cmul(*one[0], *one[1][COARSE])
        return 0

    lax.fori_loop(0, nstate // 2, pair, 0)
    k_scr[0:1] += vec_ref[1:2]
    parts = length // block
    for p in range(parts):
        stack3(rhs_scr, slice(p * lanes, (p + 1) * lanes), k_scr[p * block : (p + 1) * block])
    kf_scr[...] = dot(f_ref[...], rhs_scr[...])
    sign = signs(block, lanes)
    for p in range(parts):
        here, past = slice(p * lanes, (p + 1) * lanes), slice((p - 1) * lanes, p * lanes)
        re, im = kf_scr[:block, here], kf_scr[block:, here]
        if p:
            re = re - sign * kf_scr[block:, past]
            im = im + sign * kf_scr[:block, past]
        kh_ref[p, :block] = re * (1.0 / block)
        kh_ref[p, block:] = im * (1.0 / block)
    for save in saves:
        save.wait()


def members(own, sub, c, width, wide):
    lane = iota((1, wide), 1)
    return (iota((width, wide), 0) == (lane // sub) * own + c * sub + lane % sub).astype(f32).astype(bf16)


def ln_kernel(own, sub, x_any, *refs):
    *o_refs, x_ref, sems = refs
    count, block, width = x_ref.shape
    wide = o_refs[0].shape[-1]
    copies = [pltpu.make_async_copy(x_any.at[s], x_ref.at[s], sems.at[s]) for s in range(count)]
    for copy in copies:
        copy.start()
    places = [members(own, sub, lax.axis_index("seq") ^ d, width, wide) for d in range(len(o_refs))]
    for s in range(count):
        copies[s].wait()
        x = x_ref[s].astype(f32)
        centre = x - jnp.mean(x, axis=-1, keepdims=True)
        spread = jnp.mean(centre * centre, axis=-1, keepdims=True)
        hi, lo = halves(centre * lax.rsqrt(spread + ln_eps))
        for o_ref, cols in zip(o_refs, places):
            o_ref[s] = dot(hi, cols) + dot(lo, cols)


def ln_back_kernel(own, sub, g0, g1, g2, g3, x_ref, c_ref, o_ref):
    count, block, width = x_ref.shape
    wide = g0.shape[-1]
    tokens = count * block
    g = jnp.zeros((tokens, width), f32)
    for d, g_ref in enumerate((g0, g1, g2, g3)):
        cols = members(own, sub, lax.axis_index("seq") ^ d, width, wide)
        g = g + dot(g_ref[...].reshape(tokens, wide), cols, NT)
    x = x_ref[...].astype(f32).reshape(tokens, width)
    centre = x - jnp.mean(x, axis=-1, keepdims=True)
    inv = lax.rsqrt(jnp.mean(centre * centre, axis=-1, keepdims=True) + ln_eps)
    hat = centre * inv
    mean_g = jnp.mean(g, axis=-1, keepdims=True)
    mean_gx = jnp.mean(g * hat, axis=-1, keepdims=True)
    cot = c_ref[...].astype(f32).reshape(tokens, width)
    o_ref[...] = (cot + inv * (g - mean_g - hat * mean_gx)).astype(bf16).reshape(o_ref.shape)


def segments(len_ref, cut_ref, block, parts):
    count, docs = len_ref.shape
    last = parts + docs - 1
    for s in range(count):
        ends = []
        for d in range(docs - 1):
            ends.append(len_ref[s, d] + (ends[-1] if ends else 0))
        cut_ref[s, 0] = 0
        cut_ref[s, last] = parts * block
        for d, end in enumerate(ends):
            rank = 1 + d
            for k in range(1, parts):
                rank = rank + jnp.where(end > k * block, 1, 0)
            cut_ref[s, rank] = end
        for k in range(1, parts):
            rank = k
            for end in ends:
                rank = rank + jnp.where(end <= k * block, 1, 0)
            cut_ref[s, rank] = k * block


def document(len_ref, s, at):
    start, end, total = 0, 0, 0
    for d in range(len_ref.shape[1]):
        total = total + len_ref[s, d]
        start = jnp.where(total <= at, total, start)
    total = 0
    end = 1 << 30
    for d in range(len_ref.shape[1]):
        total = total + len_ref[s, d]
        end = jnp.minimum(end, jnp.where(total > at, total, 1 << 30))
    return start, end


def within(cut_ref, s, j, block, lanes):
    start, end = cut_ref[s, j], cut_ref[s, j + 1]
    b = start // block
    rows = b * block + iota((block, lanes), 0)
    return b, (rows >= start) & (rows < end)


def column(j, s, count, lanes):
    return pl.ds(pl.multiple_of((j * count + s) * lanes, lanes), lanes)


CHUNK = 64


def arrivals(x_refs, x_scr, len_ref, len_scr, sems):
    me = lax.axis_index("seq")
    copies = [pltpu.make_async_copy(len_ref, len_scr, sems.at[0])]
    for d, x_ref in enumerate(x_refs):
        for s in range(x_ref.shape[0]):
            copies.append(pltpu.make_async_copy(x_ref.at[s], x_scr.at[s, me ^ d], sems.at[len(copies)]))
    return copies


def split_rows(y_scr, rows, cols, value, block, half):
    hi, lo = halves(value)
    for third, part in enumerate((hi, lo, hi)):
        at = (2 * third + half) * block
        y_scr[at + rows.start : at + rows.stop, cols] = part


def row_chunks(block):
    for r in range(0, block, CHUNK):
        yield slice(r, r + CHUNK), slice(block + r, block + r + CHUNK)


def conv_kernel(x0, x1, x2, x3, len_ref, vec_ref, kh_ref, f_ref, ft_ref,
                o0, o1, o2, o3, s_out, x_out, len_scr, cut_ref, x_scr, rhs_scr, s_scr, acc_scr, y_scr, out_scr, sems):
    count, block, lanes = x0.shape
    parts = kh_ref.shape[0]
    me = lax.axis_index("seq")
    copies = arrivals((x0, x1, x2, x3), x_scr, len_ref, len_scr, sems)
    for copy in copies:
        copy.start()
    for copy in copies:
        copy.wait()
    segments(len_scr, cut_ref, block, parts)
    gain, bias = vec_ref[2:3], vec_ref[3:4]
    items = cut_ref.shape[1] - 1
    for j in range(items):
        for s in range(count):
            b, keep = within(cut_ref, s, j, block, lanes)
            cols = slice((j * count + s) * lanes, (j * count + s + 1) * lanes)
            stack3(rhs_scr, cols, jnp.where(keep, x_scr[s, b] * gain + bias, 0.0))
    s_scr[...] = dot(f_ref[...], rhs_scr[...])
    saves = [pltpu.make_async_copy(s_scr, s_out, sems.at[len(copies)]),
             pltpu.make_async_copy(x_scr, x_out, sems.at[len(copies) + 1])]
    for save in saves:
        save.start()

    def own(j, _):
        for s in range(count):
            cols = column(j, s, count, lanes)
            for re, im in row_chunks(block):
                acc_scr[re, cols], acc_scr[im, cols] = cmul(
                    kh_ref[0, re], kh_ref[0, im], s_scr[re, cols], s_scr[im, cols]
                )
            start, _ = document(len_scr, s, cut_ref[s, j])
            b = cut_ref[s, j] // block
            first = j
            for i in range(items):
                first = first - jnp.where((i < j) & (cut_ref[s, i] >= start), 1, 0)

            def add(i, _):
                p = b - cut_ref[s, i] // block
                there = column(i, s, count, lanes)
                for re, im in row_chunks(block):
                    more = cmul(kh_ref[p, re], kh_ref[p, im], s_scr[re, there], s_scr[im, there])
                    acc_scr[re, cols] += more[0]
                    acc_scr[im, cols] += more[1]
                return 0

            lax.fori_loop(first, j, add, 0)
            for re, im in row_chunks(block):
                split_rows(y_scr, re, cols, acc_scr[re, cols], block, 0)
                split_rows(y_scr, re, cols, acc_scr[im, cols], block, 1)
        return 0

    lax.fori_loop(0, items, own, 0)
    acc_scr[0:block] = dot(ft_ref[...], y_scr[...])
    for j in range(items):
        for s in range(count):
            b, keep = within(cut_ref, s, j, block, lanes)
            cols = slice((j * count + s) * lanes, (j * count + s + 1) * lanes)
            out_scr[s, b] = jnp.where(keep, acc_scr[0:block, cols], out_scr[s, b])
    for d, o_ref in enumerate((o0, o1, o2, o3)):
        for s in range(count):
            o_ref[s] = out_scr[s, me ^ d].astype(bf16)
    for save in saves:
        save.wait()


def back_kernel(c0, c1, c2, c3, x_ref, len_ref, s_ref, vec_ref, kh_ref, f_ref, ft_ref,
                g0, g1, g2, g3, dkh_ref, dvec_ref,
                len_scr, cut_ref, v_scr, x_scr, rhs_scr, s_scr, sv_scr, acc_scr, y_scr, du_scr, sems):
    count, block, lanes = c0.shape
    parts = kh_ref.shape[0]
    me = lax.axis_index("seq")
    copies = arrivals((c0, c1, c2, c3), v_scr, len_ref, len_scr, sems)
    later = [pltpu.make_async_copy(s_ref, s_scr, sems.at[len(copies)]),
             pltpu.make_async_copy(x_ref, x_scr, sems.at[len(copies) + 1])]
    for copy in copies + later:
        copy.start()
    dkh_ref[...] = jnp.zeros_like(dkh_ref)
    for copy in copies:
        copy.wait()
    segments(len_scr, cut_ref, block, parts)
    items = cut_ref.shape[1] - 1
    for j in range(items):
        for s in range(count):
            b, keep = within(cut_ref, s, j, block, lanes)
            v = jnp.where(keep, v_scr[s, b].astype(f32), 0.0).astype(bf16)
            cols = slice((j * count + s) * lanes, (j * count + s + 1) * lanes)
            rhs_scr[0:block, cols] = v
            rhs_scr[block:, cols] = v
    sv_scr[...] = dot(f_ref[:, block:], rhs_scr[...])
    later[0].wait()

    def own(j, _):
        for s in range(count):
            cols = column(j, s, count, lanes)
            for re, im in row_chunks(block):
                vr, vi, ur, ui = sv_scr[re, cols], sv_scr[im, cols], s_scr[re, cols], s_scr[im, cols]
                kr, ki = kh_ref[0, re], kh_ref[0, im]
                acc_scr[re, cols] = kr * vr + ki * vi
                acc_scr[im, cols] = kr * vi - ki * vr
                dkh_ref[0, re] += vr * ur + vi * ui
                dkh_ref[0, im] += vi * ur - vr * ui
            _, end = document(len_scr, s, cut_ref[s, j])
            b = cut_ref[s, j] // block
            last = j
            for i in range(items):
                last = last + jnp.where((i > j) & (cut_ref[s, i] < end), 1, 0)

            def add(i, _):
                p = cut_ref[s, i] // block - b
                there = column(i, s, count, lanes)
                for re, im in row_chunks(block):
                    vr, vi, ur, ui = sv_scr[re, there], sv_scr[im, there], s_scr[re, cols], s_scr[im, cols]
                    kr, ki = kh_ref[p, re], kh_ref[p, im]
                    acc_scr[re, cols] += kr * vr + ki * vi
                    acc_scr[im, cols] += kr * vi - ki * vr
                    dkh_ref[p, re] += vr * ur + vi * ui
                    dkh_ref[p, im] += vi * ur - vr * ui
                return 0

            lax.fori_loop(j + 1, last + 1, add, 0)
            for re, im in row_chunks(block):
                split_rows(y_scr, re, cols, acc_scr[re, cols], block, 0)
                split_rows(y_scr, re, cols, acc_scr[im, cols], block, 1)
        return 0

    lax.fori_loop(0, items, own, 0)
    acc_scr[0:block] = dot(ft_ref[...], y_scr[...])
    for j in range(items):
        for s in range(count):
            b, keep = within(cut_ref, s, j, block, lanes)
            cols = slice((j * count + s) * lanes, (j * count + s + 1) * lanes)
            du_scr[s, b] = jnp.where(keep, acc_scr[0:block, cols], du_scr[s, b])
    for copy in later[1:]:
        copy.wait()
    gain = vec_ref[2:3]
    d_gain = jnp.zeros((8, lanes), f32)
    d_bias = jnp.zeros((8, lanes), f32)
    for d, g_ref in enumerate((g0, g1, g2, g3)):
        for s in range(count):
            for r in range(0, block, CHUNK):
                du = du_scr[s, me ^ d, r : r + CHUNK]
                d_bias += jnp.sum(du.reshape(CHUNK // 8, 8, lanes), axis=0)
                d_gain += jnp.sum((du * x_scr[s, me ^ d, r : r + CHUNK]).reshape(CHUNK // 8, 8, lanes), axis=0)
                g_ref[s, r : r + CHUNK] = (du * gain).astype(bf16)
    dvec_ref[0:1] = jnp.sum(d_gain, axis=0, keepdims=True)
    dvec_ref[1:2] = jnp.sum(d_bias, axis=0, keepdims=True)
    dvec_ref[2:3] = vec_ref[0:1]


def normal_cdf(v, bell):
    t = 1.0 / (1.0 + np.float32(0.3275911 / np.sqrt(2.0)) * jnp.abs(v))
    tail = t * (0.127414796 + t * (-0.142248368 + t * (0.7107068705 + t * (-0.7265760135 + t * 0.5307027145)))) * bell
    return jnp.where(v < 0.0, tail, 1.0 - tail)


def dense_kernel(q0, q1, q2, q3, x_any, c_any, w_ref, lb_ref,
                 out_ref, act_ref, dpre_ref, dlb_ref, d0, d1, d2, d3, x_ref, c_ref, slope_scr, pre_scr, dact_scr, sems):
    count, block, wide = q0.shape
    width = act_ref.shape[1]
    me = lax.axis_index("seq")
    copies = [pltpu.make_async_copy(x_any, x_ref, sems.at[0]), pltpu.make_async_copy(c_any, c_ref, sems.at[1])]
    for copy in copies:
        copy.start()

    def cols_of(d):
        return pl.ds(pl.multiple_of((me ^ d) * wide, wide), wide)

    def sequence(s, lb_sum):
        def slope(r, _):
            rows = pl.ds(pl.multiple_of(r * CHUNK, CHUNK), CHUNK)
            flat = pl.ds(pl.multiple_of(s * block + r * CHUNK, CHUNK), CHUNK)
            for d, q_ref in enumerate((q0, q1, q2, q3)):
                v = q_ref[s, rows].astype(f32)
                bell = jnp.exp(-0.5 * v * v)
                cdf = normal_cdf(v, bell)
                act_ref[flat, cols_of(d)] = (v * cdf).astype(bf16)
                slope_scr[rows, cols_of(d)] = cdf + v * (bell * np.float32(1.0 / np.sqrt(2.0 * np.pi)))
            return 0

        lax.fori_loop(0, block // CHUNK, slope, 0)
        whole = pl.ds(pl.multiple_of(s * block, block), block)
        pre_scr[...] = dot(act_ref[whole, :], w_ref[...])

        @pl.when(s == 0)
        def _():
            for copy in copies:
                copy.wait()

        def gate(r, total):
            rows = pl.ds(pl.multiple_of(r * 32, 32), 32)
            flat = pl.ds(pl.multiple_of(s * block + r * 32, 32), 32)
            first = pre_scr[rows, 0:width] + lb_ref[:, 0:width]
            sig = 1.0 / (1.0 + jnp.exp(-(pre_scr[rows, width:] + lb_ref[:, width:])))
            out_ref[s, rows] = (x_ref[s, rows].astype(f32) + first * sig).astype(bf16)
            d_first = c_ref[s, rows].astype(f32) * sig
            d_second = d_first * first * (1.0 - sig)
            d_pre = jnp.concatenate([d_first, d_second], axis=1).astype(bf16)
            dpre_ref[flat, :] = d_pre
            return total + jnp.sum(d_pre.astype(f32).reshape(4, 8, 2 * width), axis=0)

        lb_sum = lax.fori_loop(0, block // 32, gate, lb_sum)
        dact_scr[...] = dot(dpre_ref[whole, :], w_ref[...], NT)
        for d, o_ref in enumerate((d0, d1, d2, d3)):
            o_ref[s] = (dact_scr[:, cols_of(d)] * slope_scr[:, cols_of(d)]).astype(bf16)
        return lb_sum

    lb_sum = lax.fori_loop(0, count, sequence, jnp.zeros((8, 2 * width), f32))
    dlb_ref[...] = jnp.sum(lb_sum, axis=0, keepdims=True)


def rows_kernel(sub, nseq, masks, shared_ref, *refs):
    *w_refs, o_ref, lb_ref = refs
    cols = w_refs[0].shape[-1]
    span = o_ref.shape[0] // nseq
    me = lax.axis_index("dp")
    bias_row = shared_ref.shape[1] - 8 + 2
    t = 0
    for w_ref in w_refs:
        for slot in range(w_ref.shape[0]):
            at = pl.ds(pl.multiple_of((me ^ masks[t]) * cols, cols), cols)
            lb_ref[:, at] = shared_ref[t, bias_row : bias_row + 1, 0:cols]
            t += 1
            for c in range(nseq):
                for i in range(span // sub):
                    o_ref[c * span + i * sub : c * span + (i + 1) * sub, at] = w_ref[
                        slot, (i * nseq + c) * sub : (i * nseq + c + 1) * sub
                    ]


def weight_kernel(act_ref, dpre_ref, *o_refs):
    ndp = len(o_refs)
    part = o_refs[0].shape[1]
    for d, o_ref in enumerate(o_refs):
        at = pl.ds(pl.multiple_of((lax.axis_index("dp") ^ d) * part, part), part)
        o_ref[...] = dot(act_ref[...], dpre_ref[:, at], TN).astype(bf16)


def sum_all_kernel(*refs):
    *x_refs, o_ref = refs
    total = x_refs[0][...].astype(f32)
    for x_ref in x_refs[1:]:
        total = total + x_ref[...].astype(f32)
    o_ref[...] = total.astype(o_ref.dtype)


def state_grad_kernel(sub, length, w_any, term_any, dkh_ref, dvec_ref, dlb_ref, ft_ref, o_ref,
                      w_ref, term_ref, dk_scr, f_scr, dw_scr, y_scr, sems):
    loads = [pltpu.make_async_copy(w_any, w_ref, sems.at[0]), pltpu.make_async_copy(term_any, term_ref, sems.at[1])]
    for load in loads:
        load.start()
    ndp = o_ref.shape[0]
    n_w, lanes = w_ref.shape
    nstate = n_w // 2
    per = nstate // ndp
    groups = LANES // sub
    height = n_w // groups
    parts, twice, _ = dkh_ref.shape
    block = twice // 2
    sign = signs(block, lanes)
    for p in range(parts):
        re, im = dkh_ref[p, :block], dkh_ref[p, block:]
        if p + 1 < parts:
            re = re + sign * dkh_ref[p + 1, block:]
            im = im - sign * dkh_ref[p + 1, :block]
        stack3(y_scr, slice(p * lanes, (p + 1) * lanes), jnp.concatenate([re, im], axis=0))
    all_lags = dot(ft_ref[...], y_scr[...]) * (1.0 / block)
    for p in range(parts):
        dk_scr[p * block : (p + 1) * block] = all_lags[:, p * lanes : (p + 1) * lanes]
    at8 = iota((8, lanes), 0).astype(f32)
    for load in loads:
        load.wait()

    def one(n, _):
        (fr, fi), w = rows8(term_ref[2, pl.ds(n, 1), :], term_ref[3, pl.ds(n, 1), :])
        pows = powers(*w)
        zero = jnp.zeros((8, lanes), f32)
        s_re, s_im, e_re, e_im, h_re, h_im = (zero,) * 6
        for u in range(DOCMAX // FINE // COARSE - 1, -1, -1):
            t_re, t_im, o_re, o_im = (zero,) * 4
            for v in range(COARSE - 1, 0, -1):
                at = (u * COARSE + v) * FINE
                dk = dk_scr[at : at + FINE]
                t_re = t_re + dk * pows[v][0]
                t_im = t_im + dk * pows[v][1]
                o_re = o_re + t_re
                o_im = o_im + t_im
            t_re = t_re + dk_scr[u * COARSE * FINE : u * COARSE * FINE + FINE]
            e_re, e_im = cmul(e_re, e_im, *pows[COARSE])
            s_re, s_im = cmul(s_re, s_im, *pows[COARSE])
            h_re, h_im = cmul(h_re, h_im, *pows[COARSE])
            e_re, e_im = e_re + s_re, e_im + s_im
            s_re, s_im = s_re + t_re, s_im + t_im
            h_re, h_im = h_re + o_re, h_im + o_im
        m_re = (FINE * COARSE) * e_re + FINE * h_re + at8 * s_re
        m_im = (FINE * COARSE) * e_im + FINE * h_im + at8 * s_im
        s_re, s_im = cmul(s_re, s_im, fr, fi)
        m_re, m_im = cmul(m_re, m_im, fr, fi)
        for slot, value in enumerate((s_re, s_im, m_re, m_im)):
            f_scr[slot, pl.ds(n, 1), :] = jnp.sum(value, axis=0, keepdims=True)
        return 0

    lax.fori_loop(0, nstate, one, 0)
    a, b, z_re, z_im, one_re, one_im, far_re, far_im, den_re, den_im, inv, g_re, g_im = (
        term_ref[slot] for slot in range(TERMS)
    )
    f0, f1 = (f_scr[0], f_scr[1]), (f_scr[2], f_scr[3])
    gf_re, gf_im = cmul(g_re, g_im, *f0)
    dw_scr[0:nstate] = gf_re
    dw_scr[nstate:] = -gf_im
    inv_one = 1.0 / (one_re * one_re + one_im * one_im)
    near_re, near_im = cmul(z_re, z_im, one_re * inv_one, -one_im * inv_one)
    far_re, far_im = cmul(far_re, far_im, den_re * inv, -den_im * inv)
    q_re, q_im = cmul(length * far_re - near_re, length * far_im - near_im, *f0)
    c_re, c_im = cmul(w_ref[0:nstate], w_ref[nstate:], g_re, g_im)
    y_re, y_im = cmul(c_re, c_im, q_re + f1[0], q_im + f1[1])
    by_a = a * y_re
    by_step = by_a - b * y_im
    step = jnp.exp(dvec_ref[2:3])
    by_imag = -step * y_im
    d_step = jnp.sum(by_step, axis=0, keepdims=True)
    lane, state = iota((nstate, lanes), 1), iota((nstate, lanes), 0)
    col_a = jnp.sum(by_a, axis=1, keepdims=True)
    col_b = jnp.sum(by_imag, axis=1, keepdims=True)
    grid = jnp.where(lane == state % per, col_a, jnp.where(lane == state % per + per, col_b, 0.0))
    rates = exact_dot((iota((ndp, nstate), 0) == iota((ndp, nstate), 1) // per).astype(f32), grid)
    vecs = (d_step, dk_scr[0:1], dvec_ref[0:1], dvec_ref[1:2])
    group = iota((1, LANES), 1) // sub
    cols = dlb_ref.shape[1] // ndp
    for i in range(ndp):
        main = jnp.zeros((height, LANES), f32)
        row = jnp.zeros((1, LANES), f32)
        for u in range(groups):
            main = jnp.where(group == u, moved(dw_scr[u * height : (u + 1) * height], (u - i) * sub), main)
            if u < 4:
                row = jnp.where(group == u, moved(jnp.broadcast_to(vecs[u], (8, LANES)), (u - i) * sub)[0:1], row)
        o_ref[i] = jnp.zeros(o_ref.shape[1:], f32)
        o_ref[i, 0:height] = main
        o_ref[i, height : height + 1] = row
        o_ref[i, height + 1 : height + 2] = rates[i : i + 1]
        o_ref[i, height + 2 : height + 3, 0:cols] = dlb_ref[:, i * cols : (i + 1) * cols]


def sum_kernel(x_ref, o_ref):
    total = x_ref[0].astype(f32)
    for i in range(1, x_ref.shape[0]):
        total = total + x_ref[i].astype(f32)
    o_ref[...] = total.astype(o_ref.dtype)


def last_kernel(sub, m0, m1, m2, m3, w0, w1, w2, w3, w_ref, step_ref, skip_ref, gain_ref, bias_ref,
                lam_ref, imag_ref, lb_ref, dw_ref):
    n_w, own = w_ref.shape
    groups = LANES // sub
    height = n_w // groups
    per, cols = lam_ref.shape[1], lb_ref.shape[1]
    group = iota((1, LANES), 1) // sub
    parts = (m0, m1, m2, m3)
    for u in range(groups):
        acc = jnp.zeros(m0.shape, f32)
        for d, m_ref in enumerate(parts):
            c = lax.axis_index("seq") ^ d
            acc = jnp.where(group == c, pltpu.roll(m_ref[...], (c - u) * sub + LANES, 1), acc)
        w_ref[u * height : (u + 1) * height] = acc[0:height, 0:own]
        if u < 4:
            (step_ref, skip_ref, gain_ref, bias_ref)[u][...] = acc[height : height + 1, 0:own]
    total = m0[...] + m1[...] + m2[...] + m3[...]
    lam_ref[...] = total[height + 1 : height + 2, 0:per]
    imag_ref[...] = pltpu.roll(total, LANES - per, 1)[height + 1 : height + 2, 0:per]
    lb_ref[...] = total[height + 2 : height + 3, 0:cols]
    nseq = len(parts)
    width = w0.shape[0]
    span = width // nseq
    for c in range(nseq):
        rows = slice(c * span, (c + 1) * span)
        whole = w0[rows].astype(f32) + w1[rows].astype(f32) + w2[rows].astype(f32) + w3[rows].astype(f32)
        for i in range(span // sub):
            at = (i * nseq + c) * sub
            dw_ref[at : at + sub] = whole[i * sub : (i + 1) * sub]


def swap(x, axis, by):
    n = lax.axis_size(axis)
    return jax.tree.map(lambda v: lax.ppermute(v, axis, [(i, i ^ by) for i in range(n)]), x)


def trade(parts, axis):
    return [parts[0]] + [swap(parts[d], axis, d) for d in range(1, len(parts))]


def tie(*values):
    return lax.optimization_barrier(values)


def on_device(block_in, cotangent, ln_gain, ln_bias, lambda_log, lambda_imag, dss_weight, log_step, skip_gain,
              lin_weight, lin_bias, doc_lengths):
    ndp, nseq = lax.axis_size("dp"), lax.axis_size("seq")
    count, block, width = block_in.shape
    length = block * nseq
    own = ln_gain.shape[0]
    sub = own // nseq
    wide = width // nseq
    per = lambda_log.shape[0]
    nstate = per * ndp
    n_w = 2 * nstate
    cols = lin_weight.shape[1]
    tokens = count * block
    height = n_w * sub // LANES
    rows = height + 8
    steps = [1 << k for k in reversed(range(ndp.bit_length() - 1))]
    masks = [0]
    for step in steps:
        masks += [mask ^ step for mask in masks]

    def row(v):
        return v.reshape(1, -1)

    packed = call(partial(pack_kernel, sub), shape((1, rows, LANES)), [VM] * 8, name="pack", mib=60, us=2)(
        dss_weight.reshape(n_w, own), row(log_step), row(skip_gain), row(ln_gain), row(ln_bias),
        row(lambda_log), row(lambda_imag), row(lin_bias)
    )

    piece, piece32 = shape((count, block, wide), bf16), shape((count, block, wide))
    shared, shared_parts = packed, [packed]
    w_slots = [lin_weight[None]]
    f_table = hats = None
    for number, step in enumerate(steps):
        if number == 2:
            shared, hats[1] = tie(shared, hats[1])
        more = swap(shared, "dp", step)
        if number == 0:
            f_table, ft_table = call(
                table_kernel, [shape((2 * block, 3 * block), bf16), shape((block, 6 * block), bf16)], [], name="tables", us=2
            )()
            more, f_table, ft_table, x_late = tie(more, f_table, ft_table, block_in)
        elif number == 1:
            hats = call(
                partial(ln_kernel, own, sub), [piece32] * nseq, [AN],
                scratch=[pltpu.VMEM((count, block, width), bf16), DMA((count,))], name="layer_norm", us=2,
            )(x_late)
            more, *hats = tie(more, *hats)
            hats = trade(hats, "seq")
        shared_parts.append(more)
        if number < len(steps) - 1:
            shared = jnp.concatenate([shared, more], axis=0)

    w_more = swap(w_slots[0], "dp", steps[0])

    spec = (nseq, 2 * block, wide)
    kh, vec, w_all, terms = call(
        partial(lag_kernel, sub, length, masks, len(shared_parts)),
        [shape(spec), shape((8, wide)), shape((n_w, wide)), shape((TERMS, nstate, wide))],
        [VM] * (len(shared_parts) + 1), outs=[VM, VM, AN, AN],
        scratch=[pltpu.VMEM((n_w, wide), f32), pltpu.VMEM((TERMS, nstate, wide), f32),
                 pltpu.VMEM((length, wide), f32), pltpu.VMEM((2, nstate, wide), f32),
                 pltpu.VMEM((3 * block, nseq * wide), bf16), pltpu.VMEM((2 * block, nseq * wide), f32), DMA((2,))],
        name="lag_kernel", us=6, keep=[ft_table],
    )(*shared_parts, f_table)

    kh, w_more = tie(kh, w_more)
    w_late = jnp.concatenate([w_slots[0], w_more], axis=0)
    ahead = steps[1:]
    if len(ahead) == 2:
        w_slots = [w_late, swap(w_late, "dp", ahead[0]), swap(w_late, "dp", ahead[1])]
    else:
        w_slots = [w_late]
        for step in ahead:
            w_slots = [jnp.concatenate(w_slots + [swap(slot, "dp", step) for slot in w_slots], axis=0)]

    blocks4 = (count, nseq, block, wide)
    items = nseq + doc_lengths.shape[1] - 1
    lens = pltpu.SMEM(doc_lengths.shape, i32)
    cuts = pltpu.SMEM((count, items + 1), i32)
    across = items * count * wide
    *convs, spectra_u, x_blocks = call(
        conv_kernel, [piece] * nseq + [shape((2 * block, across)), shape(blocks4)],
        [AN] * (nseq + 1) + [VM] * 4, outs=[VM] * nseq + [AN, AN],
        scratch=[lens, cuts, pltpu.VMEM(blocks4, f32), pltpu.VMEM((3 * block, across), bf16),
                 pltpu.VMEM((2 * block, across), f32), pltpu.VMEM((2 * block, across), f32),
                 pltpu.VMEM((6 * block, across), bf16), pltpu.VMEM(blocks4, f32), DMA((count * nseq + 3,))],
        name="doc_conv", mib=24, us=7, keep=[w_all, terms],
    )(*hats, doc_lengths, vec, kh, f_table, ft_table)
    keep = [w_all, terms, vec, kh, f_table, ft_table, spectra_u, x_blocks]
    if len(ahead) == 2:
        *convs, w_slots[1], w_slots[2] = tie(*convs, w_slots[1], w_slots[2])
        w_slots.append(swap(w_slots[1], "dp", ahead[1]))
    convs = trade(convs, "seq")
    if cols % LANES == 0 and sub % 16 == 0:
        shared = jnp.concatenate([shared, shared_parts[-1]], axis=0)
        shared, convs[1] = tie(shared, convs[1])
        w_lin, bias_full = call(
            partial(rows_kernel, sub, nseq, masks), [shape((width, 2 * width), bf16), shape((1, 2 * width))],
            [VM] * (1 + len(w_slots)), name="linear_rows", us=1, keep=keep,
        )(shared, *w_slots)
    else:
        shared = jnp.concatenate([shared, shared_parts[-1]], axis=0)
        place = jnp.asarray([masks.index(i) for i in range(ndp)])[lax.axis_index("dp") ^ jnp.arange(ndp)]
        w_lin = jnp.take(jnp.concatenate(w_slots, axis=0), place, axis=0)
        w_lin = w_lin.reshape(ndp, ndp, nseq, sub, cols).transpose(2, 1, 3, 0, 4).reshape(width, 2 * width)
        bias_full = jnp.take(shared[:, height + 2, :cols], place, axis=0).reshape(1, 2 * width)

    block_out, act, d_pre, d_lin_bias, *d_convs = call(
        dense_kernel,
        [shape((count, block, width), bf16), shape((tokens, width), bf16), shape((tokens, 2 * width), bf16),
         shape((1, 2 * width))] + [piece] * nseq,
        [VM] * nseq + [AN, AN, VM, VM],
        scratch=[pltpu.VMEM((count, block, width), bf16), pltpu.VMEM((count, block, width), bf16),
                 pltpu.VMEM((block, width), f32), pltpu.VMEM((block, 2 * width), f32), pltpu.VMEM((block, width), f32), DMA((2,))],
        name="gated_linear", mib=16, us=5, keep=keep,
    )(*convs, block_in, cotangent, w_lin, bias_full)
    d_convs = trade(d_convs, "seq")

    act, d_pre, d_convs[1] = tie(act, d_pre, d_convs[1])
    if cols % LANES == 0:
        dw_parts = call(
            weight_kernel, [shape((width, cols), bf16)] * ndp, [VM, VM], name="weight_grad", us=1, keep=keep
        )(act, d_pre)
        dw_parts = trade(dw_parts, "dp")
    else:
        full = lax.dot_general(act, d_pre, TN, preferred_element_type=f32).astype(bf16)
        full = full.reshape(width, ndp, cols).transpose(1, 0, 2)
        dw_parts = list(lax.all_to_all(full, "dp", 0, 0, tiled=True))

    out = call(
        back_kernel, [piece] * nseq + [shape(spec), shape((3, wide))],
        [AN] * (nseq + 3) + [VM] * 4,
        scratch=[lens, cuts, pltpu.VMEM(blocks4, bf16), pltpu.VMEM(blocks4, f32),
                 pltpu.VMEM((2 * block, across), bf16), pltpu.VMEM((2 * block, across), f32),
                 pltpu.VMEM((2 * block, across), f32), pltpu.VMEM((2 * block, across), f32),
                 pltpu.VMEM((6 * block, across), bf16), pltpu.VMEM(blocks4, f32), DMA((count * nseq + 3,))],
        name="doc_conv_grad", mib=30, us=8, keep=[w_all, terms],
    )(*d_convs, x_blocks, doc_lengths, spectra_u, vec, kh, f_table, ft_table)
    g_own, dkh, d_norm = out[:nseq], out[nseq], out[nseq + 1]
    gs = trade(g_own, "seq")

    small = call(
        partial(state_grad_kernel, sub, length), shape((ndp, rows, LANES)), [AN, AN] + [VM] * 4,
        scratch=[pltpu.VMEM((n_w, wide), f32), pltpu.VMEM((TERMS, nstate, wide), f32),
                 pltpu.VMEM((length, wide), f32), pltpu.VMEM((4, nstate, wide), f32), pltpu.VMEM((n_w, wide), f32),
                 pltpu.VMEM((6 * block, nseq * wide), bf16), DMA((2,))],
        name="state_grad", mib=10, us=10,
    )(w_all, terms, dkh, d_norm, d_lin_bias, ft_table)
    small, dw_parts, gs = tie(small, tuple(dw_parts), tuple(gs))
    small = lax.all_to_all(small, "dp", 0, 0, tiled=True)
    dw_own = call(sum_all_kernel, shape((width, cols), bf16), [VM] * ndp, name="weight_sum")(*dw_parts)
    dws = trade([dw_own] * nseq, "seq")
    gs, dws[1] = tie(gs, dws[1])
    grad_in = call(
        partial(ln_back_kernel, own, sub), shape((count, block, width), bf16), [VM] * (nseq + 2),
        name="layer_norm_grad", mib=12,
    )(*gs, block_in, cotangent)
    small, grad_in, *dws = tie(small, grad_in, *dws)
    small = call(sum_kernel, shape((rows, LANES)), [VM], name="small_sum", us=0.5)(small)
    smalls = trade([small] * nseq, "seq")
    d_w, d_step, d_skip, d_gain, d_bias, d_lam, d_imag, d_lb, dw = call(
        partial(last_kernel, sub),
        [shape((n_w, own))] + [shape((1, own))] * 4 + [shape((1, per))] * 2 + [shape((1, cols)), shape((width, cols))],
        [VM] * (2 * nseq), name="last", us=1,
    )(*smalls, *dws)
    return (
        block_out, grad_in, d_gain.reshape(own), d_bias.reshape(own), d_lam.reshape(per), d_imag.reshape(per),
        d_w.reshape(2, nstate, own), d_step.reshape(own), d_skip.reshape(own), dw, d_lb.reshape(cols),
    )


def solution(mesh):
    placed = (
        P("dp", "seq", None), P("dp", "seq", None), P("dp"), P("dp"), P("dp"), P("dp"),
        P(None, None, "dp"), P("dp"), P("dp"), P(None, "dp"), P("dp"), P("dp", None),
    )
    return jax.shard_map(
        on_device,
        mesh=mesh,
        in_specs=placed,
        out_specs=(
            P("dp", "seq", None), P("dp", "seq", None), P("dp"), P("dp"), P("dp"), P("dp"),
            P(None, None, "dp"), P("dp"), P("dp"), P(None, "dp"), P("dp"),
        ),
        check_vma=False,
    )
```

```python
from functools import partial

import jax
import jax.numpy as jnp
import numpy as np
from jax import lax
from jax.experimental import pallas as pl
from jax.experimental.pallas import tpu as pltpu
from jax.sharding import PartitionSpec as P

f32, bf16, i32 = jnp.float32, jnp.bfloat16, jnp.int32
ln_eps = 1e-05
DOCMAX = 800
FINE = 8
COARSE = 10
LANES = 128
NN = (((1,), (0,)), ((), ()))
NT = (((1,), (1,)), ((), ()))
TN = (((0,), (0,)), ((), ()))
VM = pl.BlockSpec(memory_space=pltpu.VMEM)
AN = pl.BlockSpec(memory_space=pl.ANY)
DMA = pltpu.SemaphoreType.DMA


def dot(a, b, dims=NN):
    return lax.dot_general(a, b, dims, preferred_element_type=f32)


def exact_dot(a, b, dims=NN):
    return lax.dot_general(a, b, dims, precision=lax.Precision.HIGHEST, preferred_element_type=f32)


def shape(dims, dtype=f32):
    return jax.ShapeDtypeStruct(dims, dtype)


def call(body, out, specs, scratch=(), name=None, mib=8, outs=None, us=0, keep=()):
    inputs, kept = len(specs), len(keep)

    def whole(*refs):
        body(*refs[:inputs], *refs[inputs + kept :])

    kernel = pl.pallas_call(
        whole,
        out_shape=out,
        in_specs=list(specs) + [AN] * kept,
        out_specs=outs if outs is not None else jax.tree.map(lambda _: VM, out),
        scratch_shapes=list(scratch),
        cost_estimate=pl.CostEstimate(flops=int(us * 1.15e9), bytes_accessed=1000, transcendentals=0),
        compiler_params=pltpu.CompilerParams(vmem_limit_bytes=mib * 2**20),
        name=name,
    )
    return lambda *args: kernel(*args, *keep)


def iota(dims, axis):
    return lax.broadcasted_iota(i32, dims, axis)


def cmul(ar, ai, br, bi):
    return ar * br - ai * bi, ar * bi + ai * br


def small_expm1(a):
    poly = jnp.full_like(a, 1.0)
    for k in range(9, 1, -1):
        poly = 1.0 + poly * a * (1.0 / k)
    return jnp.where(jnp.abs(a) < 0.5, a * poly, jnp.exp(a) - 1.0)


def state_terms(rate_log, freq, step_log, length):
    step = jnp.exp(step_log)
    a = -jnp.exp(rate_log) * step
    b = freq * step
    half = jnp.sin(0.5 * b)
    cos_b, sin_b, mag = jnp.cos(b), jnp.sin(b), jnp.exp(a)
    one_re = 2.0 * half * half - small_expm1(a) * cos_b
    one_im = -mag * sin_b
    far = jnp.exp(length * a)
    far_re, far_im = far * jnp.cos(length * b), far * jnp.sin(length * b)
    den_re, den_im = 1.0 - far_re, -far_im
    inv = 1.0 / (den_re * den_re + den_im * den_im)
    g_re = (one_re * den_re + one_im * den_im) * inv
    g_im = (one_im * den_re - one_re * den_im) * inv
    return a, b, mag * cos_b, mag * sin_b, one_re, one_im, far_re, far_im, den_re, den_im, inv, g_re, g_im


TERMS = 13


def rows8(zr, zi):
    dims = (8, zr.shape[-1])
    at = iota(dims, 0)
    r1, i1 = jnp.broadcast_to(zr, dims), jnp.broadcast_to(zi, dims)
    r2, i2 = cmul(r1, i1, r1, i1)
    r4, i4 = cmul(r2, i2, r2, i2)
    p = (jnp.where(at & 1 > 0, r1, 1.0), jnp.where(at & 1 > 0, i1, 0.0))
    p = cmul(*p, jnp.where(at & 2 > 0, r2, 1.0), jnp.where(at & 2 > 0, i2, 0.0))
    p = cmul(*p, jnp.where(at & 4 > 0, r4, 1.0), jnp.where(at & 4 > 0, i4, 0.0))
    return p, cmul(r4, i4, r4, i4)


def powers(wr, wi):
    pows = [None, (wr, wi)]
    for v in range(2, COARSE + 1):
        pows.append(cmul(*pows[v // 2], *pows[v - v // 2]))
    return pows


def halves(x):
    hi = x.astype(bf16)
    return hi, (x - hi.astype(f32)).astype(bf16)


def stack3(ref, cols, x):
    height = x.shape[0]
    hi, lo = halves(x)
    ref[0:height, cols] = hi
    ref[height : 2 * height, cols] = lo
    ref[2 * height : 3 * height, cols] = hi


def signs(block, lanes):
    return jnp.where(iota((block, lanes), 0) & 1 > 0, -1.0, 1.0)


def dft_tables(block):
    k, j = np.arange(block)[:, None], np.arange(block)[None, :]
    theta = np.pi * (((2 * k + 1) * j) % (4 * block)) / (2 * block)
    full = np.concatenate([np.cos(theta), -np.sin(theta)], axis=0)
    high = full.astype(jnp.bfloat16)
    low = (full - high.astype(np.float64)).astype(jnp.bfloat16)
    return (jnp.asarray(np.concatenate([high, high, low], axis=1)),
            jnp.asarray(np.concatenate([high.T, high.T, low.T], axis=1)))


def moved(x, by):
    return x if by % LANES == 0 else pltpu.roll(x, by % LANES, 1)


def pack_kernel(sub, w_ref, step_ref, skip_ref, gain_ref, bias_ref, lam_ref, imag_ref, lb_ref, o_ref):
    own, per, cols = step_ref.shape[1], lam_ref.shape[1], lb_ref.shape[1]
    groups = LANES // sub
    height = w_ref.shape[0] // groups
    pick = (iota((own, LANES), 0) == lax.axis_index("seq") * sub + iota((own, LANES), 1) % sub).astype(f32)
    w = exact_dot(w_ref[...], pick)
    vec = exact_dot(jnp.concatenate([step_ref[...], skip_ref[...], gain_ref[...], bias_ref[...]] * 2, axis=0), pick)
    group = iota((1, LANES), 1) // sub
    main = jnp.zeros((height, LANES), f32)
    row = jnp.zeros((1, LANES), f32)
    for u in range(groups):
        main = jnp.where(group == u, w[u * height : (u + 1) * height], main)
        if u < 4:
            row = jnp.where(group == u, vec[u : u + 1], row)
    spot, lane = iota((per, LANES), 0), iota((per, LANES), 1)
    rates = exact_dot(jnp.broadcast_to(lam_ref[...], (8, per)), (lane == spot).astype(f32)) + exact_dot(
        jnp.broadcast_to(imag_ref[...], (8, per)), (lane == spot + per).astype(f32)
    )
    o_ref[...] = jnp.zeros(o_ref.shape, f32)
    o_ref[0, 0:height] = main
    o_ref[0, height : height + 1] = row
    o_ref[0, height + 1 : height + 2] = rates[0:1]
    o_ref[0, height + 2 : height + 3, 0:cols] = lb_ref[...]


def lag_kernel(sub, length, masks, n_parts, *refs):
    pieces, refs = refs[:n_parts], refs[n_parts:]
    f_ref, kh_ref, vec_ref, w_ref, term_ref, k_scr, z_scr, rhs_scr, kf_scr = refs
    slots = [piece.at[t] for piece in pieces for t in range(piece.shape[0])]
    ndp = len(slots)
    me = lax.axis_index("dp")
    n_w, lanes = w_ref.shape
    nstate = n_w // 2
    per = nstate // ndp
    groups = LANES // sub
    height = n_w // groups
    block = f_ref.shape[0] // 2
    group = iota((1, LANES), 1) // sub
    for u in range(groups):
        acc = jnp.zeros(slots[0].shape, f32)
        for t in range(ndp):
            i = me ^ masks[t]
            acc = jnp.where(group == i, pltpu.roll(slots[t][...], (i - u) * sub + LANES * ndp, 1), acc)
        w_ref[u * height : (u + 1) * height] = acc[0:height]
        if u < 4:
            vec_ref[u : u + 1] = acc[height : height + 1]
    vec_ref[4:8] = jnp.zeros((4, lanes), f32)
    rows = jnp.concatenate([slot[height + 1 : height + 2] for slot in slots], axis=0)
    source = jnp.zeros((nstate, ndp), i32)
    for t in range(ndp):
        source = jnp.where(iota((nstate, ndp), 1) == t, me ^ masks[t], source)
    spread = exact_dot((iota((nstate, ndp), 0) // per == source).astype(f32), rows)
    lane, state = iota((nstate, lanes), 1), iota((nstate, lanes), 0)
    lam = jnp.sum(jnp.where(lane == state % per, spread, 0.0), axis=1, keepdims=True)
    imag = jnp.sum(jnp.where(lane == state % per + per, spread, 0.0), axis=1, keepdims=True)
    terms = state_terms(lam, imag, vec_ref[0:1], float(length))
    for slot, value in enumerate(terms):
        term_ref[slot] = value
    z_scr[0], z_scr[1] = cmul(w_ref[0:nstate], w_ref[nstate:], terms[11], terms[12])
    k_scr[...] = jnp.zeros_like(k_scr)

    def pair(m, _):
        ready = []
        for n in (2 * m, 2 * m + 1):
            (fr, fi), w = rows8(term_ref[2, pl.ds(n, 1), :], term_ref[3, pl.ds(n, 1), :])
            cr = jnp.broadcast_to(z_scr[0, pl.ds(n, 1), :], (8, lanes))
            ci = jnp.broadcast_to(z_scr[1, pl.ds(n, 1), :], (8, lanes))
            ready.append([cmul(fr, fi, cr, ci), powers(*w)])
        for u in range(DOCMAX // FINE // COARSE):
            for v in range(COARSE):
                at = (u * COARSE + v) * FINE
                total = k_scr[at : at + FINE]
                for (xr, xi), pows in ready:
                    total = total + (xr * pows[v][0] - xi * pows[v][1] if v else xr)
                k_scr[at : at + FINE] = total
            for one in ready:
                one[0] = cmul(*one[0], *one[1][COARSE])
        return 0

    lax.fori_loop(0, nstate // 2, pair, 0)
    k_scr[0:1] += vec_ref[1:2]
    parts = length // block
    for p in range(parts):
        stack3(rhs_scr, slice(p * lanes, (p + 1) * lanes), k_scr[p * block : (p + 1) * block])
    kf_scr[...] = dot(f_ref[...], rhs_scr[...])
    sign = signs(block, lanes)
    for p in range(parts):
        here, past = slice(p * lanes, (p + 1) * lanes), slice((p - 1) * lanes, p * lanes)
        re, im = kf_scr[:block, here], kf_scr[block:, here]
        if p:
            re = re - sign * kf_scr[block:, past]
            im = im + sign * kf_scr[:block, past]
        kh_ref[p, :block] = re * (1.0 / block)
        kh_ref[p, block:] = im * (1.0 / block)


def members(own, sub, c, width, wide):
    lane = iota((1, wide), 1)
    return (iota((width, wide), 0) == (lane // sub) * own + c * sub + lane % sub).astype(f32).astype(bf16)


def ln_kernel(own, sub, x_any, *refs):
    *o_refs, x_ref, sems = refs
    count, block, width = x_ref.shape
    wide = o_refs[0].shape[-1]
    copies = [pltpu.make_async_copy(x_any.at[s], x_ref.at[s], sems.at[s]) for s in range(count)]
    for copy in copies:
        copy.start()
    places = [members(own, sub, lax.axis_index("seq") ^ d, width, wide) for d in range(len(o_refs))]
    for s in range(count):
        copies[s].wait()
        x = x_ref[s].astype(f32)
        centre = x - jnp.mean(x, axis=-1, keepdims=True)
        spread = jnp.mean(centre * centre, axis=-1, keepdims=True)
        hi, lo = halves(centre * lax.rsqrt(spread + ln_eps))
        for o_ref, cols in zip(o_refs, places):
            o_ref[s] = dot(hi, cols) + dot(lo, cols)


def ln_back_kernel(own, sub, g0, g1, g2, g3, x_ref, c_ref, o_ref):
    count, block, width = x_ref.shape
    wide = g0.shape[-1]
    tokens = count * block
    g = jnp.zeros((tokens, width), f32)
    for d, g_ref in enumerate((g0, g1, g2, g3)):
        cols = members(own, sub, lax.axis_index("seq") ^ d, width, wide)
        g = g + dot(g_ref[...].reshape(tokens, wide), cols, NT)
    x = x_ref[...].astype(f32).reshape(tokens, width)
    centre = x - jnp.mean(x, axis=-1, keepdims=True)
    inv = lax.rsqrt(jnp.mean(centre * centre, axis=-1, keepdims=True) + ln_eps)
    hat = centre * inv
    mean_g = jnp.mean(g, axis=-1, keepdims=True)
    mean_gx = jnp.mean(g * hat, axis=-1, keepdims=True)
    cot = c_ref[...].astype(f32).reshape(tokens, width)
    o_ref[...] = (cot + inv * (g - mean_g - hat * mean_gx)).astype(bf16).reshape(o_ref.shape)


def segments(len_ref, cut_ref, block, parts):
    count, docs = len_ref.shape
    last = parts + docs - 1
    for s in range(count):
        ends = []
        for d in range(docs - 1):
            ends.append(len_ref[s, d] + (ends[-1] if ends else 0))
        cut_ref[s, 0] = 0
        cut_ref[s, last] = parts * block
        for d, end in enumerate(ends):
            rank = 1 + d
            for k in range(1, parts):
                rank = rank + jnp.where(end > k * block, 1, 0)
            cut_ref[s, rank] = end
        for k in range(1, parts):
            rank = k
            for end in ends:
                rank = rank + jnp.where(end <= k * block, 1, 0)
            cut_ref[s, rank] = k * block


def document(len_ref, s, at):
    start, end, total = 0, 0, 0
    for d in range(len_ref.shape[1]):
        total = total + len_ref[s, d]
        start = jnp.where(total <= at, total, start)
    total = 0
    end = 1 << 30
    for d in range(len_ref.shape[1]):
        total = total + len_ref[s, d]
        end = jnp.minimum(end, jnp.where(total > at, total, 1 << 30))
    return start, end


def within(cut_ref, s, j, block, lanes):
    start, end = cut_ref[s, j], cut_ref[s, j + 1]
    b = start // block
    rows = b * block + iota((block, lanes), 0)
    return b, (rows >= start) & (rows < end)


def column(j, s, count, lanes):
    return pl.ds(pl.multiple_of((j * count + s) * lanes, lanes), lanes)


CHUNK = 64


def lengths_in(len_ref, len_scr, sem):
    copy = pltpu.make_async_copy(len_ref, len_scr, sem)
    copy.start()
    copy.wait()


def split_rows(y_scr, rows, cols, value, block, half):
    hi, lo = halves(value)
    for third, part in enumerate((hi, lo, hi)):
        at = (2 * third + half) * block
        y_scr[at + rows.start : at + rows.stop, cols] = part


def row_chunks(block):
    for r in range(0, block, CHUNK):
        yield slice(r, r + CHUNK), slice(block + r, block + r + CHUNK)


def conv_kernel(x0, x1, x2, x3, len_ref, vec_ref, kh_ref, f_ref, ft_ref,
                o0, o1, o2, o3, s_scr, x_scr, len_scr, cut_ref, rhs_scr, acc_scr, y_scr, out_scr, sem):
    count, block, lanes = x0.shape
    parts = kh_ref.shape[0]
    me = lax.axis_index("seq")
    lengths_in(len_ref, len_scr, sem)
    for d, x_ref in enumerate((x0, x1, x2, x3)):
        for s in range(count):
            x_scr[s, me ^ d] = x_ref[s]
    segments(len_scr, cut_ref, block, parts)
    gain, bias = vec_ref[2:3], vec_ref[3:4]
    items = cut_ref.shape[1] - 1
    for j in range(items):
        for s in range(count):
            b, keep = within(cut_ref, s, j, block, lanes)
            cols = slice((j * count + s) * lanes, (j * count + s + 1) * lanes)
            stack3(rhs_scr, cols, jnp.where(keep, x_scr[s, b] * gain + bias, 0.0))
    s_scr[...] = dot(f_ref[...], rhs_scr[...])

    def own(j, _):
        for s in range(count):
            cols = column(j, s, count, lanes)
            for re, im in row_chunks(block):
                acc_scr[re, cols], acc_scr[im, cols] = cmul(
                    kh_ref[0, re], kh_ref[0, im], s_scr[re, cols], s_scr[im, cols]
                )
            start, _ = document(len_scr, s, cut_ref[s, j])
            b = cut_ref[s, j] // block
            first = j
            for i in range(items):
                first = first - jnp.where((i < j) & (cut_ref[s, i] >= start), 1, 0)

            def add(i, _):
                p = b - cut_ref[s, i] // block
                there = column(i, s, count, lanes)
                for re, im in row_chunks(block):
                    more = cmul(kh_ref[p, re], kh_ref[p, im], s_scr[re, there], s_scr[im, there])
                    acc_scr[re, cols] += more[0]
                    acc_scr[im, cols] += more[1]
                return 0

            lax.fori_loop(first, j, add, 0)
            for re, im in row_chunks(block):
                split_rows(y_scr, re, cols, acc_scr[re, cols], block, 0)
                split_rows(y_scr, re, cols, acc_scr[im, cols], block, 1)
        return 0

    lax.fori_loop(0, items, own, 0)
    acc_scr[0:block] = dot(ft_ref[...], y_scr[...])
    for j in range(items):
        for s in range(count):
            b, keep = within(cut_ref, s, j, block, lanes)
            cols = slice((j * count + s) * lanes, (j * count + s + 1) * lanes)
            out_scr[s, b] = jnp.where(keep, acc_scr[0:block, cols], out_scr[s, b])
    for d, o_ref in enumerate((o0, o1, o2, o3)):
        for s in range(count):
            o_ref[s] = out_scr[s, me ^ d].astype(bf16)


def back_kernel(c0, c1, c2, c3, x_scr, len_ref, s_scr, vec_ref, kh_ref, f_ref, ft_ref,
                g0, g1, g2, g3, dkh_ref, dvec_ref,
                len_scr, cut_ref, v_scr, rhs_scr, sv_scr, acc_scr, y_scr, du_scr, sem):
    count, block, lanes = c0.shape
    parts = kh_ref.shape[0]
    me = lax.axis_index("seq")
    lengths_in(len_ref, len_scr, sem)
    for d, c_ref in enumerate((c0, c1, c2, c3)):
        for s in range(count):
            v_scr[s, me ^ d] = c_ref[s]
    dkh_ref[...] = jnp.zeros_like(dkh_ref)
    segments(len_scr, cut_ref, block, parts)
    items = cut_ref.shape[1] - 1
    for j in range(items):
        for s in range(count):
            b, keep = within(cut_ref, s, j, block, lanes)
            v = jnp.where(keep, v_scr[s, b].astype(f32), 0.0).astype(bf16)
            cols = slice((j * count + s) * lanes, (j * count + s + 1) * lanes)
            rhs_scr[0:block, cols] = v
            rhs_scr[block:, cols] = v
    sv_scr[...] = dot(f_ref[:, block:], rhs_scr[...])

    def own(j, _):
        for s in range(count):
            cols = column(j, s, count, lanes)
            for re, im in row_chunks(block):
                vr, vi, ur, ui = sv_scr[re, cols], sv_scr[im, cols], s_scr[re, cols], s_scr[im, cols]
                kr, ki = kh_ref[0, re], kh_ref[0, im]
                acc_scr[re, cols] = kr * vr + ki * vi
                acc_scr[im, cols] = kr * vi - ki * vr
                dkh_ref[0, re] += vr * ur + vi * ui
                dkh_ref[0, im] += vi * ur - vr * ui
            _, end = document(len_scr, s, cut_ref[s, j])
            b = cut_ref[s, j] // block
            last = j
            for i in range(items):
                last = last + jnp.where((i > j) & (cut_ref[s, i] < end), 1, 0)

            def add(i, _):
                p = cut_ref[s, i] // block - b
                there = column(i, s, count, lanes)
                for re, im in row_chunks(block):
                    vr, vi, ur, ui = sv_scr[re, there], sv_scr[im, there], s_scr[re, cols], s_scr[im, cols]
                    kr, ki = kh_ref[p, re], kh_ref[p, im]
                    acc_scr[re, cols] += kr * vr + ki * vi
                    acc_scr[im, cols] += kr * vi - ki * vr
                    dkh_ref[p, re] += vr * ur + vi * ui
                    dkh_ref[p, im] += vi * ur - vr * ui
                return 0

            lax.fori_loop(j + 1, last + 1, add, 0)
            for re, im in row_chunks(block):
                split_rows(y_scr, re, cols, acc_scr[re, cols], block, 0)
                split_rows(y_scr, re, cols, acc_scr[im, cols], block, 1)
        return 0

    lax.fori_loop(0, items, own, 0)
    acc_scr[0:block] = dot(ft_ref[...], y_scr[...])
    for j in range(items):
        for s in range(count):
            b, keep = within(cut_ref, s, j, block, lanes)
            cols = slice((j * count + s) * lanes, (j * count + s + 1) * lanes)
            du_scr[s, b] = jnp.where(keep, acc_scr[0:block, cols], du_scr[s, b])
    gain = vec_ref[2:3]
    d_gain = jnp.zeros((8, lanes), f32)
    d_bias = jnp.zeros((8, lanes), f32)
    for d, g_ref in enumerate((g0, g1, g2, g3)):
        for s in range(count):
            for r in range(0, block, CHUNK):
                du = du_scr[s, me ^ d, r : r + CHUNK]
                d_bias += jnp.sum(du.reshape(CHUNK // 8, 8, lanes), axis=0)
                d_gain += jnp.sum((du * x_scr[s, me ^ d, r : r + CHUNK]).reshape(CHUNK // 8, 8, lanes), axis=0)
                g_ref[s, r : r + CHUNK] = (du * gain).astype(bf16)
    dvec_ref[0:1] = jnp.sum(d_gain, axis=0, keepdims=True)
    dvec_ref[1:2] = jnp.sum(d_bias, axis=0, keepdims=True)
    dvec_ref[2:3] = vec_ref[0:1]


def normal_cdf(v, bell):
    t = 1.0 / (1.0 + np.float32(0.3275911 / np.sqrt(2.0)) * jnp.abs(v))
    tail = t * (0.127414796 + t * (-0.142248368 + t * (0.7107068705 + t * (-0.7265760135 + t * 0.5307027145)))) * bell
    return jnp.where(v < 0.0, tail, 1.0 - tail)


def dense_kernel(q0, q1, q2, q3, x_any, c_any, w_ref, lb_ref,
                 out_ref, dlb_ref, d0, d1, d2, d3, stay_ref, send_ref,
                 x_ref, c_ref, act_ref, dpre_ref, slope_scr, pre_scr, dact_scr, sems):
    count, block, wide = q0.shape
    width = act_ref.shape[1]
    me = lax.axis_index("seq")
    copies = [pltpu.make_async_copy(x_any, x_ref, sems.at[0]), pltpu.make_async_copy(c_any, c_ref, sems.at[1])]
    for copy in copies:
        copy.start()

    def cols_of(d):
        return pl.ds(pl.multiple_of((me ^ d) * wide, wide), wide)

    def sequence(s, lb_sum):
        def slope(r, _):
            rows = pl.ds(pl.multiple_of(r * CHUNK, CHUNK), CHUNK)
            flat = pl.ds(pl.multiple_of(s * block + r * CHUNK, CHUNK), CHUNK)
            for d, q_ref in enumerate((q0, q1, q2, q3)):
                v = q_ref[s, rows].astype(f32)
                bell = jnp.exp(-0.5 * v * v)
                cdf = normal_cdf(v, bell)
                act_ref[flat, cols_of(d)] = (v * cdf).astype(bf16)
                slope_scr[rows, cols_of(d)] = cdf + v * (bell * np.float32(1.0 / np.sqrt(2.0 * np.pi)))
            return 0

        lax.fori_loop(0, block // CHUNK, slope, 0)
        whole = pl.ds(pl.multiple_of(s * block, block), block)
        pre_scr[...] = dot(act_ref[whole, :], w_ref[...])

        @pl.when(s == 0)
        def _():
            for copy in copies:
                copy.wait()

        def gate(r, total):
            rows = pl.ds(pl.multiple_of(r * 32, 32), 32)
            flat = pl.ds(pl.multiple_of(s * block + r * 32, 32), 32)
            first = pre_scr[rows, 0:width] + lb_ref[:, 0:width]
            sig = 1.0 / (1.0 + jnp.exp(-(pre_scr[rows, width:] + lb_ref[:, width:])))
            out_ref[s, rows] = (x_ref[s, rows].astype(f32) + first * sig).astype(bf16)
            d_first = c_ref[s, rows].astype(f32) * sig
            d_second = d_first * first * (1.0 - sig)
            d_pre = jnp.concatenate([d_first, d_second], axis=1).astype(bf16)
            dpre_ref[flat, :] = d_pre
            return total + jnp.sum(d_pre.astype(f32).reshape(4, 8, 2 * width), axis=0)

        lb_sum = lax.fori_loop(0, block // 32, gate, lb_sum)
        dact_scr[...] = dot(dpre_ref[whole, :], w_ref[...], NT)
        for d, o_ref in enumerate((d0, d1, d2, d3)):
            o_ref[s] = (dact_scr[:, cols_of(d)] * slope_scr[:, cols_of(d)]).astype(bf16)
        return lb_sum

    lb_sum = lax.fori_loop(0, count, sequence, jnp.zeros((8, 2 * width), f32))
    dlb_ref[...] = jnp.sum(lb_sum, axis=0, keepdims=True)
    for d in range(4):
        (send_ref if d & 1 else stay_ref)[d // 2] = dot(act_ref[:, cols_of(d)], dpre_ref[...], TN).astype(bf16)


def rows_kernel(sub, nseq, masks, shared_ref, *refs):
    *w_refs, o_ref, lb_ref = refs
    cols = w_refs[0].shape[-1]
    span = o_ref.shape[0] // nseq
    me = lax.axis_index("dp")
    bias_row = shared_ref.shape[1] - 8 + 2
    for t, mask in enumerate(masks):
        at = pl.ds(pl.multiple_of((me ^ mask) * cols, cols), cols)
        lb_ref[:, at] = shared_ref[t, bias_row : bias_row + 1, 0:cols]
    t = 0
    for w_ref in w_refs:
        for slot in range(w_ref.shape[0]):
            at = pl.ds(pl.multiple_of((me ^ masks[t]) * cols, cols), cols)
            t += 1
            for c in range(nseq):
                for i in range(span // sub):
                    o_ref[c * span + i * sub : c * span + (i + 1) * sub, at] = w_ref[
                        slot, (i * nseq + c) * sub : (i * nseq + c + 1) * sub
                    ]


def halve_kernel(mine_ref, other_ref, stay_ref, send_ref):
    for k in range(mine_ref.shape[0]):
        total = mine_ref[k].astype(f32) + other_ref[k].astype(f32)
        (send_ref if k & 1 else stay_ref)[k // 2] = total.astype(stay_ref.dtype)


def deal_kernel(mine_ref, other_ref, stay_ref, send_ref):
    part = stay_ref.shape[2]
    me = lax.axis_index("dp")
    for d in range(2 * stay_ref.shape[0]):
        cols = pl.ds(pl.multiple_of((me ^ d) * part, part), part)
        (send_ref if d & 1 else stay_ref)[d // 2] = mine_ref[0, :, cols].astype(f32) + other_ref[0, :, cols].astype(f32)


def merge_kernel(x_ref, mine_ref, other_ref, o_ref):
    rows = x_ref.shape[1]
    total = x_ref[0]
    for i in range(1, x_ref.shape[0]):
        total = total + x_ref[i]
    o_ref[0:rows] = total
    o_ref[rows:] = mine_ref[0] + other_ref[0]


def state_grad_kernel(sub, length, w_ref, term_ref, dkh_ref, dvec_ref, dlb_ref, ft_ref, o_ref,
                      dk_scr, f_scr, dw_scr, y_scr):
    ndp = o_ref.shape[0]
    n_w, lanes = w_ref.shape
    nstate = n_w // 2
    per = nstate // ndp
    groups = LANES // sub
    height = n_w // groups
    parts, twice, _ = dkh_ref.shape
    block = twice // 2
    sign = signs(block, lanes)
    for p in range(parts):
        re, im = dkh_ref[p, :block], dkh_ref[p, block:]
        if p + 1 < parts:
            re = re + sign * dkh_ref[p + 1, block:]
            im = im - sign * dkh_ref[p + 1, :block]
        stack3(y_scr, slice(p * lanes, (p + 1) * lanes), jnp.concatenate([re, im], axis=0))
    all_lags = dot(ft_ref[...], y_scr[...]) * (1.0 / block)
    for p in range(parts):
        dk_scr[p * block : (p + 1) * block] = all_lags[:, p * lanes : (p + 1) * lanes]
    at8 = iota((8, lanes), 0).astype(f32)

    def one(n, _):
        (fr, fi), w = rows8(term_ref[2, pl.ds(n, 1), :], term_ref[3, pl.ds(n, 1), :])
        pows = powers(*w)
        zero = jnp.zeros((8, lanes), f32)
        s_re, s_im, e_re, e_im, h_re, h_im = (zero,) * 6
        for u in range(DOCMAX // FINE // COARSE - 1, -1, -1):
            t_re, t_im, o_re, o_im = (zero,) * 4
            for v in range(COARSE - 1, 0, -1):
                at = (u * COARSE + v) * FINE
                dk = dk_scr[at : at + FINE]
                t_re = t_re + dk * pows[v][0]
                t_im = t_im + dk * pows[v][1]
                o_re = o_re + t_re
                o_im = o_im + t_im
            t_re = t_re + dk_scr[u * COARSE * FINE : u * COARSE * FINE + FINE]
            e_re, e_im = cmul(e_re, e_im, *pows[COARSE])
            s_re, s_im = cmul(s_re, s_im, *pows[COARSE])
            h_re, h_im = cmul(h_re, h_im, *pows[COARSE])
            e_re, e_im = e_re + s_re, e_im + s_im
            s_re, s_im = s_re + t_re, s_im + t_im
            h_re, h_im = h_re + o_re, h_im + o_im
        m_re = (FINE * COARSE) * e_re + FINE * h_re + at8 * s_re
        m_im = (FINE * COARSE) * e_im + FINE * h_im + at8 * s_im
        s_re, s_im = cmul(s_re, s_im, fr, fi)
        m_re, m_im = cmul(m_re, m_im, fr, fi)
        for slot, value in enumerate((s_re, s_im, m_re, m_im)):
            f_scr[slot, pl.ds(n, 1), :] = jnp.sum(value, axis=0, keepdims=True)
        return 0

    lax.fori_loop(0, nstate, one, 0)
    a, b, z_re, z_im, one_re, one_im, far_re, far_im, den_re, den_im, inv, g_re, g_im = (
        term_ref[slot] for slot in range(TERMS)
    )
    f0, f1 = (f_scr[0], f_scr[1]), (f_scr[2], f_scr[3])
    gf_re, gf_im = cmul(g_re, g_im, *f0)
    dw_scr[0:nstate] = gf_re
    dw_scr[nstate:] = -gf_im
    inv_one = 1.0 / (one_re * one_re + one_im * one_im)
    near_re, near_im = cmul(z_re, z_im, one_re * inv_one, -one_im * inv_one)
    far_re, far_im = cmul(far_re, far_im, den_re * inv, -den_im * inv)
    q_re, q_im = cmul(length * far_re - near_re, length * far_im - near_im, *f0)
    c_re, c_im = cmul(w_ref[0:nstate], w_ref[nstate:], g_re, g_im)
    y_re, y_im = cmul(c_re, c_im, q_re + f1[0], q_im + f1[1])
    by_a = a * y_re
    by_step = by_a - b * y_im
    step = jnp.exp(dvec_ref[2:3])
    by_imag = -step * y_im
    d_step = jnp.sum(by_step, axis=0, keepdims=True)
    lane, state = iota((nstate, lanes), 1), iota((nstate, lanes), 0)
    col_a = jnp.sum(by_a, axis=1, keepdims=True)
    col_b = jnp.sum(by_imag, axis=1, keepdims=True)
    grid = jnp.where(lane == state % per, col_a, jnp.where(lane == state % per + per, col_b, 0.0))
    rates = exact_dot((iota((ndp, nstate), 0) == iota((ndp, nstate), 1) // per).astype(f32), grid)
    vecs = (d_step, dk_scr[0:1], dvec_ref[0:1], dvec_ref[1:2])
    group = iota((1, LANES), 1) // sub
    cols = dlb_ref.shape[1] // ndp
    for i in range(ndp):
        main = jnp.zeros((height, LANES), f32)
        row = jnp.zeros((1, LANES), f32)
        for u in range(groups):
            main = jnp.where(group == u, moved(dw_scr[u * height : (u + 1) * height], (u - i) * sub), main)
            if u < 4:
                row = jnp.where(group == u, moved(jnp.broadcast_to(vecs[u], (8, LANES)), (u - i) * sub)[0:1], row)
        o_ref[i] = jnp.zeros(o_ref.shape[1:], f32)
        o_ref[i, 0:height] = main
        o_ref[i, height : height + 1] = row
        o_ref[i, height + 1 : height + 2] = rates[i : i + 1]
        o_ref[i, height + 2 : height + 3, 0:cols] = dlb_ref[:, i * cols : (i + 1) * cols]


def sum_kernel(x_ref, o_ref):
    total = x_ref[0].astype(f32)
    for i in range(1, x_ref.shape[0]):
        total = total + x_ref[i].astype(f32)
    o_ref[...] = total.astype(o_ref.dtype)


def last_kernel(sub, rows, *refs):
    *parts, w_ref, step_ref, skip_ref, gain_ref, bias_ref, lam_ref, imag_ref, lb_ref, dw_ref = refs
    n_w, own = w_ref.shape
    nseq = LANES * own // sub // LANES
    parts, dws = parts[:nseq], parts[nseq:]
    groups = LANES // sub
    height = n_w // groups
    per, cols = lam_ref.shape[1], lb_ref.shape[1]
    group = iota((1, LANES), 1) // sub
    me = lax.axis_index("seq")
    small = [part[0:rows] for part in parts]
    for u in range(groups):
        acc = jnp.zeros((rows, LANES), f32)
        for d, value in enumerate(small):
            c = me ^ d
            acc = jnp.where(group == c, pltpu.roll(value, (c - u) * sub + LANES, 1), acc)
        w_ref[u * height : (u + 1) * height] = acc[0:height, 0:own]
        if u < 4:
            (step_ref, skip_ref, gain_ref, bias_ref)[u][...] = acc[height : height + 1, 0:own]
    total = sum(small[1:], small[0])
    lam_ref[...] = total[height + 1 : height + 2, 0:per]
    imag_ref[...] = pltpu.roll(total, LANES - per, 1)[height + 1 : height + 2, 0:per]
    lb_ref[...] = total[height + 2 : height + 3, 0:cols]
    for d in range(nseq):
        part_ref, first = (dws[d], 0) if dws else (parts[d], rows)
        c = me ^ d
        for i in range((part_ref.shape[0] - first) // sub):
            at = pl.multiple_of((i * nseq + c) * sub, sub)
            dw_ref[pl.ds(at, sub)] = part_ref[first + i * sub : first + (i + 1) * sub]


def swap(x, axis, by):
    n = lax.axis_size(axis)
    return jax.tree.map(lambda v: lax.ppermute(v, axis, [(i, i ^ by) for i in range(n)]), x)


def trade(parts, axis):
    return [parts[0]] + [swap(parts[d], axis, d) for d in range(1, len(parts))]


def tie(*values):
    return lax.optimization_barrier(values)


def on_device(block_in, cotangent, ln_gain, ln_bias, lambda_log, lambda_imag, dss_weight, log_step, skip_gain,
              lin_weight, lin_bias, doc_lengths):
    ndp, nseq = lax.axis_size("dp"), lax.axis_size("seq")
    count, block, width = block_in.shape
    length = block * nseq
    own = ln_gain.shape[0]
    sub = own // nseq
    wide = width // nseq
    per = lambda_log.shape[0]
    nstate = per * ndp
    n_w = 2 * nstate
    cols = lin_weight.shape[1]
    tokens = count * block
    height = n_w * sub // LANES
    rows = height + 8
    steps = [1 << k for k in reversed(range(ndp.bit_length() - 1))]
    masks = [0]
    for step in steps:
        masks += [mask ^ step for mask in masks]

    def row(v):
        return v.reshape(1, -1)

    packed = call(partial(pack_kernel, sub), shape((1, rows, LANES)), [VM] * 8, name="pack", mib=60, us=2)(
        dss_weight.reshape(n_w, own), row(log_step), row(skip_gain), row(ln_gain), row(ln_bias),
        row(lambda_log), row(lambda_imag), row(lin_bias)
    )

    piece, piece32 = shape((count, block, wide), bf16), shape((count, block, wide))
    shared, shared_parts = packed, [packed]
    w_slots = [lin_weight[None]]
    f_table, ft_table = dft_tables(block)
    w_more = hats = None
    for number, step in enumerate(steps):
        more = swap(shared, "dp", step)
        if number == 0:
            x_late, _ = tie(block_in, packed)
            hats = call(
                partial(ln_kernel, own, sub), [piece32] * nseq, [AN],
                scratch=[pltpu.VMEM((count, block, width), bf16), DMA((count,))], name="layer_norm", us=2,
            )(x_late)
            more, *hats = tie(more, *hats)
        elif number == 1:
            hats = trade(hats, "seq")
            more, hats[1] = tie(more, hats[1])
        elif number == 2:
            w_more = swap(w_slots[0], "dp", steps[0])
        shared_parts.append(more)
        if number < len(steps) - 1:
            shared = jnp.concatenate([shared, more], axis=0)

    spec = (nseq, 2 * block, wide)
    kh, vec, w_all, terms = call(
        partial(lag_kernel, sub, length, masks, len(shared_parts)),
        [shape(spec), shape((8, wide)), shape((n_w, wide)), shape((TERMS, nstate, wide))],
        [VM] * (len(shared_parts) + 1),
        scratch=[pltpu.VMEM((length, wide), f32), pltpu.VMEM((2, nstate, wide), f32),
                 pltpu.VMEM((3 * block, nseq * wide), bf16), pltpu.VMEM((2 * block, nseq * wide), f32)],
        name="lag_kernel", us=0, keep=[ft_table, block_in, cotangent],
    )(*shared_parts, f_table)

    kh, w_more = tie(kh, w_more)
    w_late = jnp.concatenate([w_slots[0], w_more], axis=0)
    ahead = steps[1:]
    if len(ahead) == 2:
        w_slots = [w_late, swap(w_late, "dp", ahead[0]), swap(w_late, "dp", ahead[1])]
    else:
        w_slots = [w_late]
        for step in ahead:
            w_slots = [jnp.concatenate(w_slots + [swap(slot, "dp", step) for slot in w_slots], axis=0)]

    blocks4 = (count, nseq, block, wide)
    items = nseq + doc_lengths.shape[1] - 1
    lens = pltpu.SMEM(doc_lengths.shape, i32)
    cuts = pltpu.SMEM((count, items + 1), i32)
    across = items * count * wide
    *convs, spectra_u, x_blocks = call(
        conv_kernel, [piece] * nseq + [shape((2 * block, across)), shape(blocks4)],
        [VM] * nseq + [AN] + [VM] * 4,
        scratch=[lens, cuts, pltpu.VMEM((3 * block, across), bf16), pltpu.VMEM((2 * block, across), f32),
                 pltpu.VMEM((6 * block, across), bf16), pltpu.VMEM(blocks4, f32), DMA],
        name="doc_conv", mib=20, us=7, keep=[w_all, terms, block_in, cotangent],
    )(*hats, doc_lengths, vec, kh, f_table, ft_table)
    keep = [w_all, terms, vec, kh, f_table, ft_table, spectra_u, x_blocks]
    if len(ahead) == 2:
        *convs, w_slots[1], w_slots[2] = tie(*convs, w_slots[1], w_slots[2])
    convs = trade(convs, "seq")
    if len(ahead) == 2:
        w_slots.append(swap(w_slots[1], "dp", ahead[1]))
    if cols % LANES == 0 and sub % 16 == 0:
        shared = jnp.concatenate([shared, shared_parts[-1]], axis=0)
        shared, convs[1] = tie(shared, convs[1])
        w_lin, bias_full = call(
            partial(rows_kernel, sub, nseq, masks), [shape((width, 2 * width), bf16), shape((1, 2 * width))],
            [VM] * (1 + len(w_slots)), name="linear_rows", us=1, keep=keep,
        )(shared, *w_slots)
    else:
        shared = jnp.concatenate([shared, shared_parts[-1]], axis=0)
        place = jnp.asarray([masks.index(i) for i in range(ndp)])[lax.axis_index("dp") ^ jnp.arange(ndp)]
        w_lin = jnp.take(jnp.concatenate(w_slots, axis=0), place, axis=0)
        w_lin = w_lin.reshape(ndp, ndp, nseq, sub, cols).transpose(2, 1, 3, 0, 4).reshape(width, 2 * width)
        bias_full = jnp.take(shared[:, height + 2, :cols], place, axis=0).reshape(1, 2 * width)

    group = shape((2, wide, 2 * width), bf16)
    block_out, d_lin_bias, *d_convs, stay, send = call(
        dense_kernel,
        [shape((count, block, width), bf16), shape((1, 2 * width))] + [piece] * nseq + [group] * 2,
        [VM] * nseq + [AN, AN, VM, VM],
        scratch=[pltpu.VMEM((count, block, width), bf16), pltpu.VMEM((count, block, width), bf16),
                 pltpu.VMEM((tokens, width), bf16), pltpu.VMEM((tokens, 2 * width), bf16),
                 pltpu.VMEM((block, width), f32), pltpu.VMEM((block, 2 * width), f32), pltpu.VMEM((block, width), f32), DMA((2,))],
        name="gated_linear", mib=16, us=5, keep=keep,
    )(*convs, block_in, cotangent, w_lin, bias_full)
    d_convs = trade(d_convs, "seq")

    staged = cols % LANES == 0
    if staged:
        stay, send = call(
            halve_kernel, [shape((1, wide, 2 * width), bf16)] * 2, [VM, VM], name="weight_half", keep=keep
        )(stay, swap(send, "seq", 1))
        d_convs[2], *_ = tie(d_convs[2], send)
        dw_other = swap(send, "seq", 2)
    else:
        full = jnp.stack([stay[0], send[0], stay[1], send[1]])
        full = full.reshape(nseq, wide, ndp, cols).transpose(2, 0, 1, 3)
        dw_own = jnp.sum(lax.all_to_all(full, "dp", 0, 0, tiled=True).astype(f32), axis=0)
        dw_own = sum(trade([dw_own[d] for d in range(nseq)], "seq"))

    out = call(
        back_kernel, [piece] * nseq + [shape(spec), shape((3, wide))],
        [VM] * (nseq + 1) + [AN] + [VM] * 5,
        scratch=[lens, cuts, pltpu.VMEM(blocks4, bf16), pltpu.VMEM((2 * block, across), bf16),
                 pltpu.VMEM((2 * block, across), f32), pltpu.VMEM((2 * block, across), f32),
                 pltpu.VMEM((6 * block, across), bf16), pltpu.VMEM(blocks4, f32), DMA],
        name="doc_conv_grad", mib=24, us=8, keep=[w_all, terms],
    )(*d_convs, x_blocks, doc_lengths, spectra_u, vec, kh, f_table, ft_table)
    g_own, dkh, d_norm = out[:nseq], out[nseq], out[nseq + 1]
    if staged:
        stay, send = call(
            deal_kernel, [shape((ndp // 2, wide, cols))] * 2, [VM, VM], name="weight_deal", us=1, keep=keep[:2]
        )(stay, dw_other)
        dkh, *_ = tie(dkh, send)
        dw_other = swap(send, "dp", 1)

    small = call(
        partial(state_grad_kernel, sub, length), shape((ndp, rows, LANES)), [VM] * 6,
        scratch=[pltpu.VMEM((length, wide), f32), pltpu.VMEM((4, nstate, wide), f32), pltpu.VMEM((n_w, wide), f32),
                 pltpu.VMEM((6 * block, nseq * wide), bf16)],
        name="state_grad", mib=10, us=10,
    )(w_all, terms, dkh, d_norm, d_lin_bias, ft_table)
    small, *g_own = tie(small, *g_own)
    if staged:
        small, dw_other = tie(small, dw_other)
    small = lax.all_to_all(small, "dp", 0, 0, tiled=True)
    gs = trade(g_own, "seq")
    if staged:
        step = 2
        while step < ndp:
            stay, send = call(
                halve_kernel, [shape((ndp // 2 // step, wide, cols))] * 2, [VM, VM], name="weight_half"
            )(stay, dw_other)
            dw_other = swap(send, "dp", step)
            step *= 2
    grad_in = call(
        partial(ln_back_kernel, own, sub), shape((count, block, width), bf16), [VM] * (nseq + 2),
        name="layer_norm_grad", mib=12,
    )(*gs, block_in, cotangent)
    if staged:
        merged = call(merge_kernel, shape((rows + wide, cols)), [VM] * 3, name="last_sums", us=0.5)(small, stay, dw_other)
        merged = trade([merged] * nseq, "seq")
        smalls, dws = merged, []
    else:
        small = call(sum_kernel, shape((rows, LANES)), [VM], name="small_sum", us=0.5)(small)
        smalls, dws = trade([small] * nseq, "seq"), trade([dw_own] * nseq, "seq")
    d_w, d_step, d_skip, d_gain, d_bias, d_lam, d_imag, d_lb, dw = call(
        partial(last_kernel, sub, rows),
        [shape((n_w, own))] + [shape((1, own))] * 4 + [shape((1, per))] * 2 + [shape((1, cols)), shape((width, cols))],
        [VM] * (len(smalls) + len(dws)), name="last", us=1,
    )(*smalls, *dws)
    return (
        block_out, grad_in, d_gain.reshape(own), d_bias.reshape(own), d_lam.reshape(per), d_imag.reshape(per),
        d_w.reshape(2, nstate, own), d_step.reshape(own), d_skip.reshape(own), dw, d_lb.reshape(cols),
    )


def solution(mesh):
    placed = (
        P("dp", "seq", None), P("dp", "seq", None), P("dp"), P("dp"), P("dp"), P("dp"),
        P(None, None, "dp"), P("dp"), P("dp"), P(None, "dp"), P("dp"), P("dp", None),
    )
    return jax.shard_map(
        on_device,
        mesh=mesh,
        in_specs=placed,
        out_specs=(
            P("dp", "seq", None), P("dp", "seq", None), P("dp"), P("dp"), P("dp"), P("dp"),
            P(None, None, "dp"), P("dp"), P("dp"), P(None, "dp"), P("dp"),
        ),
        check_vma=False,
    )
```

```python
from functools import partial

import jax
import jax.numpy as jnp
import numpy as np
from jax import lax
from jax.experimental import pallas as pl
from jax.experimental.pallas import tpu as pltpu
from jax.sharding import PartitionSpec as P

f32, bf16, i32 = jnp.float32, jnp.bfloat16, jnp.int32
ln_eps = 1e-05
DOCMAX = 800
FINE = 8
COARSE = 10
LANES = 128
NN = (((1,), (0,)), ((), ()))
NT = (((1,), (1,)), ((), ()))
TN = (((0,), (0,)), ((), ()))
VM = pl.BlockSpec(memory_space=pltpu.VMEM)
AN = pl.BlockSpec(memory_space=pl.ANY)
DMA = pltpu.SemaphoreType.DMA


def dot(a, b, dims=NN):
    return lax.dot_general(a, b, dims, preferred_element_type=f32)


def exact_dot(a, b, dims=NN):
    return lax.dot_general(a, b, dims, precision=lax.Precision.HIGHEST, preferred_element_type=f32)


def shape(dims, dtype=f32):
    return jax.ShapeDtypeStruct(dims, dtype)


def call(body, out, specs, scratch=(), name=None, mib=8, outs=None, us=0, keep=()):
    inputs, kept = len(specs), len(keep)

    def whole(*refs):
        body(*refs[:inputs], *refs[inputs + kept :])

    kernel = pl.pallas_call(
        whole,
        out_shape=out,
        in_specs=list(specs) + [AN] * kept,
        out_specs=outs if outs is not None else jax.tree.map(lambda _: VM, out),
        scratch_shapes=list(scratch),
        cost_estimate=pl.CostEstimate(flops=int(us * 1.15e9), bytes_accessed=1000, transcendentals=0),
        compiler_params=pltpu.CompilerParams(vmem_limit_bytes=mib * 2**20),
        name=name,
    )
    return lambda *args: kernel(*args, *keep)


def iota(dims, axis):
    return lax.broadcasted_iota(i32, dims, axis)


def cmul(ar, ai, br, bi):
    return ar * br - ai * bi, ar * bi + ai * br


def small_expm1(a):
    poly = jnp.full_like(a, 1.0)
    for k in range(9, 1, -1):
        poly = 1.0 + poly * a * (1.0 / k)
    return jnp.where(jnp.abs(a) < 0.5, a * poly, jnp.exp(a) - 1.0)


def state_terms(rate_log, freq, step_log, length):
    step = jnp.exp(step_log)
    a = -jnp.exp(rate_log) * step
    b = freq * step
    half = jnp.sin(0.5 * b)
    cos_b, sin_b, mag = jnp.cos(b), jnp.sin(b), jnp.exp(a)
    one_re = 2.0 * half * half - small_expm1(a) * cos_b
    one_im = -mag * sin_b
    far = jnp.exp(length * a)
    far_re, far_im = far * jnp.cos(length * b), far * jnp.sin(length * b)
    den_re, den_im = 1.0 - far_re, -far_im
    inv = 1.0 / (den_re * den_re + den_im * den_im)
    g_re = (one_re * den_re + one_im * den_im) * inv
    g_im = (one_im * den_re - one_re * den_im) * inv
    return a, b, mag * cos_b, mag * sin_b, one_re, one_im, far_re, far_im, den_re, den_im, inv, g_re, g_im


TERMS = 13


POWERS = (1, 2, 4) + tuple(8 * v for v in range(1, COARSE + 1))


def power_table(zr, zi):
    table = {1: (zr, zi)}
    for p in POWERS[1:]:
        at = p // 16 * 8 if p > 8 else p // 2
        table[p] = cmul(*table[at], *table[p - at])
    return [table[p] for p in POWERS]


def wide_row(ref, p, half, n):
    return jnp.broadcast_to(ref[2 * POWERS.index(p) + half, pl.ds(n, 1), :], (8, LANES))


def rows8(ref, n):
    at = iota((8, LANES), 0)
    total = None
    for p in (1, 2, 4):
        here = at & p > 0
        one = jnp.where(here, wide_row(ref, p, 0, n), 1.0), jnp.where(here, wide_row(ref, p, 1, n), 0.0)
        total = one if total is None else cmul(*total, *one)
    return total


def powers(ref, n):
    return [None] + [(wide_row(ref, 8 * v, 0, n), wide_row(ref, 8 * v, 1, n)) for v in range(1, COARSE + 1)]


def halves(x):
    hi = x.astype(bf16)
    return hi, (x - hi.astype(f32)).astype(bf16)


def stack3(ref, cols, x):
    height = x.shape[0]
    hi, lo = halves(x)
    ref[0:height, cols] = hi
    ref[height : 2 * height, cols] = lo
    ref[2 * height : 3 * height, cols] = hi


def signs(block, lanes):
    return jnp.where(iota((block, lanes), 0) & 1 > 0, -1.0, 1.0)


def dft_tables(block):
    k, j = np.arange(block)[:, None], np.arange(block)[None, :]
    theta = np.pi * (((2 * k + 1) * j) % (4 * block)) / (2 * block)
    full = np.concatenate([np.cos(theta), -np.sin(theta)], axis=0)
    high = full.astype(jnp.bfloat16)
    low = (full - high.astype(np.float64)).astype(jnp.bfloat16)
    return (jnp.asarray(np.concatenate([high, high, low], axis=1)),
            jnp.asarray(np.concatenate([high.T, high.T, low.T], axis=1)))


def moved(x, by):
    return x if by % LANES == 0 else pltpu.roll(x, by % LANES, 1)


def pack_kernel(sub, w_ref, step_ref, skip_ref, gain_ref, bias_ref, lam_ref, imag_ref, lb_ref, o_ref):
    own, per, cols = step_ref.shape[1], lam_ref.shape[1], lb_ref.shape[1]
    groups = LANES // sub
    height = w_ref.shape[0] // groups
    pick = (iota((own, LANES), 0) == lax.axis_index("seq") * sub + iota((own, LANES), 1) % sub).astype(f32)
    w = exact_dot(w_ref[...], pick)
    vec = exact_dot(jnp.concatenate([step_ref[...], skip_ref[...], gain_ref[...], bias_ref[...]] * 2, axis=0), pick)
    group = iota((1, LANES), 1) // sub
    main = jnp.zeros((height, LANES), f32)
    row = jnp.zeros((1, LANES), f32)
    for u in range(groups):
        main = jnp.where(group == u, w[u * height : (u + 1) * height], main)
        if u < 4:
            row = jnp.where(group == u, vec[u : u + 1], row)
    spot, lane = iota((per, LANES), 0), iota((per, LANES), 1)
    rates = exact_dot(jnp.broadcast_to(lam_ref[...], (8, per)), (lane == spot).astype(f32)) + exact_dot(
        jnp.broadcast_to(imag_ref[...], (8, per)), (lane == spot + per).astype(f32)
    )
    o_ref[...] = jnp.zeros(o_ref.shape, f32)
    o_ref[0, 0:height] = main
    o_ref[0, height : height + 1] = row
    o_ref[0, height + 1 : height + 2] = rates[0:1]
    o_ref[0, height + 2 : height + 3, 0:cols] = lb_ref[...]


def lag_kernel(sub, length, masks, n_parts, *refs):
    pieces, refs = refs[:n_parts], refs[n_parts:]
    f_ref, kh_ref, vec_ref, w_ref, term_ref, pow_ref, k_scr, z_scr, rhs_scr, kf_scr = refs
    slots = [piece.at[t] for piece in pieces for t in range(piece.shape[0])]
    ndp = len(slots)
    me = lax.axis_index("dp")
    n_w, lanes = w_ref.shape
    nstate = n_w // 2
    per = nstate // ndp
    groups = LANES // sub
    height = n_w // groups
    block = f_ref.shape[0] // 2
    group = iota((1, LANES), 1) // sub
    for u in range(groups):
        acc = jnp.zeros(slots[0].shape, f32)
        for t in range(ndp):
            i = me ^ masks[t]
            acc = jnp.where(group == i, pltpu.roll(slots[t][...], (i - u) * sub + LANES * ndp, 1), acc)
        w_ref[u * height : (u + 1) * height] = acc[0:height]
        if u < 4:
            vec_ref[u : u + 1] = acc[height : height + 1]
    vec_ref[4:8] = jnp.zeros((4, lanes), f32)
    rows = jnp.concatenate([slot[height + 1 : height + 2] for slot in slots], axis=0)
    source = jnp.zeros((nstate, ndp), i32)
    for t in range(ndp):
        source = jnp.where(iota((nstate, ndp), 1) == t, me ^ masks[t], source)
    spread = exact_dot((iota((nstate, ndp), 0) // per == source).astype(f32), rows)
    lane, state = iota((nstate, lanes), 1), iota((nstate, lanes), 0)
    lam = jnp.sum(jnp.where(lane == state % per, spread, 0.0), axis=1, keepdims=True)
    imag = jnp.sum(jnp.where(lane == state % per + per, spread, 0.0), axis=1, keepdims=True)
    terms = state_terms(lam, imag, vec_ref[0:1], float(length))
    for slot, value in enumerate(terms):
        term_ref[slot] = value
    z_scr[0], z_scr[1] = cmul(w_ref[0:nstate], w_ref[nstate:], terms[11], terms[12])
    for slot, pair in enumerate(power_table(terms[2], terms[3])):
        pow_ref[2 * slot], pow_ref[2 * slot + 1] = pair
    k_scr[...] = jnp.zeros_like(k_scr)

    def pair(m, _):
        ready = []
        for n in (2 * m, 2 * m + 1):
            fr, fi = rows8(pow_ref, n)
            cr = jnp.broadcast_to(z_scr[0, pl.ds(n, 1), :], (8, lanes))
            ci = jnp.broadcast_to(z_scr[1, pl.ds(n, 1), :], (8, lanes))
            ready.append([cmul(fr, fi, cr, ci), powers(pow_ref, n)])
        for u in range(DOCMAX // FINE // COARSE):
            for v in range(COARSE):
                at = (u * COARSE + v) * FINE
                total = k_scr[at : at + FINE]
                for (xr, xi), pows in ready:
                    total = total + (xr * pows[v][0] - xi * pows[v][1] if v else xr)
                k_scr[at : at + FINE] = total
            for one in ready:
                one[0] = cmul(*one[0], *one[1][COARSE])
        return 0

    lax.fori_loop(0, nstate // 2, pair, 0)
    k_scr[0:1] += vec_ref[1:2]
    parts = length // block
    for p in range(parts):
        stack3(rhs_scr, slice(p * lanes, (p + 1) * lanes), k_scr[p * block : (p + 1) * block])
    kf_scr[...] = dot(f_ref[...], rhs_scr[...])
    sign = signs(block, lanes)
    for p in range(parts):
        here, past = slice(p * lanes, (p + 1) * lanes), slice((p - 1) * lanes, p * lanes)
        re, im = kf_scr[:block, here], kf_scr[block:, here]
        if p:
            re = re - sign * kf_scr[block:, past]
            im = im + sign * kf_scr[:block, past]
        kh_ref[p, :block] = re * (1.0 / block)
        kh_ref[p, block:] = im * (1.0 / block)


def members(own, sub, c, width, wide):
    lane = iota((1, wide), 1)
    return (iota((width, wide), 0) == (lane // sub) * own + c * sub + lane % sub).astype(f32).astype(bf16)


def ln_kernel(own, sub, x_any, *refs):
    *o_refs, x_ref, sems = refs
    count, block, width = x_ref.shape
    wide = o_refs[0].shape[-1]
    copies = [pltpu.make_async_copy(x_any.at[s], x_ref.at[s], sems.at[s]) for s in range(count)]
    for copy in copies:
        copy.start()
    places = [members(own, sub, lax.axis_index("seq") ^ d, width, wide) for d in range(len(o_refs))]
    for s in range(count):
        copies[s].wait()
        x = x_ref[s].astype(f32)
        centre = x - jnp.mean(x, axis=-1, keepdims=True)
        spread = jnp.mean(centre * centre, axis=-1, keepdims=True)
        hi, lo = halves(centre * lax.rsqrt(spread + ln_eps))
        for o_ref, cols in zip(o_refs, places):
            o_ref[s] = dot(hi, cols) + dot(lo, cols)


def ln_back_kernel(own, sub, g0, g1, g2, g3, x_ref, c_ref, o_ref):
    count, block, width = x_ref.shape
    wide = g0.shape[-1]
    tokens = count * block
    g = jnp.zeros((tokens, width), f32)
    for d, g_ref in enumerate((g0, g1, g2, g3)):
        cols = members(own, sub, lax.axis_index("seq") ^ d, width, wide)
        g = g + dot(g_ref[...].reshape(tokens, wide), cols, NT)
    x = x_ref[...].astype(f32).reshape(tokens, width)
    centre = x - jnp.mean(x, axis=-1, keepdims=True)
    inv = lax.rsqrt(jnp.mean(centre * centre, axis=-1, keepdims=True) + ln_eps)
    hat = centre * inv
    mean_g = jnp.mean(g, axis=-1, keepdims=True)
    mean_gx = jnp.mean(g * hat, axis=-1, keepdims=True)
    cot = c_ref[...].astype(f32).reshape(tokens, width)
    o_ref[...] = (cot + inv * (g - mean_g - hat * mean_gx)).astype(bf16).reshape(o_ref.shape)


def segments(len_ref, cut_ref, block, parts):
    count, docs = len_ref.shape
    last = parts + docs - 1
    for s in range(count):
        ends = []
        for d in range(docs - 1):
            ends.append(len_ref[s, d] + (ends[-1] if ends else 0))
        cut_ref[s, 0] = 0
        cut_ref[s, last] = parts * block
        for d, end in enumerate(ends):
            rank = 1 + d
            for k in range(1, parts):
                rank = rank + jnp.where(end > k * block, 1, 0)
            cut_ref[s, rank] = end
        for k in range(1, parts):
            rank = k
            for end in ends:
                rank = rank + jnp.where(end <= k * block, 1, 0)
            cut_ref[s, rank] = k * block


def document(len_ref, s, at):
    start, end, total = 0, 0, 0
    for d in range(len_ref.shape[1]):
        total = total + len_ref[s, d]
        start = jnp.where(total <= at, total, start)
    total = 0
    end = 1 << 30
    for d in range(len_ref.shape[1]):
        total = total + len_ref[s, d]
        end = jnp.minimum(end, jnp.where(total > at, total, 1 << 30))
    return start, end


def within(cut_ref, s, j, block, lanes):
    start, end = cut_ref[s, j], cut_ref[s, j + 1]
    b = start // block
    rows = b * block + iota((block, lanes), 0)
    return b, (rows >= start) & (rows < end)


def column(j, s, count, lanes):
    return pl.ds(pl.multiple_of((j * count + s) * lanes, lanes), lanes)


CHUNK = 64


def lengths_in(len_ref, len_scr, sem):
    copy = pltpu.make_async_copy(len_ref, len_scr, sem)
    copy.start()
    copy.wait()


def split_rows(y_scr, rows, cols, value, block, half):
    hi, lo = halves(value)
    for third, part in enumerate((hi, lo, hi)):
        at = (2 * third + half) * block
        y_scr[at + rows.start : at + rows.stop, cols] = part


def row_chunks(block):
    for r in range(0, block, CHUNK):
        yield slice(r, r + CHUNK), slice(block + r, block + r + CHUNK)


def conv_kernel(x0, x1, x2, x3, len_ref, vec_ref, kh_ref, f_ref, ft_ref,
                o0, o1, o2, o3, s_scr, x_scr, len_scr, cut_ref, rhs_scr, acc_scr, y_scr, out_scr, sem):
    count, block, lanes = x0.shape
    parts = kh_ref.shape[0]
    me = lax.axis_index("seq")
    lengths_in(len_ref, len_scr, sem)
    for d, x_ref in enumerate((x0, x1, x2, x3)):
        for s in range(count):
            x_scr[s, me ^ d] = x_ref[s]
    segments(len_scr, cut_ref, block, parts)
    gain, bias = vec_ref[2:3], vec_ref[3:4]
    items = cut_ref.shape[1] - 1
    for j in range(items):
        for s in range(count):
            b, keep = within(cut_ref, s, j, block, lanes)
            cols = slice((j * count + s) * lanes, (j * count + s + 1) * lanes)
            stack3(rhs_scr, cols, jnp.where(keep, x_scr[s, b] * gain + bias, 0.0))
        tile = slice(j * count * lanes, (j + 1) * count * lanes)
        s_scr[:, tile] = dot(f_ref[...], rhs_scr[:, tile])

    def own(j, _):
        for s in range(count):
            cols = column(j, s, count, lanes)
            for re, im in row_chunks(block):
                acc_scr[re, cols], acc_scr[im, cols] = cmul(
                    kh_ref[0, re], kh_ref[0, im], s_scr[re, cols], s_scr[im, cols]
                )
            start, _ = document(len_scr, s, cut_ref[s, j])
            b = cut_ref[s, j] // block
            first = j
            for i in range(items):
                first = first - jnp.where((i < j) & (cut_ref[s, i] >= start), 1, 0)

            def add(i, _):
                p = b - cut_ref[s, i] // block
                there = column(i, s, count, lanes)
                for re, im in row_chunks(block):
                    more = cmul(kh_ref[p, re], kh_ref[p, im], s_scr[re, there], s_scr[im, there])
                    acc_scr[re, cols] += more[0]
                    acc_scr[im, cols] += more[1]
                return 0

            lax.fori_loop(first, j, add, 0)
            for re, im in row_chunks(block):
                split_rows(y_scr, re, cols, acc_scr[re, cols], block, 0)
                split_rows(y_scr, re, cols, acc_scr[im, cols], block, 1)
        return 0

    lax.fori_loop(0, items, own, 0)
    acc_scr[0:block] = dot(ft_ref[...], y_scr[...])
    for j in range(items):
        for s in range(count):
            b, keep = within(cut_ref, s, j, block, lanes)
            cols = slice((j * count + s) * lanes, (j * count + s + 1) * lanes)
            out_scr[s, b] = jnp.where(keep, acc_scr[0:block, cols], out_scr[s, b])
    for d, o_ref in enumerate((o0, o1, o2, o3)):
        for s in range(count):
            o_ref[s] = out_scr[s, me ^ d].astype(bf16)


def back_kernel(c0, c1, c2, c3, x_scr, len_ref, s_scr, vec_ref, kh_ref, f_ref, ft_ref,
                g0, g1, g2, g3, dkh_ref, dvec_ref,
                len_scr, cut_ref, v_scr, rhs_scr, sv_scr, acc_scr, y_scr, du_scr, sem):
    count, block, lanes = c0.shape
    parts = kh_ref.shape[0]
    me = lax.axis_index("seq")
    lengths_in(len_ref, len_scr, sem)
    for d, c_ref in enumerate((c0, c1, c2, c3)):
        for s in range(count):
            v_scr[s, me ^ d] = c_ref[s]
    dkh_ref[...] = jnp.zeros_like(dkh_ref)
    segments(len_scr, cut_ref, block, parts)
    items = cut_ref.shape[1] - 1
    for j in range(items):
        for s in range(count):
            b, keep = within(cut_ref, s, j, block, lanes)
            v = jnp.where(keep, v_scr[s, b].astype(f32), 0.0).astype(bf16)
            cols = slice((j * count + s) * lanes, (j * count + s + 1) * lanes)
            rhs_scr[0:block, cols] = v
            rhs_scr[block:, cols] = v
        tile = slice(j * count * lanes, (j + 1) * count * lanes)
        sv_scr[:, tile] = dot(f_ref[:, block:], rhs_scr[:, tile])

    def own(j, _):
        for s in range(count):
            cols = column(j, s, count, lanes)
            for re, im in row_chunks(block):
                vr, vi, ur, ui = sv_scr[re, cols], sv_scr[im, cols], s_scr[re, cols], s_scr[im, cols]
                kr, ki = kh_ref[0, re], kh_ref[0, im]
                acc_scr[re, cols] = kr * vr + ki * vi
                acc_scr[im, cols] = kr * vi - ki * vr
                dkh_ref[0, re] += vr * ur + vi * ui
                dkh_ref[0, im] += vi * ur - vr * ui
            _, end = document(len_scr, s, cut_ref[s, j])
            b = cut_ref[s, j] // block
            last = j
            for i in range(items):
                last = last + jnp.where((i > j) & (cut_ref[s, i] < end), 1, 0)

            def add(i, _):
                p = cut_ref[s, i] // block - b
                there = column(i, s, count, lanes)
                for re, im in row_chunks(block):
                    vr, vi, ur, ui = sv_scr[re, there], sv_scr[im, there], s_scr[re, cols], s_scr[im, cols]
                    kr, ki = kh_ref[p, re], kh_ref[p, im]
                    acc_scr[re, cols] += kr * vr + ki * vi
                    acc_scr[im, cols] += kr * vi - ki * vr
                    dkh_ref[p, re] += vr * ur + vi * ui
                    dkh_ref[p, im] += vi * ur - vr * ui
                return 0

            lax.fori_loop(j + 1, last + 1, add, 0)
            for re, im in row_chunks(block):
                split_rows(y_scr, re, cols, acc_scr[re, cols], block, 0)
                split_rows(y_scr, re, cols, acc_scr[im, cols], block, 1)
        return 0

    lax.fori_loop(0, items, own, 0)
    acc_scr[0:block] = dot(ft_ref[...], y_scr[...])
    for j in range(items):
        for s in range(count):
            b, keep = within(cut_ref, s, j, block, lanes)
            cols = slice((j * count + s) * lanes, (j * count + s + 1) * lanes)
            du_scr[s, b] = jnp.where(keep, acc_scr[0:block, cols], du_scr[s, b])
    gain = vec_ref[2:3]
    d_gain = jnp.zeros((8, lanes), f32)
    d_bias = jnp.zeros((8, lanes), f32)
    for d, g_ref in enumerate((g0, g1, g2, g3)):
        for s in range(count):
            for r in range(0, block, CHUNK):
                du = du_scr[s, me ^ d, r : r + CHUNK]
                d_bias += jnp.sum(du.reshape(CHUNK // 8, 8, lanes), axis=0)
                d_gain += jnp.sum((du * x_scr[s, me ^ d, r : r + CHUNK]).reshape(CHUNK // 8, 8, lanes), axis=0)
                g_ref[s, r : r + CHUNK] = (du * gain).astype(bf16)
    dvec_ref[0:1] = jnp.sum(d_gain, axis=0, keepdims=True)
    dvec_ref[1:2] = jnp.sum(d_bias, axis=0, keepdims=True)
    dvec_ref[2:3] = vec_ref[0:1]


def normal_cdf(v, bell):
    t = 1.0 / (1.0 + np.float32(0.3275911 / np.sqrt(2.0)) * jnp.abs(v))
    tail = t * (0.127414796 + t * (-0.142248368 + t * (0.7107068705 + t * (-0.7265760135 + t * 0.5307027145)))) * bell
    return jnp.where(v < 0.0, tail, 1.0 - tail)


def dense_kernel(q0, q1, q2, q3, x_any, c_any, w_ref, lb_ref,
                 out_ref, dlb_ref, d0, d1, d2, d3, stay_ref, send_ref,
                 x_ref, c_ref, act_ref, dpre_ref, slope_scr, pre_scr, dact_scr, sems):
    count, block, wide = q0.shape
    width = act_ref.shape[1]
    me = lax.axis_index("seq")
    copies = [pltpu.make_async_copy(x_any, x_ref, sems.at[0]), pltpu.make_async_copy(c_any, c_ref, sems.at[1])]
    for copy in copies:
        copy.start()

    def cols_of(d):
        return pl.ds(pl.multiple_of((me ^ d) * wide, wide), wide)

    def sequence(s, lb_sum):
        def slope(r, _):
            rows = pl.ds(pl.multiple_of(r * CHUNK, CHUNK), CHUNK)
            flat = pl.ds(pl.multiple_of(s * block + r * CHUNK, CHUNK), CHUNK)
            for d, q_ref in enumerate((q0, q1, q2, q3)):
                v = q_ref[s, rows].astype(f32)
                bell = jnp.exp(-0.5 * v * v)
                cdf = normal_cdf(v, bell)
                act_ref[flat, cols_of(d)] = (v * cdf).astype(bf16)
                slope_scr[rows, cols_of(d)] = cdf + v * (bell * np.float32(1.0 / np.sqrt(2.0 * np.pi)))
            return 0

        lax.fori_loop(0, block // CHUNK, slope, 0)
        whole = pl.ds(pl.multiple_of(s * block, block), block)
        pre_scr[...] = dot(act_ref[whole, :], w_ref[...])

        @pl.when(s == 0)
        def _():
            for copy in copies:
                copy.wait()

        def gate(r, total):
            rows = pl.ds(pl.multiple_of(r * 32, 32), 32)
            flat = pl.ds(pl.multiple_of(s * block + r * 32, 32), 32)
            first = pre_scr[rows, 0:width] + lb_ref[:, 0:width]
            sig = 1.0 / (1.0 + jnp.exp(-(pre_scr[rows, width:] + lb_ref[:, width:])))
            out_ref[s, rows] = (x_ref[s, rows].astype(f32) + first * sig).astype(bf16)
            d_first = c_ref[s, rows].astype(f32) * sig
            d_second = d_first * first * (1.0 - sig)
            d_pre = jnp.concatenate([d_first, d_second], axis=1).astype(bf16)
            dpre_ref[flat, :] = d_pre
            return total + jnp.sum(d_pre.astype(f32).reshape(4, 8, 2 * width), axis=0)

        lb_sum = lax.fori_loop(0, block // 32, gate, lb_sum)
        dact_scr[...] = dot(dpre_ref[whole, :], w_ref[...], NT)
        for d, o_ref in enumerate((d0, d1, d2, d3)):
            o_ref[s] = (dact_scr[:, cols_of(d)] * slope_scr[:, cols_of(d)]).astype(bf16)
        return lb_sum

    lb_sum = lax.fori_loop(0, count, sequence, jnp.zeros((8, 2 * width), f32))
    dlb_ref[...] = jnp.sum(lb_sum, axis=0, keepdims=True)
    for d in range(4):
        (send_ref if d & 1 else stay_ref)[d // 2] = dot(act_ref[:, cols_of(d)], dpre_ref[...], TN).astype(bf16)


def rows_kernel(sub, nseq, masks, shared_ref, *refs):
    *w_refs, o_ref, lb_ref = refs
    cols = w_refs[0].shape[-1]
    span = o_ref.shape[0] // nseq
    me = lax.axis_index("dp")
    bias_row = shared_ref.shape[1] - 8 + 2
    for t, mask in enumerate(masks):
        at = pl.ds(pl.multiple_of((me ^ mask) * cols, cols), cols)
        lb_ref[:, at] = shared_ref[t, bias_row : bias_row + 1, 0:cols]
    t = 0
    for w_ref in w_refs:
        for slot in range(w_ref.shape[0]):
            at = pl.ds(pl.multiple_of((me ^ masks[t]) * cols, cols), cols)
            t += 1
            for c in range(nseq):
                for i in range(span // sub):
                    o_ref[c * span + i * sub : c * span + (i + 1) * sub, at] = w_ref[
                        slot, (i * nseq + c) * sub : (i * nseq + c + 1) * sub
                    ]


def halve_kernel(mine_ref, other_ref, stay_ref, send_ref):
    for k in range(mine_ref.shape[0]):
        total = mine_ref[k].astype(f32) + other_ref[k].astype(f32)
        (send_ref if k & 1 else stay_ref)[k // 2] = total.astype(stay_ref.dtype)


def deal_kernel(mine_ref, other_ref, stay_ref, send_ref):
    part = stay_ref.shape[2]
    me = lax.axis_index("dp")
    for d in range(2 * stay_ref.shape[0]):
        cols = pl.ds(pl.multiple_of((me ^ d) * part, part), part)
        (send_ref if d & 1 else stay_ref)[d // 2] = mine_ref[0, :, cols].astype(f32) + other_ref[0, :, cols].astype(f32)


def merge_kernel(x_ref, mine_ref, other_ref, o_ref):
    rows = x_ref.shape[1]
    total = x_ref[0]
    for i in range(1, x_ref.shape[0]):
        total = total + x_ref[i]
    o_ref[0:rows] = total
    o_ref[rows:] = mine_ref[0] + other_ref[0]


PAIR = 2 * FINE


def power_kernel(pow_ref, o_ref):
    def some(g, _):
        rows = pl.ds(pl.multiple_of(g * 8, 8), 8)
        at = [2 * POWERS.index(PAIR * v) for v in range(1, COARSE // 2 + 1)]
        small = [(pow_ref[i, rows], pow_ref[i + 1, rows]) for i in at]
        x = jnp.ones((8, LANES), f32), jnp.zeros((8, LANES), f32)
        for u in range(DOCMAX // PAIR // (COARSE // 2)):
            for v in range(COARSE // 2):
                m = u * (COARSE // 2) + v
                o_ref[2 * m, rows], o_ref[2 * m + 1, rows] = cmul(*x, *small[v - 1]) if v else x
            x = cmul(*x, *small[-1])
        return 0

    lax.fori_loop(0, pow_ref.shape[1] // 8, some, 0)


CHAINS = 2


def state_grad_kernel(sub, length, w_ref, term_ref, pow_ref, far_ref, dkh_ref, dvec_ref, dlb_ref, ft_ref, o_ref,
                      dk_scr, f_scr, dw_scr, y_scr):
    ndp = o_ref.shape[0]
    n_w, lanes = w_ref.shape
    nstate = n_w // 2
    per = nstate // ndp
    groups = LANES // sub
    height = n_w // groups
    parts, twice, _ = dkh_ref.shape
    block = twice // 2
    sign = signs(block, lanes)
    for p in range(parts):
        re, im = dkh_ref[p, :block], dkh_ref[p, block:]
        if p + 1 < parts:
            re = re + sign * dkh_ref[p + 1, block:]
            im = im - sign * dkh_ref[p + 1, :block]
        stack3(y_scr, slice(p * lanes, (p + 1) * lanes), jnp.concatenate([re, im], axis=0))
    all_lags = dot(ft_ref[...], y_scr[...]) * (1.0 / block)
    for p in range(parts):
        dk_scr[p * block : (p + 1) * block] = all_lags[:, p * lanes : (p + 1) * lanes]
    at8 = iota((8, lanes), 0).astype(f32)

    def one(n, _):
        fr, fi = rows8(pow_ref, n)
        zero = jnp.zeros((8, lanes), f32)
        span = DOCMAX // PAIR // CHAINS
        sums = []
        for c in range(CHAINS):
            acc = [[zero] * 4, [zero] * 4]
            for m in range(c * span + span - 1, c * span - 1, -1):
                if m:
                    p_re = jnp.broadcast_to(far_ref[2 * m, pl.ds(n, 1), :], (8, lanes))
                    p_im = jnp.broadcast_to(far_ref[2 * m + 1, pl.ds(n, 1), :], (8, lanes))
                for h, one_acc in enumerate(acc):
                    at = m * PAIR + h * FINE
                    dk = dk_scr[at : at + FINE]
                    one_acc[0] = one_acc[0] + (dk * p_re if m else dk)
                    if m:
                        one_acc[1] = one_acc[1] + dk * p_im
                    if m > c * span:
                        one_acc[2], one_acc[3] = one_acc[2] + one_acc[0], one_acc[3] + one_acc[1]
            for one_acc in acc:
                one_acc[2], one_acc[3] = (one_acc[2 + k] + (c * span) * one_acc[k] for k in (0, 1))
            sums.append(acc)
        low, high = (
            [sum((acc[h][k] for acc in sums[1:]), sums[0][h][k]) for k in range(4)] for h in (0, 1)
        )
        for h, part in enumerate((low, high)):
            for k in (0, 1):
                part[2 + k] = PAIR * part[2 + k] + (at8 + float(h * FINE)) * part[k]
        shift = wide_row(pow_ref, FINE, 0, n), wide_row(pow_ref, FINE, 1, n)
        values = []
        for k in (0, 2):
            up = cmul(high[k], high[k + 1], *shift)
            values.append(cmul(low[k] + up[0], low[k + 1] + up[1], fr, fi))
        (s_re, s_im), (m_re, m_im) = values
        for slot, value in enumerate((s_re, s_im, m_re, m_im)):
            f_scr[slot, pl.ds(n, 1), :] = jnp.sum(value, axis=0, keepdims=True)
        return 0

    lax.fori_loop(0, nstate, one, 0, unroll=2)
    a, b, z_re, z_im, one_re, one_im, far_re, far_im, den_re, den_im, inv, g_re, g_im = (
        term_ref[slot] for slot in range(TERMS)
    )
    f0, f1 = (f_scr[0], f_scr[1]), (f_scr[2], f_scr[3])
    gf_re, gf_im = cmul(g_re, g_im, *f0)
    dw_scr[0:nstate] = gf_re
    dw_scr[nstate:] = -gf_im
    inv_one = 1.0 / (one_re * one_re + one_im * one_im)
    near_re, near_im = cmul(z_re, z_im, one_re * inv_one, -one_im * inv_one)
    far_re, far_im = cmul(far_re, far_im, den_re * inv, -den_im * inv)
    q_re, q_im = cmul(length * far_re - near_re, length * far_im - near_im, *f0)
    c_re, c_im = cmul(w_ref[0:nstate], w_ref[nstate:], g_re, g_im)
    y_re, y_im = cmul(c_re, c_im, q_re + f1[0], q_im + f1[1])
    by_a = a * y_re
    by_step = by_a - b * y_im
    step = jnp.exp(dvec_ref[2:3])
    by_imag = -step * y_im
    d_step = jnp.sum(by_step, axis=0, keepdims=True)
    lane, state = iota((nstate, lanes), 1), iota((nstate, lanes), 0)
    col_a = jnp.sum(by_a, axis=1, keepdims=True)
    col_b = jnp.sum(by_imag, axis=1, keepdims=True)
    grid = jnp.where(lane == state % per, col_a, jnp.where(lane == state % per + per, col_b, 0.0))
    rates = exact_dot((iota((ndp, nstate), 0) == iota((ndp, nstate), 1) // per).astype(f32), grid)
    vecs = (d_step, dk_scr[0:1], dvec_ref[0:1], dvec_ref[1:2])
    group = iota((1, LANES), 1) // sub
    cols = dlb_ref.shape[1] // ndp
    for i in range(ndp):
        main = jnp.zeros((height, LANES), f32)
        row = jnp.zeros((1, LANES), f32)
        for u in range(groups):
            main = jnp.where(group == u, moved(dw_scr[u * height : (u + 1) * height], (u - i) * sub), main)
            if u < 4:
                row = jnp.where(group == u, moved(jnp.broadcast_to(vecs[u], (8, LANES)), (u - i) * sub)[0:1], row)
        o_ref[i] = jnp.zeros(o_ref.shape[1:], f32)
        o_ref[i, 0:height] = main
        o_ref[i, height : height + 1] = row
        o_ref[i, height + 1 : height + 2] = rates[i : i + 1]
        o_ref[i, height + 2 : height + 3, 0:cols] = dlb_ref[:, i * cols : (i + 1) * cols]


def sum_kernel(x_ref, o_ref):
    total = x_ref[0].astype(f32)
    for i in range(1, x_ref.shape[0]):
        total = total + x_ref[i].astype(f32)
    o_ref[...] = total.astype(o_ref.dtype)


def last_kernel(sub, rows, *refs):
    *parts, w_ref, step_ref, skip_ref, gain_ref, bias_ref, lam_ref, imag_ref, lb_ref, dw_ref = refs
    n_w, own = w_ref.shape
    nseq = LANES * own // sub // LANES
    parts, dws = parts[:nseq], parts[nseq:]
    groups = LANES // sub
    height = n_w // groups
    per, cols = lam_ref.shape[1], lb_ref.shape[1]
    group = iota((1, LANES), 1) // sub
    me = lax.axis_index("seq")
    small = [part[0:rows] for part in parts]
    for u in range(groups):
        acc = jnp.zeros((rows, LANES), f32)
        for d, value in enumerate(small):
            c = me ^ d
            acc = jnp.where(group == c, pltpu.roll(value, (c - u) * sub + LANES, 1), acc)
        w_ref[u * height : (u + 1) * height] = acc[0:height, 0:own]
        if u < 4:
            (step_ref, skip_ref, gain_ref, bias_ref)[u][...] = acc[height : height + 1, 0:own]
    total = sum(small[1:], small[0])
    lam_ref[...] = total[height + 1 : height + 2, 0:per]
    imag_ref[...] = pltpu.roll(total, LANES - per, 1)[height + 1 : height + 2, 0:per]
    lb_ref[...] = total[height + 2 : height + 3, 0:cols]
    for d in range(nseq):
        part_ref, first = (dws[d], 0) if dws else (parts[d], rows)
        c = me ^ d
        for i in range((part_ref.shape[0] - first) // sub):
            at = pl.multiple_of((i * nseq + c) * sub, sub)
            dw_ref[pl.ds(at, sub)] = part_ref[first + i * sub : first + (i + 1) * sub]


def swap(x, axis, by):
    n = lax.axis_size(axis)
    return jax.tree.map(lambda v: lax.ppermute(v, axis, [(i, i ^ by) for i in range(n)]), x)


def trade(parts, axis):
    return [parts[0]] + [swap(parts[d], axis, d) for d in range(1, len(parts))]


def tie(*values):
    return lax.optimization_barrier(values)


def on_device(block_in, cotangent, ln_gain, ln_bias, lambda_log, lambda_imag, dss_weight, log_step, skip_gain,
              lin_weight, lin_bias, doc_lengths):
    ndp, nseq = lax.axis_size("dp"), lax.axis_size("seq")
    count, block, width = block_in.shape
    length = block * nseq
    own = ln_gain.shape[0]
    sub = own // nseq
    wide = width // nseq
    per = lambda_log.shape[0]
    nstate = per * ndp
    n_w = 2 * nstate
    cols = lin_weight.shape[1]
    tokens = count * block
    height = n_w * sub // LANES
    rows = height + 8
    steps = [1 << k for k in reversed(range(ndp.bit_length() - 1))]
    masks = [0]
    for step in steps:
        masks += [mask ^ step for mask in masks]

    def row(v):
        return v.reshape(1, -1)

    packed = call(partial(pack_kernel, sub), shape((1, rows, LANES)), [VM] * 8, name="pack", mib=60, us=2)(
        dss_weight.reshape(n_w, own), row(log_step), row(skip_gain), row(ln_gain), row(ln_bias),
        row(lambda_log), row(lambda_imag), row(lin_bias)
    )

    piece, piece32 = shape((count, block, wide), bf16), shape((count, block, wide))
    shared, shared_parts = packed, [packed]
    w_slots = [lin_weight[None]]
    f_table, ft_table = dft_tables(block)
    w_more = hats = None
    for number, step in enumerate(steps):
        more = swap(shared, "dp", step)
        if number == 0:
            x_late, _ = tie(block_in, packed)
            hats = call(
                partial(ln_kernel, own, sub), [piece32] * nseq, [AN],
                scratch=[pltpu.VMEM((count, block, width), bf16), DMA((count,))], name="layer_norm", us=2,
            )(x_late)
            more, *hats = tie(more, *hats)
        elif number == 1:
            hats = trade(hats, "seq")
            more, hats[1] = tie(more, hats[1])
        elif number == 2:
            w_more = swap(w_slots[0], "dp", steps[0])
        shared_parts.append(more)
        if number < len(steps) - 1:
            shared = jnp.concatenate([shared, more], axis=0)

    spec = (nseq, 2 * block, wide)
    kh, vec, w_all, terms, pows = call(
        partial(lag_kernel, sub, length, masks, len(shared_parts)),
        [shape(spec), shape((8, wide)), shape((n_w, wide)), shape((TERMS, nstate, wide)),
         shape((2 * len(POWERS), nstate, wide))],
        [VM] * (len(shared_parts) + 1),
        scratch=[pltpu.VMEM((length, wide), f32), pltpu.VMEM((2, nstate, wide), f32),
                 pltpu.VMEM((3 * block, nseq * wide), bf16), pltpu.VMEM((2 * block, nseq * wide), f32)],
        name="lag_kernel", us=0, keep=[ft_table, block_in, cotangent],
    )(*shared_parts, f_table)

    kh, w_more = tie(kh, w_more)
    w_late = jnp.concatenate([w_slots[0], w_more], axis=0)
    ahead = steps[1:]
    if len(ahead) == 2:
        w_slots = [w_late, swap(w_late, "dp", ahead[0]), swap(w_late, "dp", ahead[1])]
    else:
        w_slots = [w_late]
        for step in ahead:
            w_slots = [jnp.concatenate(w_slots + [swap(slot, "dp", step) for slot in w_slots], axis=0)]

    blocks4 = (count, nseq, block, wide)
    items = nseq + doc_lengths.shape[1] - 1
    lens = pltpu.SMEM(doc_lengths.shape, i32)
    cuts = pltpu.SMEM((count, items + 1), i32)
    across = items * count * wide
    *convs, spectra_u, x_blocks = call(
        conv_kernel, [piece] * nseq + [shape((2 * block, across)), shape(blocks4)],
        [VM] * nseq + [AN] + [VM] * 4,
        scratch=[lens, cuts, pltpu.VMEM((3 * block, across), bf16), pltpu.VMEM((2 * block, across), f32),
                 pltpu.VMEM((6 * block, across), bf16), pltpu.VMEM(blocks4, f32), DMA],
        name="doc_conv", mib=20, us=7, keep=[w_all, terms, pows, block_in, cotangent],
    )(*hats, doc_lengths, vec, kh, f_table, ft_table)
    keep = [w_all, terms, pows, vec, kh, f_table, ft_table, spectra_u, x_blocks]
    if len(ahead) == 2:
        *convs, w_slots[1], w_slots[2] = tie(*convs, w_slots[1], w_slots[2])
    convs = trade(convs, "seq")
    if len(ahead) == 2:
        w_slots.append(swap(w_slots[1], "dp", ahead[1]))
    pows_late, _ = tie(pows, convs[1])
    far = call(power_kernel, shape((2 * DOCMAX // PAIR, nstate, wide)), [VM], name="state_powers", mib=16, us=1, keep=keep)(pows_late)
    convs[2], _ = tie(convs[2], far)
    keep.append(far)
    if cols % LANES == 0 and sub % 16 == 0:
        shared = jnp.concatenate([shared, shared_parts[-1]], axis=0)
        shared, convs[1] = tie(shared, convs[1])
        w_lin, bias_full = call(
            partial(rows_kernel, sub, nseq, masks), [shape((width, 2 * width), bf16), shape((1, 2 * width))],
            [VM] * (1 + len(w_slots)), name="linear_rows", us=1, keep=keep,
        )(shared, *w_slots)
    else:
        shared = jnp.concatenate([shared, shared_parts[-1]], axis=0)
        place = jnp.asarray([masks.index(i) for i in range(ndp)])[lax.axis_index("dp") ^ jnp.arange(ndp)]
        w_lin = jnp.take(jnp.concatenate(w_slots, axis=0), place, axis=0)
        w_lin = w_lin.reshape(ndp, ndp, nseq, sub, cols).transpose(2, 1, 3, 0, 4).reshape(width, 2 * width)
        bias_full = jnp.take(shared[:, height + 2, :cols], place, axis=0).reshape(1, 2 * width)

    group = shape((2, wide, 2 * width), bf16)
    block_out, d_lin_bias, *d_convs, stay, send = call(
        dense_kernel,
        [shape((count, block, width), bf16), shape((1, 2 * width))] + [piece] * nseq + [group] * 2,
        [VM] * nseq + [AN, AN, VM, VM],
        scratch=[pltpu.VMEM((count, block, width), bf16), pltpu.VMEM((count, block, width), bf16),
                 pltpu.VMEM((tokens, width), bf16), pltpu.VMEM((tokens, 2 * width), bf16),
                 pltpu.VMEM((block, width), f32), pltpu.VMEM((block, 2 * width), f32), pltpu.VMEM((block, width), f32), DMA((2,))],
        name="gated_linear", mib=16, us=5, keep=keep,
    )(*convs, block_in, cotangent, w_lin, bias_full)
    d_convs = trade(d_convs, "seq")

    staged = cols % LANES == 0
    if staged:
        stay, send = call(
            halve_kernel, [shape((1, wide, 2 * width), bf16)] * 2, [VM, VM], name="weight_half", keep=keep
        )(stay, swap(send, "seq", 1))
        d_convs[2], *_ = tie(d_convs[2], send)
        dw_other = swap(send, "seq", 2)
    else:
        full = jnp.stack([stay[0], send[0], stay[1], send[1]])
        full = full.reshape(nseq, wide, ndp, cols).transpose(2, 0, 1, 3)
        dw_own = jnp.sum(lax.all_to_all(full, "dp", 0, 0, tiled=True).astype(f32), axis=0)
        dw_own = sum(trade([dw_own[d] for d in range(nseq)], "seq"))

    out = call(
        back_kernel, [piece] * nseq + [shape(spec), shape((3, wide))],
        [VM] * (nseq + 1) + [AN] + [VM] * 5,
        scratch=[lens, cuts, pltpu.VMEM(blocks4, bf16), pltpu.VMEM((2 * block, across), bf16),
                 pltpu.VMEM((2 * block, across), f32), pltpu.VMEM((2 * block, across), f32),
                 pltpu.VMEM((6 * block, across), bf16), pltpu.VMEM(blocks4, f32), DMA],
        name="doc_conv_grad", mib=24, us=8, keep=[w_all, terms, pows, far],
    )(*d_convs, x_blocks, doc_lengths, spectra_u, vec, kh, f_table, ft_table)
    g_own, dkh, d_norm = out[:nseq], out[nseq], out[nseq + 1]
    if staged:
        stay, send = call(
            deal_kernel, [shape((ndp // 2, wide, cols))] * 2, [VM, VM], name="weight_deal", us=1, keep=[w_all, terms, pows, far]
        )(stay, dw_other)
        dkh, *_ = tie(dkh, send)
        dw_other = swap(send, "dp", 1)

    small = call(
        partial(state_grad_kernel, sub, length), shape((ndp, rows, LANES)), [VM] * 8,
        scratch=[pltpu.VMEM((length, wide), f32), pltpu.VMEM((4, nstate, wide), f32), pltpu.VMEM((n_w, wide), f32),
                 pltpu.VMEM((6 * block, nseq * wide), bf16)],
        name="state_grad", mib=10, us=10,
    )(w_all, terms, pows, far, dkh, d_norm, d_lin_bias, ft_table)
    small, *g_own = tie(small, *g_own)
    if staged:
        small, dw_other = tie(small, dw_other)
    small = lax.all_to_all(small, "dp", 0, 0, tiled=True)
    gs = trade(g_own, "seq")
    if staged:
        step = 2
        while step < ndp:
            stay, send = call(
                halve_kernel, [shape((ndp // 2 // step, wide, cols))] * 2, [VM, VM], name="weight_half"
            )(stay, dw_other)
            dw_other = swap(send, "dp", step)
            step *= 2
    grad_in = call(
        partial(ln_back_kernel, own, sub), shape((count, block, width), bf16), [VM] * (nseq + 2),
        name="layer_norm_grad", mib=12,
    )(*gs, block_in, cotangent)
    if staged:
        merged = call(merge_kernel, shape((rows + wide, cols)), [VM] * 3, name="last_sums", us=0.5)(small, stay, dw_other)
        merged = trade([merged] * nseq, "seq")
        smalls, dws = merged, []
    else:
        small = call(sum_kernel, shape((rows, LANES)), [VM], name="small_sum", us=0.5)(small)
        smalls, dws = trade([small] * nseq, "seq"), trade([dw_own] * nseq, "seq")
    d_w, d_step, d_skip, d_gain, d_bias, d_lam, d_imag, d_lb, dw = call(
        partial(last_kernel, sub, rows),
        [shape((n_w, own))] + [shape((1, own))] * 4 + [shape((1, per))] * 2 + [shape((1, cols)), shape((width, cols))],
        [VM] * (len(smalls) + len(dws)), name="last", us=1,
    )(*smalls, *dws)
    return (
        block_out, grad_in, d_gain.reshape(own), d_bias.reshape(own), d_lam.reshape(per), d_imag.reshape(per),
        d_w.reshape(2, nstate, own), d_step.reshape(own), d_skip.reshape(own), dw, d_lb.reshape(cols),
    )


def solution(mesh):
    placed = (
        P("dp", "seq", None), P("dp", "seq", None), P("dp"), P("dp"), P("dp"), P("dp"),
        P(None, None, "dp"), P("dp"), P("dp"), P(None, "dp"), P("dp"), P("dp", None),
    )
    return jax.shard_map(
        on_device,
        mesh=mesh,
        in_specs=placed,
        out_specs=(
            P("dp", "seq", None), P("dp", "seq", None), P("dp"), P("dp"), P("dp"), P("dp"),
            P(None, None, "dp"), P("dp"), P("dp"), P(None, "dp"), P("dp"),
        ),
        check_vma=False,
    )
```

```python
from functools import partial

import jax
import jax.numpy as jnp
import numpy as np
from jax import lax
from jax.experimental import pallas as pl
from jax.experimental.pallas import tpu as pltpu
from jax.sharding import PartitionSpec as P

f32, bf16, i32 = jnp.float32, jnp.bfloat16, jnp.int32
ln_eps = 1e-05
DOCMAX = 800
FINE = 8
COARSE = 10
LANES = 128
NN = (((1,), (0,)), ((), ()))
NT = (((1,), (1,)), ((), ()))
TN = (((0,), (0,)), ((), ()))
VM = pl.BlockSpec(memory_space=pltpu.VMEM)
AN = pl.BlockSpec(memory_space=pl.ANY)
DMA = pltpu.SemaphoreType.DMA


def dot(a, b, dims=NN):
    return lax.dot_general(a, b, dims, preferred_element_type=f32)


def exact_dot(a, b, dims=NN):
    return lax.dot_general(a, b, dims, precision=lax.Precision.HIGHEST, preferred_element_type=f32)


def shape(dims, dtype=f32):
    return jax.ShapeDtypeStruct(dims, dtype)


def call(body, out, specs, scratch=(), name=None, mib=8, outs=None, us=0, keep=()):
    inputs, kept = len(specs), len(keep)

    def whole(*refs):
        body(*refs[:inputs], *refs[inputs + kept :])

    kernel = pl.pallas_call(
        whole,
        out_shape=out,
        in_specs=list(specs) + [AN] * kept,
        out_specs=outs if outs is not None else jax.tree.map(lambda _: VM, out),
        scratch_shapes=list(scratch),
        cost_estimate=pl.CostEstimate(flops=int(us * 1.15e9), bytes_accessed=1000, transcendentals=0),
        compiler_params=pltpu.CompilerParams(vmem_limit_bytes=mib * 2**20),
        name=name,
    )
    return lambda *args: kernel(*args, *keep)


def iota(dims, axis):
    return lax.broadcasted_iota(i32, dims, axis)


def cmul(ar, ai, br, bi):
    return ar * br - ai * bi, ar * bi + ai * br


def small_expm1(a):
    poly = jnp.full_like(a, 1.0)
    for k in range(9, 1, -1):
        poly = 1.0 + poly * a * (1.0 / k)
    return jnp.where(jnp.abs(a) < 0.5, a * poly, jnp.exp(a) - 1.0)


def state_terms(rate_log, freq, step_log, length):
    step = jnp.exp(step_log)
    a = -jnp.exp(rate_log) * step
    b = freq * step
    half = jnp.sin(0.5 * b)
    cos_b, sin_b, mag = jnp.cos(b), jnp.sin(b), jnp.exp(a)
    one_re = 2.0 * half * half - small_expm1(a) * cos_b
    one_im = -mag * sin_b
    far = jnp.exp(length * a)
    far_re, far_im = far * jnp.cos(length * b), far * jnp.sin(length * b)
    den_re, den_im = 1.0 - far_re, -far_im
    inv = 1.0 / (den_re * den_re + den_im * den_im)
    g_re = (one_re * den_re + one_im * den_im) * inv
    g_im = (one_im * den_re - one_re * den_im) * inv
    return a, b, mag * cos_b, mag * sin_b, one_re, one_im, far_re, far_im, den_re, den_im, inv, g_re, g_im


TERMS = 13


POWERS = (1, 2, 4) + tuple(8 * v for v in range(1, COARSE + 1))


def power_table(zr, zi):
    table = {1: (zr, zi)}
    for p in POWERS[1:]:
        at = p // 16 * 8 if p > 8 else p // 2
        table[p] = cmul(*table[at], *table[p - at])
    return [table[p] for p in POWERS]


def wide_row(ref, p, half, n):
    return jnp.broadcast_to(ref[2 * POWERS.index(p) + half, pl.ds(n, 1), :], (8, LANES))


def rows8(ref, n):
    at = iota((8, LANES), 0)
    total = None
    for p in (1, 2, 4):
        here = at & p > 0
        one = jnp.where(here, wide_row(ref, p, 0, n), 1.0), jnp.where(here, wide_row(ref, p, 1, n), 0.0)
        total = one if total is None else cmul(*total, *one)
    return total


def powers(ref, n):
    return [None] + [(wide_row(ref, 8 * v, 0, n), wide_row(ref, 8 * v, 1, n)) for v in range(1, COARSE + 1)]


def halves(x):
    hi = x.astype(bf16)
    return hi, (x - hi.astype(f32)).astype(bf16)


def stack3(ref, cols, x):
    height = x.shape[0]
    hi, lo = halves(x)
    ref[0:height, cols] = hi
    ref[height : 2 * height, cols] = lo
    ref[2 * height : 3 * height, cols] = hi


def signs(block, lanes):
    return jnp.where(iota((block, lanes), 0) & 1 > 0, -1.0, 1.0)


def dft_tables(block):
    k, j = np.arange(block)[:, None], np.arange(block)[None, :]
    theta = np.pi * (((2 * k + 1) * j) % (4 * block)) / (2 * block)
    full = np.concatenate([np.cos(theta), -np.sin(theta)], axis=0)
    high = full.astype(jnp.bfloat16)
    low = (full - high.astype(np.float64)).astype(jnp.bfloat16)
    return (jnp.asarray(np.concatenate([high, high, low], axis=1)),
            jnp.asarray(np.concatenate([high.T, high.T, low.T], axis=1)))


def moved(x, by):
    return x if by % LANES == 0 else pltpu.roll(x, by % LANES, 1)


def pack_kernel(sub, w_ref, step_ref, skip_ref, gain_ref, bias_ref, lam_ref, imag_ref, lb_ref, o_ref):
    own, per, cols = step_ref.shape[1], lam_ref.shape[1], lb_ref.shape[1]
    groups = LANES // sub
    height = w_ref.shape[0] // groups
    pick = (iota((own, LANES), 0) == lax.axis_index("seq") * sub + iota((own, LANES), 1) % sub).astype(f32)
    w = exact_dot(w_ref[...], pick)
    vec = exact_dot(jnp.concatenate([step_ref[...], skip_ref[...], gain_ref[...], bias_ref[...]] * 2, axis=0), pick)
    group = iota((1, LANES), 1) // sub
    main = jnp.zeros((height, LANES), f32)
    row = jnp.zeros((1, LANES), f32)
    for u in range(groups):
        main = jnp.where(group == u, w[u * height : (u + 1) * height], main)
        if u < 4:
            row = jnp.where(group == u, vec[u : u + 1], row)
    spot, lane = iota((per, LANES), 0), iota((per, LANES), 1)
    rates = exact_dot(jnp.broadcast_to(lam_ref[...], (8, per)), (lane == spot).astype(f32)) + exact_dot(
        jnp.broadcast_to(imag_ref[...], (8, per)), (lane == spot + per).astype(f32)
    )
    o_ref[...] = jnp.zeros(o_ref.shape, f32)
    o_ref[0, 0:height] = main
    o_ref[0, height : height + 1] = row
    o_ref[0, height + 1 : height + 2] = rates[0:1]
    o_ref[0, height + 2 : height + 3, 0:cols] = lb_ref[...]


def lag_kernel(sub, length, masks, n_parts, *refs):
    pieces, refs = refs[:n_parts], refs[n_parts:]
    f_ref, kh_ref, vec_ref, w_ref, term_ref, pow_ref, k_scr, z_scr, rhs_scr, kf_scr = refs
    slots = [piece.at[t] for piece in pieces for t in range(piece.shape[0])]
    ndp = len(slots)
    me = lax.axis_index("dp")
    n_w, lanes = w_ref.shape
    nstate = n_w // 2
    per = nstate // ndp
    groups = LANES // sub
    height = n_w // groups
    block = f_ref.shape[0] // 2
    group = iota((1, LANES), 1) // sub
    for u in range(groups):
        acc = jnp.zeros(slots[0].shape, f32)
        for t in range(ndp):
            i = me ^ masks[t]
            acc = jnp.where(group == i, pltpu.roll(slots[t][...], (i - u) * sub + LANES * ndp, 1), acc)
        w_ref[u * height : (u + 1) * height] = acc[0:height]
        if u < 4:
            vec_ref[u : u + 1] = acc[height : height + 1]
    vec_ref[4:8] = jnp.zeros((4, lanes), f32)
    rows = jnp.concatenate([slot[height + 1 : height + 2] for slot in slots], axis=0)
    source = jnp.zeros((nstate, ndp), i32)
    for t in range(ndp):
        source = jnp.where(iota((nstate, ndp), 1) == t, me ^ masks[t], source)
    spread = exact_dot((iota((nstate, ndp), 0) // per == source).astype(f32), rows)
    lane, state = iota((nstate, lanes), 1), iota((nstate, lanes), 0)
    lam = jnp.sum(jnp.where(lane == state % per, spread, 0.0), axis=1, keepdims=True)
    imag = jnp.sum(jnp.where(lane == state % per + per, spread, 0.0), axis=1, keepdims=True)
    terms = state_terms(lam, imag, vec_ref[0:1], float(length))
    for slot, value in enumerate(terms):
        term_ref[slot] = value
    z_scr[0], z_scr[1] = cmul(w_ref[0:nstate], w_ref[nstate:], terms[11], terms[12])
    for slot, pair in enumerate(power_table(terms[2], terms[3])):
        pow_ref[2 * slot], pow_ref[2 * slot + 1] = pair
    k_scr[...] = jnp.zeros_like(k_scr)

    def pair(m, _):
        ready = []
        for n in (2 * m, 2 * m + 1):
            fr, fi = rows8(pow_ref, n)
            cr = jnp.broadcast_to(z_scr[0, pl.ds(n, 1), :], (8, lanes))
            ci = jnp.broadcast_to(z_scr[1, pl.ds(n, 1), :], (8, lanes))
            ready.append([cmul(fr, fi, cr, ci), powers(pow_ref, n)])
        for u in range(DOCMAX // FINE // COARSE):
            for v in range(COARSE):
                at = (u * COARSE + v) * FINE
                total = k_scr[at : at + FINE]
                for (xr, xi), pows in ready:
                    total = total + (xr * pows[v][0] - xi * pows[v][1] if v else xr)
                k_scr[at : at + FINE] = total
            for one in ready:
                one[0] = cmul(*one[0], *one[1][COARSE])
        return 0

    lax.fori_loop(0, nstate // 2, pair, 0)
    k_scr[0:1] += vec_ref[1:2]
    parts = length // block
    for p in range(parts):
        stack3(rhs_scr, slice(p * lanes, (p + 1) * lanes), k_scr[p * block : (p + 1) * block])
    kf_scr[...] = dot(f_ref[...], rhs_scr[...])
    sign = signs(block, lanes)
    for p in range(parts):
        here, past = slice(p * lanes, (p + 1) * lanes), slice((p - 1) * lanes, p * lanes)
        re, im = kf_scr[:block, here], kf_scr[block:, here]
        if p:
            re = re - sign * kf_scr[block:, past]
            im = im + sign * kf_scr[:block, past]
        kh_ref[p, :block] = re * (1.0 / block)
        kh_ref[p, block:] = im * (1.0 / block)


def members(own, sub, c, width, wide):
    lane = iota((1, wide), 1)
    return (iota((width, wide), 0) == (lane // sub) * own + c * sub + lane % sub).astype(f32).astype(bf16)


STAT_ROWS = 16


def terms3(x):
    hi, rest = x.astype(bf16), x
    out = [hi]
    for _ in range(2):
        rest = rest - out[-1].astype(f32)
        out.append(rest.astype(bf16))
    return out


def spread_kernel(own, sub, x_any, *refs):
    *o_refs, x_ref, sems = refs
    count, block, width = x_ref.shape
    wide = o_refs[0].shape[-1]
    copies = [pltpu.make_async_copy(x_any.at[s], x_ref.at[s], sems.at[s]) for s in range(count)]
    for copy in copies:
        copy.start()
    places = [members(own, sub, lax.axis_index("seq") ^ d, width, wide) for d in range(len(o_refs))]
    eye = (iota((block, block), 0) == iota((block, block), 1)).astype(f32).astype(bf16)
    lane = iota((block, LANES), 1)
    for s in range(count):
        copies[s].wait()
        for o_ref, cols in zip(o_refs, places):
            o_ref[s, 0:block] = dot(x_ref[s], cols).astype(bf16)
        x = x_ref[s].astype(f32)
        mean = jnp.mean(x, axis=-1, keepdims=True)
        centre = x - mean
        inv = lax.rsqrt(jnp.mean(centre * centre, axis=-1, keepdims=True) + ln_eps)
        table = jnp.zeros((block, LANES), f32)
        for k, term in enumerate(terms3(mean) + terms3(inv)):
            table = jnp.where(lane == k, term.astype(f32), table)
        turned = dot(table.astype(bf16), eye, TN)
        both = jnp.concatenate([turned[0:8, 0:LANES], turned[0:8, LANES:]], axis=0).astype(bf16)
        for o_ref in o_refs:
            o_ref[s, block:] = both


def normal_inputs(piece_ref, s, block):
    stats = piece_ref[s, block:]
    spot, lane = iota((STAT_ROWS, 4 * LANES), 0), iota((STAT_ROWS, 4 * LANES), 1) // LANES
    first = lane // 2 * 8 + lane % 2 * 3
    pick = ((spot >= first) & (spot < first + 3)).astype(f32).astype(bf16)
    cols = dot(stats, pick, TN)
    parts = []
    for half in (0, 1):
        rows = piece_ref[s, half * LANES : (half + 1) * LANES].astype(f32)
        at = 2 * half * LANES
        parts.append((rows - cols[:, at : at + LANES]) * cols[:, at + LANES : at + 2 * LANES])
    return jnp.concatenate(parts, axis=0)


def ln_back_kernel(own, sub, g0, g1, g2, g3, x_ref, c_ref, o_ref):
    count, block, width = x_ref.shape
    wide = g0.shape[-1]
    tokens = count * block
    g = jnp.zeros((tokens, width), f32)
    for d, g_ref in enumerate((g0, g1, g2, g3)):
        cols = members(own, sub, lax.axis_index("seq") ^ d, width, wide)
        g = g + dot(g_ref[...].reshape(tokens, wide), cols, NT)
    x = x_ref[...].astype(f32).reshape(tokens, width)
    centre = x - jnp.mean(x, axis=-1, keepdims=True)
    inv = lax.rsqrt(jnp.mean(centre * centre, axis=-1, keepdims=True) + ln_eps)
    hat = centre * inv
    mean_g = jnp.mean(g, axis=-1, keepdims=True)
    mean_gx = jnp.mean(g * hat, axis=-1, keepdims=True)
    cot = c_ref[...].astype(f32).reshape(tokens, width)
    o_ref[...] = (cot + inv * (g - mean_g - hat * mean_gx)).astype(bf16).reshape(o_ref.shape)


def segments(len_ref, cut_ref, block, parts):
    count, docs = len_ref.shape
    last = parts + docs - 1
    for s in range(count):
        ends = []
        for d in range(docs - 1):
            ends.append(len_ref[s, d] + (ends[-1] if ends else 0))
        cut_ref[s, 0] = 0
        cut_ref[s, last] = parts * block
        for d, end in enumerate(ends):
            rank = 1 + d
            for k in range(1, parts):
                rank = rank + jnp.where(end > k * block, 1, 0)
            cut_ref[s, rank] = end
        for k in range(1, parts):
            rank = k
            for end in ends:
                rank = rank + jnp.where(end <= k * block, 1, 0)
            cut_ref[s, rank] = k * block


def document(len_ref, s, at):
    start, end, total = 0, 0, 0
    for d in range(len_ref.shape[1]):
        total = total + len_ref[s, d]
        start = jnp.where(total <= at, total, start)
    total = 0
    end = 1 << 30
    for d in range(len_ref.shape[1]):
        total = total + len_ref[s, d]
        end = jnp.minimum(end, jnp.where(total > at, total, 1 << 30))
    return start, end


def within(cut_ref, s, j, block, lanes):
    start, end = cut_ref[s, j], cut_ref[s, j + 1]
    b = start // block
    rows = b * block + iota((block, lanes), 0)
    return b, (rows >= start) & (rows < end)


def column(j, s, count, lanes):
    return pl.ds(pl.multiple_of((j * count + s) * lanes, lanes), lanes)


CHUNK = 64


def lengths_in(len_ref, len_scr, sem):
    copy = pltpu.make_async_copy(len_ref, len_scr, sem)
    copy.start()
    copy.wait()


def split_rows(y_scr, rows, cols, value, block, half):
    hi, lo = halves(value)
    for third, part in enumerate((hi, lo, hi)):
        at = (2 * third + half) * block
        y_scr[at + rows.start : at + rows.stop, cols] = part


def row_chunks(block):
    for r in range(0, block, CHUNK):
        yield slice(r, r + CHUNK), slice(block + r, block + r + CHUNK)


def conv_kernel(x0, x1, x2, x3, len_ref, vec_ref, kh_ref, f_ref, ft_ref,
                o0, o1, o2, o3, s_scr, x_scr, len_scr, cut_ref, rhs_scr, acc_scr, y_scr, out_scr, sem):
    count, parts, block, lanes = x_scr.shape
    me = lax.axis_index("seq")
    lengths_in(len_ref, len_scr, sem)
    for d, x_ref in enumerate((x0, x1, x2, x3)):
        for s in range(count):
            x_scr[s, me ^ d] = normal_inputs(x_ref, s, block)
    segments(len_scr, cut_ref, block, parts)
    gain, bias = vec_ref[2:3], vec_ref[3:4]
    items = cut_ref.shape[1] - 1
    for j in range(items):
        for s in range(count):
            b, keep = within(cut_ref, s, j, block, lanes)
            cols = slice((j * count + s) * lanes, (j * count + s + 1) * lanes)
            stack3(rhs_scr, cols, jnp.where(keep, x_scr[s, b] * gain + bias, 0.0))
        tile = slice(j * count * lanes, (j + 1) * count * lanes)
        s_scr[:, tile] = dot(f_ref[...], rhs_scr[:, tile])

    def own(j, _):
        for s in range(count):
            cols = column(j, s, count, lanes)
            for re, im in row_chunks(block):
                acc_scr[re, cols], acc_scr[im, cols] = cmul(
                    kh_ref[0, re], kh_ref[0, im], s_scr[re, cols], s_scr[im, cols]
                )
            start, _ = document(len_scr, s, cut_ref[s, j])
            b = cut_ref[s, j] // block
            first = j
            for i in range(items):
                first = first - jnp.where((i < j) & (cut_ref[s, i] >= start), 1, 0)

            def add(i, _):
                p = b - cut_ref[s, i] // block
                there = column(i, s, count, lanes)
                for re, im in row_chunks(block):
                    more = cmul(kh_ref[p, re], kh_ref[p, im], s_scr[re, there], s_scr[im, there])
                    acc_scr[re, cols] += more[0]
                    acc_scr[im, cols] += more[1]
                return 0

            lax.fori_loop(first, j, add, 0)
            for re, im in row_chunks(block):
                split_rows(y_scr, re, cols, acc_scr[re, cols], block, 0)
                split_rows(y_scr, re, cols, acc_scr[im, cols], block, 1)
        return 0

    lax.fori_loop(0, items, own, 0)
    acc_scr[0:block] = dot(ft_ref[...], y_scr[...])
    for j in range(items):
        for s in range(count):
            b, keep = within(cut_ref, s, j, block, lanes)
            cols = slice((j * count + s) * lanes, (j * count + s + 1) * lanes)
            out_scr[s, b] = jnp.where(keep, acc_scr[0:block, cols], out_scr[s, b])
    for d, o_ref in enumerate((o0, o1, o2, o3)):
        for s in range(count):
            o_ref[s] = out_scr[s, me ^ d].astype(bf16)


def back_kernel(c0, c1, c2, c3, x_scr, len_ref, s_scr, vec_ref, kh_ref, f_ref, ft_ref,
                g0, g1, g2, g3, dkh_ref, dvec_ref,
                len_scr, cut_ref, v_scr, rhs_scr, sv_scr, acc_scr, y_scr, du_scr, sem):
    count, block, lanes = c0.shape
    parts = kh_ref.shape[0]
    me = lax.axis_index("seq")
    lengths_in(len_ref, len_scr, sem)
    for d, c_ref in enumerate((c0, c1, c2, c3)):
        for s in range(count):
            v_scr[s, me ^ d] = c_ref[s]
    dkh_ref[...] = jnp.zeros_like(dkh_ref)
    segments(len_scr, cut_ref, block, parts)
    items = cut_ref.shape[1] - 1
    for j in range(items):
        for s in range(count):
            b, keep = within(cut_ref, s, j, block, lanes)
            v = jnp.where(keep, v_scr[s, b].astype(f32), 0.0).astype(bf16)
            cols = slice((j * count + s) * lanes, (j * count + s + 1) * lanes)
            rhs_scr[0:block, cols] = v
            rhs_scr[block:, cols] = v
        tile = slice(j * count * lanes, (j + 1) * count * lanes)
        sv_scr[:, tile] = dot(f_ref[:, block:], rhs_scr[:, tile])

    def own(j, _):
        for s in range(count):
            cols = column(j, s, count, lanes)
            for re, im in row_chunks(block):
                vr, vi, ur, ui = sv_scr[re, cols], sv_scr[im, cols], s_scr[re, cols], s_scr[im, cols]
                kr, ki = kh_ref[0, re], kh_ref[0, im]
                acc_scr[re, cols] = kr * vr + ki * vi
                acc_scr[im, cols] = kr * vi - ki * vr
                dkh_ref[0, re] += vr * ur + vi * ui
                dkh_ref[0, im] += vi * ur - vr * ui
            _, end = document(len_scr, s, cut_ref[s, j])
            b = cut_ref[s, j] // block
            last = j
            for i in range(items):
                last = last + jnp.where((i > j) & (cut_ref[s, i] < end), 1, 0)

            def add(i, _):
                p = cut_ref[s, i] // block - b
                there = column(i, s, count, lanes)
                for re, im in row_chunks(block):
                    vr, vi, ur, ui = sv_scr[re, there], sv_scr[im, there], s_scr[re, cols], s_scr[im, cols]
                    kr, ki = kh_ref[p, re], kh_ref[p, im]
                    acc_scr[re, cols] += kr * vr + ki * vi
                    acc_scr[im, cols] += kr * vi - ki * vr
                    dkh_ref[p, re] += vr * ur + vi * ui
                    dkh_ref[p, im] += vi * ur - vr * ui
                return 0

            lax.fori_loop(j + 1, last + 1, add, 0)
            for re, im in row_chunks(block):
                split_rows(y_scr, re, cols, acc_scr[re, cols], block, 0)
                split_rows(y_scr, re, cols, acc_scr[im, cols], block, 1)
        return 0

    lax.fori_loop(0, items, own, 0)
    acc_scr[0:block] = dot(ft_ref[...], y_scr[...])
    for j in range(items):
        for s in range(count):
            b, keep = within(cut_ref, s, j, block, lanes)
            cols = slice((j * count + s) * lanes, (j * count + s + 1) * lanes)
            du_scr[s, b] = jnp.where(keep, acc_scr[0:block, cols], du_scr[s, b])
    gain = vec_ref[2:3]
    d_gain = jnp.zeros((8, lanes), f32)
    d_bias = jnp.zeros((8, lanes), f32)
    for d, g_ref in enumerate((g0, g1, g2, g3)):
        for s in range(count):
            for r in range(0, block, CHUNK):
                du = du_scr[s, me ^ d, r : r + CHUNK]
                d_bias += jnp.sum(du.reshape(CHUNK // 8, 8, lanes), axis=0)
                d_gain += jnp.sum((du * x_scr[s, me ^ d, r : r + CHUNK]).reshape(CHUNK // 8, 8, lanes), axis=0)
                g_ref[s, r : r + CHUNK] = (du * gain).astype(bf16)
    dvec_ref[0:1] = jnp.sum(d_gain, axis=0, keepdims=True)
    dvec_ref[1:2] = jnp.sum(d_bias, axis=0, keepdims=True)
    dvec_ref[2:3] = vec_ref[0:1]


def normal_cdf(v, bell):
    t = 1.0 / (1.0 + np.float32(0.3275911 / np.sqrt(2.0)) * jnp.abs(v))
    tail = t * (0.127414796 + t * (-0.142248368 + t * (0.7107068705 + t * (-0.7265760135 + t * 0.5307027145)))) * bell
    return jnp.where(v < 0.0, tail, 1.0 - tail)


def dense_kernel(q0, q1, q2, q3, x_any, c_any, w_ref, lb_ref,
                 out_ref, dlb_ref, d0, d1, d2, d3, stay_ref, send_ref,
                 x_ref, c_ref, act_ref, dpre_ref, slope_scr, pre_scr, dact_scr, sems):
    count, block, wide = q0.shape
    width = act_ref.shape[1]
    me = lax.axis_index("seq")
    copies = [pltpu.make_async_copy(x_any, x_ref, sems.at[0]), pltpu.make_async_copy(c_any, c_ref, sems.at[1])]
    for copy in copies:
        copy.start()

    def cols_of(d):
        return pl.ds(pl.multiple_of((me ^ d) * wide, wide), wide)

    def sequence(s, lb_sum):
        def slope(r, _):
            rows = pl.ds(pl.multiple_of(r * CHUNK, CHUNK), CHUNK)
            flat = pl.ds(pl.multiple_of(s * block + r * CHUNK, CHUNK), CHUNK)
            for d, q_ref in enumerate((q0, q1, q2, q3)):
                v = q_ref[s, rows].astype(f32)
                bell = jnp.exp(-0.5 * v * v)
                cdf = normal_cdf(v, bell)
                act_ref[flat, cols_of(d)] = (v * cdf).astype(bf16)
                slope_scr[rows, cols_of(d)] = cdf + v * (bell * np.float32(1.0 / np.sqrt(2.0 * np.pi)))
            return 0

        lax.fori_loop(0, block // CHUNK, slope, 0)
        whole = pl.ds(pl.multiple_of(s * block, block), block)
        pre_scr[...] = dot(act_ref[whole, :], w_ref[...])

        @pl.when(s == 0)
        def _():
            for copy in copies:
                copy.wait()

        def gate(r, total):
            rows = pl.ds(pl.multiple_of(r * 32, 32), 32)
            flat = pl.ds(pl.multiple_of(s * block + r * 32, 32), 32)
            first = pre_scr[rows, 0:width] + lb_ref[:, 0:width]
            sig = 1.0 / (1.0 + jnp.exp(-(pre_scr[rows, width:] + lb_ref[:, width:])))
            out_ref[s, rows] = (x_ref[s, rows].astype(f32) + first * sig).astype(bf16)
            d_first = c_ref[s, rows].astype(f32) * sig
            d_second = d_first * first * (1.0 - sig)
            d_pre = jnp.concatenate([d_first, d_second], axis=1).astype(bf16)
            dpre_ref[flat, :] = d_pre
            return total + jnp.sum(d_pre.astype(f32).reshape(4, 8, 2 * width), axis=0)

        lb_sum = lax.fori_loop(0, block // 32, gate, lb_sum)
        dact_scr[...] = dot(dpre_ref[whole, :], w_ref[...], NT)
        for d, o_ref in enumerate((d0, d1, d2, d3)):
            o_ref[s] = (dact_scr[:, cols_of(d)] * slope_scr[:, cols_of(d)]).astype(bf16)
        return lb_sum

    lb_sum = lax.fori_loop(0, count, sequence, jnp.zeros((8, 2 * width), f32))
    dlb_ref[...] = jnp.sum(lb_sum, axis=0, keepdims=True)
    for d in range(4):
        (send_ref if d & 1 else stay_ref)[d // 2] = dot(act_ref[:, cols_of(d)], dpre_ref[...], TN).astype(bf16)


def rows_kernel(sub, nseq, masks, shared_ref, *refs):
    *w_refs, o_ref, lb_ref = refs
    cols = w_refs[0].shape[-1]
    span = o_ref.shape[0] // nseq
    me = lax.axis_index("dp")
    bias_row = shared_ref.shape[1] - 8 + 2
    for t, mask in enumerate(masks):
        at = pl.ds(pl.multiple_of((me ^ mask) * cols, cols), cols)
        lb_ref[:, at] = shared_ref[t, bias_row : bias_row + 1, 0:cols]
    t = 0
    for w_ref in w_refs:
        for slot in range(w_ref.shape[0]):
            at = pl.ds(pl.multiple_of((me ^ masks[t]) * cols, cols), cols)
            t += 1
            for c in range(nseq):
                for i in range(span // sub):
                    o_ref[c * span + i * sub : c * span + (i + 1) * sub, at] = w_ref[
                        slot, (i * nseq + c) * sub : (i * nseq + c + 1) * sub
                    ]


def halve_kernel(mine_ref, other_ref, stay_ref, send_ref):
    for k in range(mine_ref.shape[0]):
        total = mine_ref[k].astype(f32) + other_ref[k].astype(f32)
        (send_ref if k & 1 else stay_ref)[k // 2] = total.astype(stay_ref.dtype)


def deal_kernel(mine_ref, other_ref, stay_ref, send_ref):
    part = stay_ref.shape[2]
    me = lax.axis_index("dp")
    for d in range(2 * stay_ref.shape[0]):
        cols = pl.ds(pl.multiple_of((me ^ d) * part, part), part)
        (send_ref if d & 1 else stay_ref)[d // 2] = mine_ref[0, :, cols].astype(f32) + other_ref[0, :, cols].astype(f32)


def merge_kernel(x_ref, mine_ref, other_ref, o_ref):
    rows = x_ref.shape[1]
    total = x_ref[0]
    for i in range(1, x_ref.shape[0]):
        total = total + x_ref[i]
    o_ref[0:rows] = total
    o_ref[rows:] = mine_ref[0] + other_ref[0]


PAIR = 2 * FINE


def power_kernel(pow_ref, o_ref):
    def some(g, _):
        rows = pl.ds(pl.multiple_of(g * 8, 8), 8)
        at = [2 * POWERS.index(PAIR * v) for v in range(1, COARSE // 2 + 1)]
        small = [(pow_ref[i, rows], pow_ref[i + 1, rows]) for i in at]
        x = jnp.ones((8, LANES), f32), jnp.zeros((8, LANES), f32)
        for u in range(DOCMAX // PAIR // (COARSE // 2)):
            for v in range(COARSE // 2):
                m = u * (COARSE // 2) + v
                o_ref[2 * m, rows], o_ref[2 * m + 1, rows] = cmul(*x, *small[v - 1]) if v else x
            x = cmul(*x, *small[-1])
        return 0

    lax.fori_loop(0, pow_ref.shape[1] // 8, some, 0)


CHAINS = 2


def state_grad_kernel(sub, length, w_ref, term_ref, pow_ref, far_ref, dkh_ref, dvec_ref, dlb_ref, ft_ref, o_ref,
                      dk_scr, f_scr, dw_scr, y_scr):
    ndp = o_ref.shape[0]
    n_w, lanes = w_ref.shape
    nstate = n_w // 2
    per = nstate // ndp
    groups = LANES // sub
    height = n_w // groups
    parts, twice, _ = dkh_ref.shape
    block = twice // 2
    sign = signs(block, lanes)
    for p in range(parts):
        re, im = dkh_ref[p, :block], dkh_ref[p, block:]
        if p + 1 < parts:
            re = re + sign * dkh_ref[p + 1, block:]
            im = im - sign * dkh_ref[p + 1, :block]
        stack3(y_scr, slice(p * lanes, (p + 1) * lanes), jnp.concatenate([re, im], axis=0))
    all_lags = dot(ft_ref[...], y_scr[...]) * (1.0 / block)
    for p in range(parts):
        dk_scr[p * block : (p + 1) * block] = all_lags[:, p * lanes : (p + 1) * lanes]
    at8 = iota((8, lanes), 0).astype(f32)

    def one(n, _):
        fr, fi = rows8(pow_ref, n)
        zero = jnp.zeros((8, lanes), f32)
        span = DOCMAX // PAIR // CHAINS
        sums = []
        for c in range(CHAINS):
            acc = [[zero] * 4, [zero] * 4]
            for m in range(c * span + span - 1, c * span - 1, -1):
                if m:
                    p_re = jnp.broadcast_to(far_ref[2 * m, pl.ds(n, 1), :], (8, lanes))
                    p_im = jnp.broadcast_to(far_ref[2 * m + 1, pl.ds(n, 1), :], (8, lanes))
                for h, one_acc in enumerate(acc):
                    at = m * PAIR + h * FINE
                    dk = dk_scr[at : at + FINE]
                    one_acc[0] = one_acc[0] + (dk * p_re if m else dk)
                    if m:
                        one_acc[1] = one_acc[1] + dk * p_im
                    if m > c * span:
                        one_acc[2], one_acc[3] = one_acc[2] + one_acc[0], one_acc[3] + one_acc[1]
            for one_acc in acc:
                one_acc[2], one_acc[3] = (one_acc[2 + k] + (c * span) * one_acc[k] for k in (0, 1))
            sums.append(acc)
        low, high = (
            [sum((acc[h][k] for acc in sums[1:]), sums[0][h][k]) for k in range(4)] for h in (0, 1)
        )
        for h, part in enumerate((low, high)):
            for k in (0, 1):
                part[2 + k] = PAIR * part[2 + k] + (at8 + float(h * FINE)) * part[k]
        shift = wide_row(pow_ref, FINE, 0, n), wide_row(pow_ref, FINE, 1, n)
        values = []
        for k in (0, 2):
            up = cmul(high[k], high[k + 1], *shift)
            values.append(cmul(low[k] + up[0], low[k + 1] + up[1], fr, fi))
        (s_re, s_im), (m_re, m_im) = values
        for slot, value in enumerate((s_re, s_im, m_re, m_im)):
            f_scr[slot, pl.ds(n, 1), :] = jnp.sum(value, axis=0, keepdims=True)
        return 0

    lax.fori_loop(0, nstate, one, 0, unroll=2)
    a, b, z_re, z_im, one_re, one_im, far_re, far_im, den_re, den_im, inv, g_re, g_im = (
        term_ref[slot] for slot in range(TERMS)
    )
    f0, f1 = (f_scr[0], f_scr[1]), (f_scr[2], f_scr[3])
    gf_re, gf_im = cmul(g_re, g_im, *f0)
    dw_scr[0:nstate] = gf_re
    dw_scr[nstate:] = -gf_im
    inv_one = 1.0 / (one_re * one_re + one_im * one_im)
    near_re, near_im = cmul(z_re, z_im, one_re * inv_one, -one_im * inv_one)
    far_re, far_im = cmul(far_re, far_im, den_re * inv, -den_im * inv)
    q_re, q_im = cmul(length * far_re - near_re, length * far_im - near_im, *f0)
    c_re, c_im = cmul(w_ref[0:nstate], w_ref[nstate:], g_re, g_im)
    y_re, y_im = cmul(c_re, c_im, q_re + f1[0], q_im + f1[1])
    by_a = a * y_re
    by_step = by_a - b * y_im
    step = jnp.exp(dvec_ref[2:3])
    by_imag = -step * y_im
    d_step = jnp.sum(by_step, axis=0, keepdims=True)
    lane, state = iota((nstate, lanes), 1), iota((nstate, lanes), 0)
    col_a = jnp.sum(by_a, axis=1, keepdims=True)
    col_b = jnp.sum(by_imag, axis=1, keepdims=True)
    grid = jnp.where(lane == state % per, col_a, jnp.where(lane == state % per + per, col_b, 0.0))
    rates = exact_dot((iota((ndp, nstate), 0) == iota((ndp, nstate), 1) // per).astype(f32), grid)
    vecs = (d_step, dk_scr[0:1], dvec_ref[0:1], dvec_ref[1:2])
    group = iota((1, LANES), 1) // sub
    cols = dlb_ref.shape[1] // ndp
    for i in range(ndp):
        main = jnp.zeros((height, LANES), f32)
        row = jnp.zeros((1, LANES), f32)
        for u in range(groups):
            main = jnp.where(group == u, moved(dw_scr[u * height : (u + 1) * height], (u - i) * sub), main)
            if u < 4:
                row = jnp.where(group == u, moved(jnp.broadcast_to(vecs[u], (8, LANES)), (u - i) * sub)[0:1], row)
        o_ref[i] = jnp.zeros(o_ref.shape[1:], f32)
        o_ref[i, 0:height] = main
        o_ref[i, height : height + 1] = row
        o_ref[i, height + 1 : height + 2] = rates[i : i + 1]
        o_ref[i, height + 2 : height + 3, 0:cols] = dlb_ref[:, i * cols : (i + 1) * cols]


def sum_kernel(x_ref, o_ref):
    total = x_ref[0].astype(f32)
    for i in range(1, x_ref.shape[0]):
        total = total + x_ref[i].astype(f32)
    o_ref[...] = total.astype(o_ref.dtype)


def last_kernel(sub, rows, *refs):
    *parts, w_ref, step_ref, skip_ref, gain_ref, bias_ref, lam_ref, imag_ref, lb_ref, dw_ref = refs
    n_w, own = w_ref.shape
    nseq = LANES * own // sub // LANES
    parts, dws = parts[:nseq], parts[nseq:]
    groups = LANES // sub
    height = n_w // groups
    per, cols = lam_ref.shape[1], lb_ref.shape[1]
    group = iota((1, LANES), 1) // sub
    me = lax.axis_index("seq")
    small = [part[0:rows] for part in parts]
    for u in range(groups):
        acc = jnp.zeros((rows, LANES), f32)
        for d, value in enumerate(small):
            c = me ^ d
            acc = jnp.where(group == c, pltpu.roll(value, (c - u) * sub + LANES, 1), acc)
        w_ref[u * height : (u + 1) * height] = acc[0:height, 0:own]
        if u < 4:
            (step_ref, skip_ref, gain_ref, bias_ref)[u][...] = acc[height : height + 1, 0:own]
    total = sum(small[1:], small[0])
    lam_ref[...] = total[height + 1 : height + 2, 0:per]
    imag_ref[...] = pltpu.roll(total, LANES - per, 1)[height + 1 : height + 2, 0:per]
    lb_ref[...] = total[height + 2 : height + 3, 0:cols]
    for d in range(nseq):
        part_ref, first = (dws[d], 0) if dws else (parts[d], rows)
        c = me ^ d
        for i in range((part_ref.shape[0] - first) // sub):
            at = pl.multiple_of((i * nseq + c) * sub, sub)
            dw_ref[pl.ds(at, sub)] = part_ref[first + i * sub : first + (i + 1) * sub]


def swap(x, axis, by):
    n = lax.axis_size(axis)
    return jax.tree.map(lambda v: lax.ppermute(v, axis, [(i, i ^ by) for i in range(n)]), x)


def trade(parts, axis):
    return [parts[0]] + [swap(parts[d], axis, d) for d in range(1, len(parts))]


def tie(*values):
    return lax.optimization_barrier(values)


def on_device(block_in, cotangent, ln_gain, ln_bias, lambda_log, lambda_imag, dss_weight, log_step, skip_gain,
              lin_weight, lin_bias, doc_lengths):
    ndp, nseq = lax.axis_size("dp"), lax.axis_size("seq")
    count, block, width = block_in.shape
    length = block * nseq
    own = ln_gain.shape[0]
    sub = own // nseq
    wide = width // nseq
    per = lambda_log.shape[0]
    nstate = per * ndp
    n_w = 2 * nstate
    cols = lin_weight.shape[1]
    tokens = count * block
    height = n_w * sub // LANES
    rows = height + 8
    steps = [1 << k for k in reversed(range(ndp.bit_length() - 1))]
    masks = [0]
    for step in steps:
        masks += [mask ^ step for mask in masks]

    def row(v):
        return v.reshape(1, -1)

    packed = call(partial(pack_kernel, sub), shape((1, rows, LANES)), [VM] * 8, name="pack", mib=60, us=2)(
        dss_weight.reshape(n_w, own), row(log_step), row(skip_gain), row(ln_gain), row(ln_bias),
        row(lambda_log), row(lambda_imag), row(lin_bias)
    )

    piece = shape((count, block, wide), bf16)
    shared, shared_parts = packed, [packed]
    w_slots = [lin_weight[None]]
    f_table, ft_table = dft_tables(block)
    w_more = hats = None
    for number, step in enumerate(steps):
        more = swap(shared, "dp", step)
        if number == 0:
            x_late, _ = tie(block_in, shared)
            hats = call(
                partial(spread_kernel, own, sub), [shape((count, block + STAT_ROWS, wide), bf16)] * nseq, [AN],
                scratch=[pltpu.VMEM((count, block, width), bf16), DMA((count,))], name="spread", us=2,
            )(x_late)
            more, *_ = tie(more, *hats)
        if number == 1:
            hats = trade(hats, "seq")
            more, _ = tie(more, hats[1])
        if number == 2:
            w_more = swap(w_slots[0], "dp", steps[0])
        shared_parts.append(more)
        if number < len(steps) - 1:
            shared = jnp.concatenate([shared, more], axis=0)

    spec = (nseq, 2 * block, wide)
    kh, vec, w_all, terms, pows = call(
        partial(lag_kernel, sub, length, masks, len(shared_parts)),
        [shape(spec), shape((8, wide)), shape((n_w, wide)), shape((TERMS, nstate, wide)),
         shape((2 * len(POWERS), nstate, wide))],
        [VM] * (len(shared_parts) + 1),
        scratch=[pltpu.VMEM((length, wide), f32), pltpu.VMEM((2, nstate, wide), f32),
                 pltpu.VMEM((3 * block, nseq * wide), bf16), pltpu.VMEM((2 * block, nseq * wide), f32)],
        name="lag_kernel", us=0, keep=[ft_table, block_in, cotangent],
    )(*shared_parts, f_table)

    kh, w_more = tie(kh, w_more)
    w_late = jnp.concatenate([w_slots[0], w_more], axis=0)
    ahead = steps[1:]
    if len(ahead) == 2:
        w_slots = [w_late, swap(w_late, "dp", ahead[0]), swap(w_late, "dp", ahead[1])]
    else:
        w_slots = [w_late]
        for step in ahead:
            w_slots = [jnp.concatenate(w_slots + [swap(slot, "dp", step) for slot in w_slots], axis=0)]

    blocks4 = (count, nseq, block, wide)
    items = nseq + doc_lengths.shape[1] - 1
    lens = pltpu.SMEM(doc_lengths.shape, i32)
    cuts = pltpu.SMEM((count, items + 1), i32)
    across = items * count * wide
    *convs, spectra_u, x_blocks = call(
        conv_kernel, [piece] * nseq + [shape((2 * block, across)), shape(blocks4)],
        [VM] * nseq + [AN] + [VM] * 4,
        scratch=[lens, cuts, pltpu.VMEM((3 * block, across), bf16), pltpu.VMEM((2 * block, across), f32),
                 pltpu.VMEM((6 * block, across), bf16), pltpu.VMEM(blocks4, f32), DMA],
        name="doc_conv", mib=20, us=7, keep=[w_all, terms, pows, block_in, cotangent],
    )(*hats, doc_lengths, vec, kh, f_table, ft_table)
    keep = [w_all, terms, pows, vec, kh, f_table, ft_table, spectra_u, x_blocks]
    if len(ahead) == 2:
        *convs, w_slots[1], w_slots[2] = tie(*convs, w_slots[1], w_slots[2])
    convs = trade(convs, "seq")
    if len(ahead) == 2:
        w_slots.append(swap(w_slots[1], "dp", ahead[1]))
    pows_late, _ = tie(pows, convs[1])
    far = call(power_kernel, shape((2 * DOCMAX // PAIR, nstate, wide)), [VM], name="state_powers", mib=16, us=1, keep=keep)(pows_late)
    convs[2], _ = tie(convs[2], far)
    keep.append(far)
    if cols % LANES == 0 and sub % 16 == 0:
        shared = jnp.concatenate([shared, shared_parts[-1]], axis=0)
        shared, convs[1] = tie(shared, convs[1])
        w_lin, bias_full = call(
            partial(rows_kernel, sub, nseq, masks), [shape((width, 2 * width), bf16), shape((1, 2 * width))],
            [VM] * (1 + len(w_slots)), name="linear_rows", us=1, keep=keep,
        )(shared, *w_slots)
    else:
        shared = jnp.concatenate([shared, shared_parts[-1]], axis=0)
        place = jnp.asarray([masks.index(i) for i in range(ndp)])[lax.axis_index("dp") ^ jnp.arange(ndp)]
        w_lin = jnp.take(jnp.concatenate(w_slots, axis=0), place, axis=0)
        w_lin = w_lin.reshape(ndp, ndp, nseq, sub, cols).transpose(2, 1, 3, 0, 4).reshape(width, 2 * width)
        bias_full = jnp.take(shared[:, height + 2, :cols], place, axis=0).reshape(1, 2 * width)

    group = shape((2, wide, 2 * width), bf16)
    block_out, d_lin_bias, *d_convs, stay, send = call(
        dense_kernel,
        [shape((count, block, width), bf16), shape((1, 2 * width))] + [piece] * nseq + [group] * 2,
        [VM] * nseq + [AN, AN, VM, VM],
        scratch=[pltpu.VMEM((count, block, width), bf16), pltpu.VMEM((count, block, width), bf16),
                 pltpu.VMEM((tokens, width), bf16), pltpu.VMEM((tokens, 2 * width), bf16),
                 pltpu.VMEM((block, width), f32), pltpu.VMEM((block, 2 * width), f32), pltpu.VMEM((block, width), f32), DMA((2,))],
        name="gated_linear", mib=16, us=5, keep=keep,
    )(*convs, block_in, cotangent, w_lin, bias_full)
    d_convs = trade(d_convs, "seq")

    staged = cols % LANES == 0
    if staged:
        stay, send = call(
            halve_kernel, [shape((1, wide, 2 * width), bf16)] * 2, [VM, VM], name="weight_half", keep=keep
        )(stay, swap(send, "seq", 1))
        d_convs[2], *_ = tie(d_convs[2], send)
        dw_other = swap(send, "seq", 2)
    else:
        full = jnp.stack([stay[0], send[0], stay[1], send[1]])
        full = full.reshape(nseq, wide, ndp, cols).transpose(2, 0, 1, 3)
        dw_own = jnp.sum(lax.all_to_all(full, "dp", 0, 0, tiled=True).astype(f32), axis=0)
        dw_own = sum(trade([dw_own[d] for d in range(nseq)], "seq"))

    out = call(
        back_kernel, [piece] * nseq + [shape(spec), shape((3, wide))],
        [VM] * (nseq + 1) + [AN] + [VM] * 5,
        scratch=[lens, cuts, pltpu.VMEM(blocks4, bf16), pltpu.VMEM((2 * block, across), bf16),
                 pltpu.VMEM((2 * block, across), f32), pltpu.VMEM((2 * block, across), f32),
                 pltpu.VMEM((6 * block, across), bf16), pltpu.VMEM(blocks4, f32), DMA],
        name="doc_conv_grad", mib=24, us=8, keep=[w_all, terms, pows, far],
    )(*d_convs, x_blocks, doc_lengths, spectra_u, vec, kh, f_table, ft_table)
    g_own, dkh, d_norm = out[:nseq], out[nseq], out[nseq + 1]
    if staged:
        stay, send = call(
            deal_kernel, [shape((ndp // 2, wide, cols))] * 2, [VM, VM], name="weight_deal", us=1, keep=[w_all, terms, pows, far]
        )(stay, dw_other)
        dkh, *_ = tie(dkh, send)
        dw_other = swap(send, "dp", 1)

    small = call(
        partial(state_grad_kernel, sub, length), shape((ndp, rows, LANES)), [VM] * 8,
        scratch=[pltpu.VMEM((length, wide), f32), pltpu.VMEM((4, nstate, wide), f32), pltpu.VMEM((n_w, wide), f32),
                 pltpu.VMEM((6 * block, nseq * wide), bf16)],
        name="state_grad", mib=10, us=10,
    )(w_all, terms, pows, far, dkh, d_norm, d_lin_bias, ft_table)
    small, *g_own = tie(small, *g_own)
    if staged:
        small, dw_other = tie(small, dw_other)
    small = lax.all_to_all(small, "dp", 0, 0, tiled=True)
    gs = trade(g_own, "seq")
    if staged:
        step = 2
        while step < ndp:
            stay, send = call(
                halve_kernel, [shape((ndp // 2 // step, wide, cols))] * 2, [VM, VM], name="weight_half"
            )(stay, dw_other)
            dw_other = swap(send, "dp", step)
            step *= 2
    grad_in = call(
        partial(ln_back_kernel, own, sub), shape((count, block, width), bf16), [VM] * (nseq + 2),
        name="layer_norm_grad", mib=12,
    )(*gs, block_in, cotangent)
    if staged:
        merged = call(merge_kernel, shape((rows + wide, cols)), [VM] * 3, name="last_sums", us=0.5)(small, stay, dw_other)
        merged = trade([merged] * nseq, "seq")
        smalls, dws = merged, []
    else:
        small = call(sum_kernel, shape((rows, LANES)), [VM], name="small_sum", us=0.5)(small)
        smalls, dws = trade([small] * nseq, "seq"), trade([dw_own] * nseq, "seq")
    d_w, d_step, d_skip, d_gain, d_bias, d_lam, d_imag, d_lb, dw = call(
        partial(last_kernel, sub, rows),
        [shape((n_w, own))] + [shape((1, own))] * 4 + [shape((1, per))] * 2 + [shape((1, cols)), shape((width, cols))],
        [VM] * (len(smalls) + len(dws)), name="last", us=1,
    )(*smalls, *dws)
    return (
        block_out, grad_in, d_gain.reshape(own), d_bias.reshape(own), d_lam.reshape(per), d_imag.reshape(per),
        d_w.reshape(2, nstate, own), d_step.reshape(own), d_skip.reshape(own), dw, d_lb.reshape(cols),
    )


def solution(mesh):
    placed = (
        P("dp", "seq", None), P("dp", "seq", None), P("dp"), P("dp"), P("dp"), P("dp"),
        P(None, None, "dp"), P("dp"), P("dp"), P(None, "dp"), P("dp"), P("dp", None),
    )
    return jax.shard_map(
        on_device,
        mesh=mesh,
        in_specs=placed,
        out_specs=(
            P("dp", "seq", None), P("dp", "seq", None), P("dp"), P("dp"), P("dp"), P("dp"),
            P(None, None, "dp"), P("dp"), P("dp"), P(None, "dp"), P("dp"),
        ),
        check_vma=False,
    )
```

```python
from functools import partial

import jax
import jax.numpy as jnp
import numpy as np
from jax import lax
from jax.experimental import pallas as pl
from jax.experimental.pallas import tpu as pltpu
from jax.sharding import PartitionSpec as P

f32, bf16, i32 = jnp.float32, jnp.bfloat16, jnp.int32
ln_eps = 1e-05
DOCMAX = 800
FINE = 8
COARSE = 10
LANES = 128
NN = (((1,), (0,)), ((), ()))
NT = (((1,), (1,)), ((), ()))
TN = (((0,), (0,)), ((), ()))
VM = pl.BlockSpec(memory_space=pltpu.VMEM)
AN = pl.BlockSpec(memory_space=pl.ANY)
DMA = pltpu.SemaphoreType.DMA


def dot(a, b, dims=NN):
    return lax.dot_general(a, b, dims, preferred_element_type=f32)


def exact_dot(a, b, dims=NN):
    return lax.dot_general(a, b, dims, precision=lax.Precision.HIGHEST, preferred_element_type=f32)


def shape(dims, dtype=f32):
    return jax.ShapeDtypeStruct(dims, dtype)


def call(body, out, specs, scratch=(), name=None, mib=8, outs=None, us=0, keep=()):
    inputs, kept = len(specs), len(keep)

    def whole(*refs):
        body(*refs[:inputs], *refs[inputs + kept :])

    kernel = pl.pallas_call(
        whole,
        out_shape=out,
        in_specs=list(specs) + [AN] * kept,
        out_specs=outs if outs is not None else jax.tree.map(lambda _: VM, out),
        scratch_shapes=list(scratch),
        cost_estimate=pl.CostEstimate(flops=int(us * 1.15e9), bytes_accessed=1000, transcendentals=0),
        compiler_params=pltpu.CompilerParams(vmem_limit_bytes=mib * 2**20),
        name=name,
    )
    return lambda *args: kernel(*args, *keep)


def iota(dims, axis):
    return lax.broadcasted_iota(i32, dims, axis)


def cmul(ar, ai, br, bi):
    return ar * br - ai * bi, ar * bi + ai * br


def small_expm1(a):
    poly = jnp.full_like(a, 1.0)
    for k in range(9, 1, -1):
        poly = 1.0 + poly * a * (1.0 / k)
    return jnp.where(jnp.abs(a) < 0.5, a * poly, jnp.exp(a) - 1.0)


def state_terms(rate_log, freq, step_log, length):
    step = jnp.exp(step_log)
    a = -jnp.exp(rate_log) * step
    b = freq * step
    half = jnp.sin(0.5 * b)
    cos_b, sin_b, mag = jnp.cos(b), jnp.sin(b), jnp.exp(a)
    one_re = 2.0 * half * half - small_expm1(a) * cos_b
    one_im = -mag * sin_b
    far = jnp.exp(length * a)
    far_re, far_im = far * jnp.cos(length * b), far * jnp.sin(length * b)
    den_re, den_im = 1.0 - far_re, -far_im
    inv = 1.0 / (den_re * den_re + den_im * den_im)
    g_re = (one_re * den_re + one_im * den_im) * inv
    g_im = (one_im * den_re - one_re * den_im) * inv
    return a, b, mag * cos_b, mag * sin_b, one_re, one_im, far_re, far_im, den_re, den_im, inv, g_re, g_im


TERMS = 13


POWERS = (1, 2, 4) + tuple(8 * v for v in range(1, COARSE + 1))


def power_table(zr, zi):
    table = {1: (zr, zi)}
    for p in POWERS[1:]:
        at = p // 16 * 8 if p > 8 else p // 2
        table[p] = cmul(*table[at], *table[p - at])
    return [table[p] for p in POWERS]


def wide_row(ref, p, half, n):
    return jnp.broadcast_to(ref[2 * POWERS.index(p) + half, pl.ds(n, 1), :], (8, LANES))


def rows8(ref, n):
    at = iota((8, LANES), 0)
    total = None
    for p in (1, 2, 4):
        here = at & p > 0
        one = jnp.where(here, wide_row(ref, p, 0, n), 1.0), jnp.where(here, wide_row(ref, p, 1, n), 0.0)
        total = one if total is None else cmul(*total, *one)
    return total


def powers(ref, n):
    return [None] + [(wide_row(ref, 8 * v, 0, n), wide_row(ref, 8 * v, 1, n)) for v in range(1, COARSE + 1)]


def halves(x):
    hi = x.astype(bf16)
    return hi, (x - hi.astype(f32)).astype(bf16)


def stack3(ref, cols, x):
    height = x.shape[0]
    hi, lo = halves(x)
    ref[0:height, cols] = hi
    ref[height : 2 * height, cols] = lo
    ref[2 * height : 3 * height, cols] = hi


def signs(block, lanes):
    return jnp.where(iota((block, lanes), 0) & 1 > 0, -1.0, 1.0)


def dft_tables(block):
    k, j = np.arange(block)[:, None], np.arange(block)[None, :]
    theta = np.pi * (((2 * k + 1) * j) % (4 * block)) / (2 * block)
    full = np.concatenate([np.cos(theta), -np.sin(theta)], axis=0)
    high = full.astype(jnp.bfloat16)
    low = (full - high.astype(np.float64)).astype(jnp.bfloat16)
    return (jnp.asarray(np.concatenate([high, high, low], axis=1)),
            jnp.asarray(np.concatenate([high.T, high.T, low.T], axis=1)))


def moved(x, by):
    return x if by % LANES == 0 else pltpu.roll(x, by % LANES, 1)


def pack_kernel(sub, w_ref, step_ref, skip_ref, gain_ref, bias_ref, lam_ref, imag_ref, lb_ref, o_ref):
    own, per, cols = step_ref.shape[1], lam_ref.shape[1], lb_ref.shape[1]
    groups = LANES // sub
    height = w_ref.shape[0] // groups
    pick = (iota((own, LANES), 0) == lax.axis_index("seq") * sub + iota((own, LANES), 1) % sub).astype(f32)
    w = exact_dot(w_ref[...], pick)
    vec = exact_dot(jnp.concatenate([step_ref[...], skip_ref[...], gain_ref[...], bias_ref[...]] * 2, axis=0), pick)
    group = iota((1, LANES), 1) // sub
    main = jnp.zeros((height, LANES), f32)
    row = jnp.zeros((1, LANES), f32)
    for u in range(groups):
        main = jnp.where(group == u, w[u * height : (u + 1) * height], main)
        if u < 4:
            row = jnp.where(group == u, vec[u : u + 1], row)
    spot, lane = iota((per, LANES), 0), iota((per, LANES), 1)
    rates = exact_dot(jnp.broadcast_to(lam_ref[...], (8, per)), (lane == spot).astype(f32)) + exact_dot(
        jnp.broadcast_to(imag_ref[...], (8, per)), (lane == spot + per).astype(f32)
    )
    o_ref[...] = jnp.zeros(o_ref.shape, f32)
    o_ref[0, 0:height] = main
    o_ref[0, height : height + 1] = row
    o_ref[0, height + 1 : height + 2] = rates[0:1]
    o_ref[0, height + 2 : height + 3, 0:cols] = lb_ref[...]


def lag_kernel(sub, length, masks, n_parts, *refs):
    pieces, refs = refs[:n_parts], refs[n_parts:]
    f_ref, kh_ref, vec_ref, w_ref, term_ref, pow_ref, k_scr, z_scr, rhs_scr, kf_scr = refs
    slots = [piece.at[t] for piece in pieces for t in range(piece.shape[0])]
    ndp = len(slots)
    me = lax.axis_index("dp")
    n_w, lanes = w_ref.shape
    nstate = n_w // 2
    per = nstate // ndp
    groups = LANES // sub
    height = n_w // groups
    block = f_ref.shape[0] // 2
    group = iota((1, LANES), 1) // sub
    for u in range(groups):
        acc = jnp.zeros(slots[0].shape, f32)
        for t in range(ndp):
            i = me ^ masks[t]
            acc = jnp.where(group == i, pltpu.roll(slots[t][...], (i - u) * sub + LANES * ndp, 1), acc)
        w_ref[u * height : (u + 1) * height] = acc[0:height]
        if u < 4:
            vec_ref[u : u + 1] = acc[height : height + 1]
    vec_ref[4:8] = jnp.zeros((4, lanes), f32)
    rows = jnp.concatenate([slot[height + 1 : height + 2] for slot in slots], axis=0)
    source = jnp.zeros((nstate, ndp), i32)
    for t in range(ndp):
        source = jnp.where(iota((nstate, ndp), 1) == t, me ^ masks[t], source)
    spread = exact_dot((iota((nstate, ndp), 0) // per == source).astype(f32), rows)
    lane, state = iota((nstate, lanes), 1), iota((nstate, lanes), 0)
    lam = jnp.sum(jnp.where(lane == state % per, spread, 0.0), axis=1, keepdims=True)
    imag = jnp.sum(jnp.where(lane == state % per + per, spread, 0.0), axis=1, keepdims=True)
    terms = state_terms(lam, imag, vec_ref[0:1], float(length))
    for slot, value in enumerate(terms):
        term_ref[slot] = value
    z_scr[0], z_scr[1] = cmul(w_ref[0:nstate], w_ref[nstate:], terms[11], terms[12])
    for slot, pair in enumerate(power_table(terms[2], terms[3])):
        pow_ref[2 * slot], pow_ref[2 * slot + 1] = pair
    k_scr[...] = jnp.zeros_like(k_scr)

    def pair(m, _):
        ready = []
        for n in (2 * m, 2 * m + 1):
            fr, fi = rows8(pow_ref, n)
            cr = jnp.broadcast_to(z_scr[0, pl.ds(n, 1), :], (8, lanes))
            ci = jnp.broadcast_to(z_scr[1, pl.ds(n, 1), :], (8, lanes))
            ready.append([cmul(fr, fi, cr, ci), powers(pow_ref, n)])
        for u in range(DOCMAX // FINE // COARSE):
            for v in range(COARSE):
                at = (u * COARSE + v) * FINE
                total = k_scr[at : at + FINE]
                for (xr, xi), pows in ready:
                    total = total + (xr * pows[v][0] - xi * pows[v][1] if v else xr)
                k_scr[at : at + FINE] = total
            for one in ready:
                one[0] = cmul(*one[0], *one[1][COARSE])
        return 0

    lax.fori_loop(0, nstate // 2, pair, 0)
    k_scr[0:1] += vec_ref[1:2]
    parts = length // block
    for p in range(parts):
        stack3(rhs_scr, slice(p * lanes, (p + 1) * lanes), k_scr[p * block : (p + 1) * block])
    kf_scr[...] = dot(f_ref[...], rhs_scr[...])
    sign = signs(block, lanes)
    for p in range(parts):
        here, past = slice(p * lanes, (p + 1) * lanes), slice((p - 1) * lanes, p * lanes)
        re, im = kf_scr[:block, here], kf_scr[block:, here]
        if p:
            re = re - sign * kf_scr[block:, past]
            im = im + sign * kf_scr[:block, past]
        kh_ref[p, :block] = re * (1.0 / block)
        kh_ref[p, block:] = im * (1.0 / block)


def members(own, sub, c, width, wide):
    lane = iota((1, wide), 1)
    return (iota((width, wide), 0) == (lane // sub) * own + c * sub + lane % sub).astype(f32).astype(bf16)


STAT_ROWS = 16


def terms3(x):
    hi, rest = x.astype(bf16), x
    out = [hi]
    for _ in range(2):
        rest = rest - out[-1].astype(f32)
        out.append(rest.astype(bf16))
    return out


def spread_kernel(own, sub, x_any, *refs):
    *o_refs, x_ref, sems = refs
    count, block, width = x_ref.shape
    wide = o_refs[0].shape[-1]
    copies = [pltpu.make_async_copy(x_any.at[s], x_ref.at[s], sems.at[s]) for s in range(count)]
    for copy in copies:
        copy.start()
    places = [members(own, sub, lax.axis_index("seq") ^ d, width, wide) for d in range(len(o_refs))]
    eye = (iota((block, block), 0) == iota((block, block), 1)).astype(f32).astype(bf16)
    lane = iota((block, LANES), 1)
    for s in range(count):
        copies[s].wait()
        for o_ref, cols in zip(o_refs, places):
            o_ref[s, 0:block] = dot(x_ref[s], cols).astype(bf16)
        x = x_ref[s].astype(f32)
        mean = jnp.mean(x, axis=-1, keepdims=True)
        centre = x - mean
        inv = lax.rsqrt(jnp.mean(centre * centre, axis=-1, keepdims=True) + ln_eps)
        table = jnp.zeros((block, LANES), f32)
        for k, term in enumerate(terms3(mean) + terms3(inv)):
            table = jnp.where(lane == k, term.astype(f32), table)
        turned = dot(table.astype(bf16), eye, TN)
        both = jnp.concatenate([turned[0:8, 0:LANES], turned[0:8, LANES:]], axis=0).astype(bf16)
        for o_ref in o_refs:
            o_ref[s, block:] = both


def normal_inputs(piece_ref, s, block):
    stats = piece_ref[s, block:]
    spot, lane = iota((STAT_ROWS, 4 * LANES), 0), iota((STAT_ROWS, 4 * LANES), 1) // LANES
    first = lane // 2 * 8 + lane % 2 * 3
    pick = ((spot >= first) & (spot < first + 3)).astype(f32).astype(bf16)
    cols = dot(stats, pick, TN)
    parts = []
    for half in (0, 1):
        rows = piece_ref[s, half * LANES : (half + 1) * LANES].astype(f32)
        at = 2 * half * LANES
        parts.append((rows - cols[:, at : at + LANES]) * cols[:, at + LANES : at + 2 * LANES])
    return jnp.concatenate(parts, axis=0)


def ln_back_kernel(own, sub, g0, g1, g2, g3, x_ref, c_ref, o_ref):
    count, block, width = x_ref.shape
    wide = g0.shape[-1]
    tokens = count * block
    g = jnp.zeros((tokens, width), f32)
    for d, g_ref in enumerate((g0, g1, g2, g3)):
        cols = members(own, sub, lax.axis_index("seq") ^ d, width, wide)
        g = g + dot(g_ref[...].reshape(tokens, wide), cols, NT)
    x = x_ref[...].astype(f32).reshape(tokens, width)
    centre = x - jnp.mean(x, axis=-1, keepdims=True)
    inv = lax.rsqrt(jnp.mean(centre * centre, axis=-1, keepdims=True) + ln_eps)
    hat = centre * inv
    mean_g = jnp.mean(g, axis=-1, keepdims=True)
    mean_gx = jnp.mean(g * hat, axis=-1, keepdims=True)
    cot = c_ref[...].astype(f32).reshape(tokens, width)
    o_ref[...] = (cot + inv * (g - mean_g - hat * mean_gx)).astype(bf16).reshape(o_ref.shape)


def segments(len_ref, cut_ref, block, parts):
    count, docs = len_ref.shape
    last = parts + docs - 1
    for s in range(count):
        ends = []
        for d in range(docs - 1):
            ends.append(len_ref[s, d] + (ends[-1] if ends else 0))
        cut_ref[s, 0] = 0
        cut_ref[s, last] = parts * block
        for d, end in enumerate(ends):
            rank = 1 + d
            for k in range(1, parts):
                rank = rank + jnp.where(end > k * block, 1, 0)
            cut_ref[s, rank] = end
        for k in range(1, parts):
            rank = k
            for end in ends:
                rank = rank + jnp.where(end <= k * block, 1, 0)
            cut_ref[s, rank] = k * block


def document(len_ref, s, at):
    start, end, total = 0, 0, 0
    for d in range(len_ref.shape[1]):
        total = total + len_ref[s, d]
        start = jnp.where(total <= at, total, start)
    total = 0
    end = 1 << 30
    for d in range(len_ref.shape[1]):
        total = total + len_ref[s, d]
        end = jnp.minimum(end, jnp.where(total > at, total, 1 << 30))
    return start, end


def within(cut_ref, s, j, block, lanes):
    start, end = cut_ref[s, j], cut_ref[s, j + 1]
    b = start // block
    rows = b * block + iota((block, lanes), 0)
    return b, (rows >= start) & (rows < end)


def column(j, s, count, lanes):
    return pl.ds(pl.multiple_of((j * count + s) * lanes, lanes), lanes)


CHUNK = 64


def lengths_in(len_ref, len_scr, sem):
    copy = pltpu.make_async_copy(len_ref, len_scr, sem)
    copy.start()
    copy.wait()


def split_rows(y_scr, rows, cols, value, block, half):
    hi, lo = halves(value)
    for third, part in enumerate((hi, lo, hi)[: y_scr.shape[0] // (2 * block)]):
        at = (2 * third + half) * block
        y_scr[at + rows.start : at + rows.stop, cols] = part


def row_chunks(block):
    for r in range(0, block, CHUNK):
        yield slice(r, r + CHUNK), slice(block + r, block + r + CHUNK)


def conv_kernel(x0, x1, x2, x3, len_ref, vec_ref, kh_ref, f_ref, ft_ref,
                o0, o1, o2, o3, s_scr, x_scr, len_scr, cut_ref, rhs_scr, acc_scr, y_scr, out_scr, sem):
    count, parts, block, lanes = x_scr.shape
    me = lax.axis_index("seq")
    lengths_in(len_ref, len_scr, sem)
    for d, x_ref in enumerate((x0, x1, x2, x3)):
        for s in range(count):
            x_scr[s, me ^ d] = normal_inputs(x_ref, s, block)
    segments(len_scr, cut_ref, block, parts)
    gain, bias = vec_ref[2:3], vec_ref[3:4]
    items = cut_ref.shape[1] - 1
    for j in range(items):
        for s in range(count):
            b, keep = within(cut_ref, s, j, block, lanes)
            cols = slice((j * count + s) * lanes, (j * count + s + 1) * lanes)
            stack3(rhs_scr, cols, jnp.where(keep, x_scr[s, b] * gain + bias, 0.0))
        tile = slice(j * count * lanes, (j + 1) * count * lanes)
        s_scr[:, tile] = dot(f_ref[...], rhs_scr[:, tile])

    def own(j, _):
        for s in range(count):
            cols = column(j, s, count, lanes)
            for re, im in row_chunks(block):
                acc_scr[re, cols], acc_scr[im, cols] = cmul(
                    kh_ref[0, re], kh_ref[0, im], s_scr[re, cols], s_scr[im, cols]
                )
            start, _ = document(len_scr, s, cut_ref[s, j])
            b = cut_ref[s, j] // block
            first = j
            for i in range(items):
                first = first - jnp.where((i < j) & (cut_ref[s, i] >= start), 1, 0)

            def add(i, _):
                p = b - cut_ref[s, i] // block
                there = column(i, s, count, lanes)
                for re, im in row_chunks(block):
                    more = cmul(kh_ref[p, re], kh_ref[p, im], s_scr[re, there], s_scr[im, there])
                    acc_scr[re, cols] += more[0]
                    acc_scr[im, cols] += more[1]
                return 0

            lax.fori_loop(first, j, add, 0)
            for re, im in row_chunks(block):
                split_rows(y_scr, re, cols, acc_scr[re, cols], block, 0)
                split_rows(y_scr, re, cols, acc_scr[im, cols], block, 1)
        return 0

    lax.fori_loop(0, items, own, 0)
    acc_scr[0:block] = dot(ft_ref[:, 0 : y_scr.shape[0]], y_scr[...])
    for j in range(items):
        for s in range(count):
            b, keep = within(cut_ref, s, j, block, lanes)
            cols = slice((j * count + s) * lanes, (j * count + s + 1) * lanes)
            out_scr[s, b] = jnp.where(keep, acc_scr[0:block, cols], out_scr[s, b])
    for d, o_ref in enumerate((o0, o1, o2, o3)):
        for s in range(count):
            o_ref[s] = out_scr[s, me ^ d].astype(bf16)


def back_kernel(c0, c1, c2, c3, x_scr, len_ref, s_scr, vec_ref, kh_ref, f_ref, ft_ref,
                g0, g1, g2, g3, dkh_ref, dvec_ref,
                len_scr, cut_ref, v_scr, rhs_scr, sv_scr, acc_scr, y_scr, du_scr, sem):
    count, block, lanes = c0.shape
    parts = kh_ref.shape[0]
    me = lax.axis_index("seq")
    lengths_in(len_ref, len_scr, sem)
    for d, c_ref in enumerate((c0, c1, c2, c3)):
        for s in range(count):
            v_scr[s, me ^ d] = c_ref[s]
    dkh_ref[...] = jnp.zeros_like(dkh_ref)
    segments(len_scr, cut_ref, block, parts)
    items = cut_ref.shape[1] - 1
    for j in range(items):
        for s in range(count):
            b, keep = within(cut_ref, s, j, block, lanes)
            v = jnp.where(keep, v_scr[s, b].astype(f32), 0.0).astype(bf16)
            cols = slice((j * count + s) * lanes, (j * count + s + 1) * lanes)
            rhs_scr[:, cols] = v
        tile = slice(j * count * lanes, (j + 1) * count * lanes)
        sv_scr[:, tile] = dot(f_ref[:, 0:block], rhs_scr[:, tile])

    def own(j, _):
        for s in range(count):
            cols = column(j, s, count, lanes)
            for re, im in row_chunks(block):
                vr, vi, ur, ui = sv_scr[re, cols], sv_scr[im, cols], s_scr[re, cols], s_scr[im, cols]
                kr, ki = kh_ref[0, re], kh_ref[0, im]
                acc_scr[re, cols] = kr * vr + ki * vi
                acc_scr[im, cols] = kr * vi - ki * vr
                dkh_ref[0, re] += vr * ur + vi * ui
                dkh_ref[0, im] += vi * ur - vr * ui
            _, end = document(len_scr, s, cut_ref[s, j])
            b = cut_ref[s, j] // block
            last = j
            for i in range(items):
                last = last + jnp.where((i > j) & (cut_ref[s, i] < end), 1, 0)

            def add(i, _):
                p = cut_ref[s, i] // block - b
                there = column(i, s, count, lanes)
                for re, im in row_chunks(block):
                    vr, vi, ur, ui = sv_scr[re, there], sv_scr[im, there], s_scr[re, cols], s_scr[im, cols]
                    kr, ki = kh_ref[p, re], kh_ref[p, im]
                    acc_scr[re, cols] += kr * vr + ki * vi
                    acc_scr[im, cols] += kr * vi - ki * vr
                    dkh_ref[p, re] += vr * ur + vi * ui
                    dkh_ref[p, im] += vi * ur - vr * ui
                return 0

            lax.fori_loop(j + 1, last + 1, add, 0)
            for re, im in row_chunks(block):
                split_rows(y_scr, re, cols, acc_scr[re, cols], block, 0)
                split_rows(y_scr, re, cols, acc_scr[im, cols], block, 1)
        return 0

    lax.fori_loop(0, items, own, 0)
    acc_scr[0:block] = dot(ft_ref[:, 0 : y_scr.shape[0]], y_scr[...])
    for j in range(items):
        for s in range(count):
            b, keep = within(cut_ref, s, j, block, lanes)
            cols = slice((j * count + s) * lanes, (j * count + s + 1) * lanes)
            du_scr[s, b] = jnp.where(keep, acc_scr[0:block, cols], du_scr[s, b])
    gain = vec_ref[2:3]
    d_gain = jnp.zeros((8, lanes), f32)
    d_bias = jnp.zeros((8, lanes), f32)
    for d, g_ref in enumerate((g0, g1, g2, g3)):
        for s in range(count):
            for r in range(0, block, CHUNK):
                du = du_scr[s, me ^ d, r : r + CHUNK]
                d_bias += jnp.sum(du.reshape(CHUNK // 8, 8, lanes), axis=0)
                d_gain += jnp.sum((du * x_scr[s, me ^ d, r : r + CHUNK]).reshape(CHUNK // 8, 8, lanes), axis=0)
                g_ref[s, r : r + CHUNK] = (du * gain).astype(bf16)
    dvec_ref[0:1] = jnp.sum(d_gain, axis=0, keepdims=True)
    dvec_ref[1:2] = jnp.sum(d_bias, axis=0, keepdims=True)
    dvec_ref[2:3] = vec_ref[0:1]


def normal_cdf(v, bell):
    t = 1.0 / (1.0 + np.float32(0.3275911 / np.sqrt(2.0)) * jnp.abs(v))
    tail = t * (0.127414796 + t * (-0.142248368 + t * (0.7107068705 + t * (-0.7265760135 + t * 0.5307027145)))) * bell
    return jnp.where(v < 0.0, tail, 1.0 - tail)


def dense_kernel(q0, q1, q2, q3, x_any, c_any, w_ref, lb_ref,
                 out_ref, dlb_ref, d0, d1, d2, d3, stay_ref, send_ref,
                 x_ref, c_ref, act_ref, dpre_ref, slope_scr, pre_scr, dact_scr, sems):
    count, block, wide = q0.shape
    width = act_ref.shape[1]
    me = lax.axis_index("seq")
    copies = [pltpu.make_async_copy(x_any, x_ref, sems.at[0]), pltpu.make_async_copy(c_any, c_ref, sems.at[1])]
    for copy in copies:
        copy.start()

    def cols_of(d):
        return pl.ds(pl.multiple_of((me ^ d) * wide, wide), wide)

    def sequence(s, lb_sum):
        def slope(r, _):
            rows = pl.ds(pl.multiple_of(r * CHUNK, CHUNK), CHUNK)
            flat = pl.ds(pl.multiple_of(s * block + r * CHUNK, CHUNK), CHUNK)
            for d, q_ref in enumerate((q0, q1, q2, q3)):
                v = q_ref[s, rows].astype(f32)
                bell = jnp.exp(-0.5 * v * v)
                cdf = normal_cdf(v, bell)
                act_ref[flat, cols_of(d)] = (v * cdf).astype(bf16)
                slope_scr[rows, cols_of(d)] = cdf + v * (bell * np.float32(1.0 / np.sqrt(2.0 * np.pi)))
            return 0

        lax.fori_loop(0, block // CHUNK, slope, 0)
        whole = pl.ds(pl.multiple_of(s * block, block), block)
        pre_scr[...] = dot(act_ref[whole, :], w_ref[...])

        @pl.when(s == 0)
        def _():
            for copy in copies:
                copy.wait()

        def gate(r, total):
            rows = pl.ds(pl.multiple_of(r * 32, 32), 32)
            flat = pl.ds(pl.multiple_of(s * block + r * 32, 32), 32)
            first = pre_scr[rows, 0:width] + lb_ref[:, 0:width]
            sig = 1.0 / (1.0 + jnp.exp(-(pre_scr[rows, width:] + lb_ref[:, width:])))
            out_ref[s, rows] = (x_ref[s, rows].astype(f32) + first * sig).astype(bf16)
            d_first = c_ref[s, rows].astype(f32) * sig
            d_second = d_first * first * (1.0 - sig)
            d_pre = jnp.concatenate([d_first, d_second], axis=1).astype(bf16)
            dpre_ref[flat, :] = d_pre
            return total + jnp.sum(d_pre.astype(f32).reshape(4, 8, 2 * width), axis=0)

        lb_sum = lax.fori_loop(0, block // 32, gate, lb_sum)
        dact_scr[...] = dot(dpre_ref[whole, :], w_ref[...], NT)
        for d, o_ref in enumerate((d0, d1, d2, d3)):
            o_ref[s] = (dact_scr[:, cols_of(d)] * slope_scr[:, cols_of(d)]).astype(bf16)
        return lb_sum

    lb_sum = lax.fori_loop(0, count, sequence, jnp.zeros((8, 2 * width), f32))
    dlb_ref[...] = jnp.sum(lb_sum, axis=0, keepdims=True)
    for d in range(4):
        (send_ref if d & 1 else stay_ref)[d // 2] = dot(act_ref[:, cols_of(d)], dpre_ref[...], TN).astype(bf16)


def rows_kernel(sub, nseq, masks, shared_ref, *refs):
    *w_refs, o_ref, lb_ref = refs
    cols = w_refs[0].shape[-1]
    span = o_ref.shape[0] // nseq
    me = lax.axis_index("dp")
    bias_row = shared_ref.shape[1] - 8 + 2
    for t, mask in enumerate(masks):
        at = pl.ds(pl.multiple_of((me ^ mask) * cols, cols), cols)
        lb_ref[:, at] = shared_ref[t, bias_row : bias_row + 1, 0:cols]
    t = 0
    for w_ref in w_refs:
        for slot in range(w_ref.shape[0]):
            at = pl.ds(pl.multiple_of((me ^ masks[t]) * cols, cols), cols)
            t += 1
            for c in range(nseq):
                for i in range(span // sub):
                    o_ref[c * span + i * sub : c * span + (i + 1) * sub, at] = w_ref[
                        slot, (i * nseq + c) * sub : (i * nseq + c + 1) * sub
                    ]


def halve_kernel(mine_ref, other_ref, stay_ref, send_ref):
    for k in range(mine_ref.shape[0]):
        total = mine_ref[k].astype(f32) + other_ref[k].astype(f32)
        (send_ref if k & 1 else stay_ref)[k // 2] = total.astype(stay_ref.dtype)


def deal_kernel(mine_ref, other_ref, stay_ref, send_ref):
    part = stay_ref.shape[2]
    me = lax.axis_index("dp")
    for d in range(2 * stay_ref.shape[0]):
        cols = pl.ds(pl.multiple_of((me ^ d) * part, part), part)
        (send_ref if d & 1 else stay_ref)[d // 2] = mine_ref[0, :, cols].astype(f32) + other_ref[0, :, cols].astype(f32)


def merge_kernel(x_ref, mine_ref, other_ref, o_ref):
    rows = x_ref.shape[1]
    total = x_ref[0]
    for i in range(1, x_ref.shape[0]):
        total = total + x_ref[i]
    o_ref[0:rows] = total
    o_ref[rows:] = mine_ref[0] + other_ref[0]


PAIR = 2 * FINE


def power_kernel(pow_ref, o_ref):
    def some(g, _):
        rows = pl.ds(pl.multiple_of(g * 8, 8), 8)
        at = [2 * POWERS.index(PAIR * v) for v in range(1, COARSE // 2 + 1)]
        small = [(pow_ref[i, rows], pow_ref[i + 1, rows]) for i in at]
        x = jnp.ones((8, LANES), f32), jnp.zeros((8, LANES), f32)
        for u in range(DOCMAX // PAIR // (COARSE // 2)):
            for v in range(COARSE // 2):
                m = u * (COARSE // 2) + v
                o_ref[2 * m, rows], o_ref[2 * m + 1, rows] = cmul(*x, *small[v - 1]) if v else x
            x = cmul(*x, *small[-1])
        return 0

    lax.fori_loop(0, pow_ref.shape[1] // 8, some, 0)


CHAINS = 2


def state_grad_kernel(sub, length, w_ref, term_ref, pow_ref, far_ref, dkh_ref, dvec_ref, dlb_ref, ft_ref, o_ref,
                      dk_scr, f_scr, dw_scr, y_scr):
    ndp = o_ref.shape[0]
    n_w, lanes = w_ref.shape
    nstate = n_w // 2
    per = nstate // ndp
    groups = LANES // sub
    height = n_w // groups
    parts, twice, _ = dkh_ref.shape
    block = twice // 2
    sign = signs(block, lanes)
    for p in range(parts):
        re, im = dkh_ref[p, :block], dkh_ref[p, block:]
        if p + 1 < parts:
            re = re + sign * dkh_ref[p + 1, block:]
            im = im - sign * dkh_ref[p + 1, :block]
        stack3(y_scr, slice(p * lanes, (p + 1) * lanes), jnp.concatenate([re, im], axis=0))
    all_lags = dot(ft_ref[...], y_scr[...]) * (1.0 / block)
    for p in range(parts):
        dk_scr[p * block : (p + 1) * block] = all_lags[:, p * lanes : (p + 1) * lanes]
    at8 = iota((8, lanes), 0).astype(f32)

    def one(n, _):
        fr, fi = rows8(pow_ref, n)
        zero = jnp.zeros((8, lanes), f32)
        span = DOCMAX // PAIR // CHAINS
        sums = []
        for c in range(CHAINS):
            acc = [[zero] * 4, [zero] * 4]
            for m in range(c * span + span - 1, c * span - 1, -1):
                if m:
                    p_re = jnp.broadcast_to(far_ref[2 * m, pl.ds(n, 1), :], (8, lanes))
                    p_im = jnp.broadcast_to(far_ref[2 * m + 1, pl.ds(n, 1), :], (8, lanes))
                for h, one_acc in enumerate(acc):
                    at = m * PAIR + h * FINE
                    dk = dk_scr[at : at + FINE]
                    one_acc[0] = one_acc[0] + (dk * p_re if m else dk)
                    if m:
                        one_acc[1] = one_acc[1] + dk * p_im
                    if m > c * span:
                        one_acc[2], one_acc[3] = one_acc[2] + one_acc[0], one_acc[3] + one_acc[1]
            for one_acc in acc:
                one_acc[2], one_acc[3] = (one_acc[2 + k] + (c * span) * one_acc[k] for k in (0, 1))
            sums.append(acc)
        low, high = (
            [sum((acc[h][k] for acc in sums[1:]), sums[0][h][k]) for k in range(4)] for h in (0, 1)
        )
        for h, part in enumerate((low, high)):
            for k in (0, 1):
                part[2 + k] = PAIR * part[2 + k] + (at8 + float(h * FINE)) * part[k]
        shift = wide_row(pow_ref, FINE, 0, n), wide_row(pow_ref, FINE, 1, n)
        values = []
        for k in (0, 2):
            up = cmul(high[k], high[k + 1], *shift)
            values.append(cmul(low[k] + up[0], low[k + 1] + up[1], fr, fi))
        (s_re, s_im), (m_re, m_im) = values
        for slot, value in enumerate((s_re, s_im, m_re, m_im)):
            f_scr[slot, pl.ds(n, 1), :] = jnp.sum(value, axis=0, keepdims=True)
        return 0

    lax.fori_loop(0, nstate, one, 0, unroll=2)
    a, b, z_re, z_im, one_re, one_im, far_re, far_im, den_re, den_im, inv, g_re, g_im = (
        term_ref[slot] for slot in range(TERMS)
    )
    f0, f1 = (f_scr[0], f_scr[1]), (f_scr[2], f_scr[3])
    gf_re, gf_im = cmul(g_re, g_im, *f0)
    dw_scr[0:nstate] = gf_re
    dw_scr[nstate:] = -gf_im
    inv_one = 1.0 / (one_re * one_re + one_im * one_im)
    near_re, near_im = cmul(z_re, z_im, one_re * inv_one, -one_im * inv_one)
    far_re, far_im = cmul(far_re, far_im, den_re * inv, -den_im * inv)
    q_re, q_im = cmul(length * far_re - near_re, length * far_im - near_im, *f0)
    c_re, c_im = cmul(w_ref[0:nstate], w_ref[nstate:], g_re, g_im)
    y_re, y_im = cmul(c_re, c_im, q_re + f1[0], q_im + f1[1])
    by_a = a * y_re
    by_step = by_a - b * y_im
    step = jnp.exp(dvec_ref[2:3])
    by_imag = -step * y_im
    d_step = jnp.sum(by_step, axis=0, keepdims=True)
    lane, state = iota((nstate, lanes), 1), iota((nstate, lanes), 0)
    col_a = jnp.sum(by_a, axis=1, keepdims=True)
    col_b = jnp.sum(by_imag, axis=1, keepdims=True)
    grid = jnp.where(lane == state % per, col_a, jnp.where(lane == state % per + per, col_b, 0.0))
    rates = exact_dot((iota((ndp, nstate), 0) == iota((ndp, nstate), 1) // per).astype(f32), grid)
    vecs = (d_step, dk_scr[0:1], dvec_ref[0:1], dvec_ref[1:2])
    group = iota((1, LANES), 1) // sub
    cols = dlb_ref.shape[1] // ndp
    for i in range(ndp):
        main = jnp.zeros((height, LANES), f32)
        row = jnp.zeros((1, LANES), f32)
        for u in range(groups):
            main = jnp.where(group == u, moved(dw_scr[u * height : (u + 1) * height], (u - i) * sub), main)
            if u < 4:
                row = jnp.where(group == u, moved(jnp.broadcast_to(vecs[u], (8, LANES)), (u - i) * sub)[0:1], row)
        o_ref[i] = jnp.zeros(o_ref.shape[1:], f32)
        o_ref[i, 0:height] = main
        o_ref[i, height : height + 1] = row
        o_ref[i, height + 1 : height + 2] = rates[i : i + 1]
        o_ref[i, height + 2 : height + 3, 0:cols] = dlb_ref[:, i * cols : (i + 1) * cols]


def sum_kernel(x_ref, o_ref):
    total = x_ref[0].astype(f32)
    for i in range(1, x_ref.shape[0]):
        total = total + x_ref[i].astype(f32)
    o_ref[...] = total.astype(o_ref.dtype)


def last_kernel(sub, rows, *refs):
    *parts, w_ref, step_ref, skip_ref, gain_ref, bias_ref, lam_ref, imag_ref, lb_ref, dw_ref = refs
    n_w, own = w_ref.shape
    nseq = LANES * own // sub // LANES
    parts, dws = parts[:nseq], parts[nseq:]
    groups = LANES // sub
    height = n_w // groups
    per, cols = lam_ref.shape[1], lb_ref.shape[1]
    group = iota((1, LANES), 1) // sub
    me = lax.axis_index("seq")
    small = [part[0:rows] for part in parts]
    for u in range(groups):
        acc = jnp.zeros((rows, LANES), f32)
        for d, value in enumerate(small):
            c = me ^ d
            acc = jnp.where(group == c, pltpu.roll(value, (c - u) * sub + LANES, 1), acc)
        w_ref[u * height : (u + 1) * height] = acc[0:height, 0:own]
        if u < 4:
            (step_ref, skip_ref, gain_ref, bias_ref)[u][...] = acc[height : height + 1, 0:own]
    total = sum(small[1:], small[0])
    lam_ref[...] = total[height + 1 : height + 2, 0:per]
    imag_ref[...] = pltpu.roll(total, LANES - per, 1)[height + 1 : height + 2, 0:per]
    lb_ref[...] = total[height + 2 : height + 3, 0:cols]
    for d in range(nseq):
        part_ref, first = (dws[d], 0) if dws else (parts[d], rows)
        c = me ^ d
        for i in range((part_ref.shape[0] - first) // sub):
            at = pl.multiple_of((i * nseq + c) * sub, sub)
            dw_ref[pl.ds(at, sub)] = part_ref[first + i * sub : first + (i + 1) * sub]


def swap(x, axis, by):
    n = lax.axis_size(axis)
    return jax.tree.map(lambda v: lax.ppermute(v, axis, [(i, i ^ by) for i in range(n)]), x)


def trade(parts, axis):
    return [parts[0]] + [swap(parts[d], axis, d) for d in range(1, len(parts))]


def tie(*values):
    return lax.optimization_barrier(values)


def on_device(block_in, cotangent, ln_gain, ln_bias, lambda_log, lambda_imag, dss_weight, log_step, skip_gain,
              lin_weight, lin_bias, doc_lengths):
    ndp, nseq = lax.axis_size("dp"), lax.axis_size("seq")
    count, block, width = block_in.shape
    length = block * nseq
    own = ln_gain.shape[0]
    sub = own // nseq
    wide = width // nseq
    per = lambda_log.shape[0]
    nstate = per * ndp
    n_w = 2 * nstate
    cols = lin_weight.shape[1]
    tokens = count * block
    height = n_w * sub // LANES
    rows = height + 8
    steps = [1 << k for k in reversed(range(ndp.bit_length() - 1))]
    masks = [0]
    for step in steps:
        masks += [mask ^ step for mask in masks]

    def row(v):
        return v.reshape(1, -1)

    packed = call(partial(pack_kernel, sub), shape((1, rows, LANES)), [VM] * 8, name="pack", mib=60, us=2)(
        dss_weight.reshape(n_w, own), row(log_step), row(skip_gain), row(ln_gain), row(ln_bias),
        row(lambda_log), row(lambda_imag), row(lin_bias)
    )

    piece = shape((count, block, wide), bf16)
    shared, shared_parts = packed, [packed]
    w_slots = [lin_weight[None]]
    f_table, ft_table = dft_tables(block)
    w_more = hats = None
    for number, step in enumerate(steps):
        more = swap(shared, "dp", step)
        if number == 0:
            x_late, _ = tie(block_in, shared)
            hats = call(
                partial(spread_kernel, own, sub), [shape((count, block + STAT_ROWS, wide), bf16)] * nseq, [AN],
                scratch=[pltpu.VMEM((count, block, width), bf16), DMA((count,))], name="spread", us=2,
            )(x_late)
            more, *_ = tie(more, *hats)
        if number == 1:
            hats = trade(hats, "seq")
            more, _ = tie(more, hats[1])
        if number == 2:
            w_more = swap(w_slots[0], "dp", steps[0])
        shared_parts.append(more)
        if number < len(steps) - 1:
            shared = jnp.concatenate([shared, more], axis=0)

    spec = (nseq, 2 * block, wide)
    kh, vec, w_all, terms, pows = call(
        partial(lag_kernel, sub, length, masks, len(shared_parts)),
        [shape(spec), shape((8, wide)), shape((n_w, wide)), shape((TERMS, nstate, wide)),
         shape((2 * len(POWERS), nstate, wide))],
        [VM] * (len(shared_parts) + 1),
        scratch=[pltpu.VMEM((length, wide), f32), pltpu.VMEM((2, nstate, wide), f32),
                 pltpu.VMEM((3 * block, nseq * wide), bf16), pltpu.VMEM((2 * block, nseq * wide), f32)],
        name="lag_kernel", us=0, keep=[ft_table, block_in, cotangent],
    )(*shared_parts, f_table)

    kh, w_more = tie(kh, w_more)
    w_late = jnp.concatenate([w_slots[0], w_more], axis=0)
    ahead = steps[1:]
    if len(ahead) == 2:
        w_slots = [w_late, swap(w_late, "dp", ahead[0]), swap(w_late, "dp", ahead[1])]
    else:
        w_slots = [w_late]
        for step in ahead:
            w_slots = [jnp.concatenate(w_slots + [swap(slot, "dp", step) for slot in w_slots], axis=0)]

    blocks4 = (count, nseq, block, wide)
    items = nseq + doc_lengths.shape[1] - 1
    lens = pltpu.SMEM(doc_lengths.shape, i32)
    cuts = pltpu.SMEM((count, items + 1), i32)
    across = items * count * wide
    *convs, spectra_u, x_blocks = call(
        conv_kernel, [piece] * nseq + [shape((2 * block, across)), shape(blocks4)],
        [VM] * nseq + [AN] + [VM] * 4,
        scratch=[lens, cuts, pltpu.VMEM((3 * block, across), bf16), pltpu.VMEM((2 * block, across), f32),
                 pltpu.VMEM((6 * block, across), bf16), pltpu.VMEM(blocks4, f32), DMA],
        name="doc_conv", mib=20, us=7, keep=[w_all, terms, pows, block_in, cotangent],
    )(*hats, doc_lengths, vec, kh, f_table, ft_table)
    keep = [w_all, terms, pows, vec, kh, f_table, ft_table, spectra_u, x_blocks]
    if len(ahead) == 2:
        *convs, w_slots[1], w_slots[2] = tie(*convs, w_slots[1], w_slots[2])
    convs = trade(convs, "seq")
    if len(ahead) == 2:
        w_slots.append(swap(w_slots[1], "dp", ahead[1]))
    pows_late, _ = tie(pows, convs[1])
    far = call(power_kernel, shape((2 * DOCMAX // PAIR, nstate, wide)), [VM], name="state_powers", mib=16, us=1, keep=keep)(pows_late)
    convs[2], _ = tie(convs[2], far)
    keep.append(far)
    if cols % LANES == 0 and sub % 16 == 0:
        shared = jnp.concatenate([shared, shared_parts[-1]], axis=0)
        shared, convs[1] = tie(shared, convs[1])
        w_lin, bias_full = call(
            partial(rows_kernel, sub, nseq, masks), [shape((width, 2 * width), bf16), shape((1, 2 * width))],
            [VM] * (1 + len(w_slots)), name="linear_rows", us=1, keep=keep,
        )(shared, *w_slots)
    else:
        shared = jnp.concatenate([shared, shared_parts[-1]], axis=0)
        place = jnp.asarray([masks.index(i) for i in range(ndp)])[lax.axis_index("dp") ^ jnp.arange(ndp)]
        w_lin = jnp.take(jnp.concatenate(w_slots, axis=0), place, axis=0)
        w_lin = w_lin.reshape(ndp, ndp, nseq, sub, cols).transpose(2, 1, 3, 0, 4).reshape(width, 2 * width)
        bias_full = jnp.take(shared[:, height + 2, :cols], place, axis=0).reshape(1, 2 * width)

    group = shape((2, wide, 2 * width), bf16)
    block_out, d_lin_bias, *d_convs, stay, send = call(
        dense_kernel,
        [shape((count, block, width), bf16), shape((1, 2 * width))] + [piece] * nseq + [group] * 2,
        [VM] * nseq + [AN, AN, VM, VM],
        scratch=[pltpu.VMEM((count, block, width), bf16), pltpu.VMEM((count, block, width), bf16),
                 pltpu.VMEM((tokens, width), bf16), pltpu.VMEM((tokens, 2 * width), bf16),
                 pltpu.VMEM((block, width), f32), pltpu.VMEM((block, 2 * width), f32), pltpu.VMEM((block, width), f32), DMA((2,))],
        name="gated_linear", mib=16, us=5, keep=keep,
    )(*convs, block_in, cotangent, w_lin, bias_full)
    d_convs = trade(d_convs, "seq")

    staged = cols % LANES == 0
    if staged:
        stay, send = call(
            halve_kernel, [shape((1, wide, 2 * width), bf16)] * 2, [VM, VM], name="weight_half", keep=keep
        )(stay, swap(send, "seq", 1))
        d_convs[2], *_ = tie(d_convs[2], send)
        dw_other = swap(send, "seq", 2)
    else:
        full = jnp.stack([stay[0], send[0], stay[1], send[1]])
        full = full.reshape(nseq, wide, ndp, cols).transpose(2, 0, 1, 3)
        dw_own = jnp.sum(lax.all_to_all(full, "dp", 0, 0, tiled=True).astype(f32), axis=0)
        dw_own = sum(trade([dw_own[d] for d in range(nseq)], "seq"))

    out = call(
        back_kernel, [piece] * nseq + [shape(spec), shape((3, wide))],
        [VM] * (nseq + 1) + [AN] + [VM] * 5,
        scratch=[lens, cuts, pltpu.VMEM(blocks4, bf16), pltpu.VMEM((block, across), bf16),
                 pltpu.VMEM((2 * block, across), f32), pltpu.VMEM((2 * block, across), f32),
                 pltpu.VMEM((4 * block, across), bf16), pltpu.VMEM(blocks4, f32), DMA],
        name="doc_conv_grad", mib=24, us=8, keep=[w_all, terms, pows, far],
    )(*d_convs, x_blocks, doc_lengths, spectra_u, vec, kh, f_table, ft_table)
    g_own, dkh, d_norm = out[:nseq], out[nseq], out[nseq + 1]
    if staged:
        stay, send = call(
            deal_kernel, [shape((ndp // 2, wide, cols))] * 2, [VM, VM], name="weight_deal", us=1, keep=[w_all, terms, pows, far]
        )(stay, dw_other)
        dkh, *_ = tie(dkh, send)
        dw_other = swap(send, "dp", 1)

    small = call(
        partial(state_grad_kernel, sub, length), shape((ndp, rows, LANES)), [VM] * 8,
        scratch=[pltpu.VMEM((length, wide), f32), pltpu.VMEM((4, nstate, wide), f32), pltpu.VMEM((n_w, wide), f32),
                 pltpu.VMEM((6 * block, nseq * wide), bf16)],
        name="state_grad", mib=10, us=10,
    )(w_all, terms, pows, far, dkh, d_norm, d_lin_bias, ft_table)
    small, *g_own = tie(small, *g_own)
    if staged:
        small, dw_other = tie(small, dw_other)
    small = lax.all_to_all(small, "dp", 0, 0, tiled=True)
    gs = trade(g_own, "seq")
    if staged:
        step = 2
        while step < ndp:
            stay, send = call(
                halve_kernel, [shape((ndp // 2 // step, wide, cols))] * 2, [VM, VM], name="weight_half"
            )(stay, dw_other)
            dw_other = swap(send, "dp", step)
            step *= 2
    grad_in = call(
        partial(ln_back_kernel, own, sub), shape((count, block, width), bf16), [VM] * (nseq + 2),
        name="layer_norm_grad", mib=12,
    )(*gs, block_in, cotangent)
    if staged:
        merged = call(merge_kernel, shape((rows + wide, cols)), [VM] * 3, name="last_sums", us=0.5)(small, stay, dw_other)
        merged = trade([merged] * nseq, "seq")
        smalls, dws = merged, []
    else:
        small = call(sum_kernel, shape((rows, LANES)), [VM], name="small_sum", us=0.5)(small)
        smalls, dws = trade([small] * nseq, "seq"), trade([dw_own] * nseq, "seq")
    d_w, d_step, d_skip, d_gain, d_bias, d_lam, d_imag, d_lb, dw = call(
        partial(last_kernel, sub, rows),
        [shape((n_w, own))] + [shape((1, own))] * 4 + [shape((1, per))] * 2 + [shape((1, cols)), shape((width, cols))],
        [VM] * (len(smalls) + len(dws)), name="last", us=1,
    )(*smalls, *dws)
    return (
        block_out, grad_in, d_gain.reshape(own), d_bias.reshape(own), d_lam.reshape(per), d_imag.reshape(per),
        d_w.reshape(2, nstate, own), d_step.reshape(own), d_skip.reshape(own), dw, d_lb.reshape(cols),
    )


def solution(mesh):
    placed = (
        P("dp", "seq", None), P("dp", "seq", None), P("dp"), P("dp"), P("dp"), P("dp"),
        P(None, None, "dp"), P("dp"), P("dp"), P(None, "dp"), P("dp"), P("dp", None),
    )
    return jax.shard_map(
        on_device,
        mesh=mesh,
        in_specs=placed,
        out_specs=(
            P("dp", "seq", None), P("dp", "seq", None), P("dp"), P("dp"), P("dp"), P("dp"),
            P(None, None, "dp"), P("dp"), P("dp"), P(None, "dp"), P("dp"),
        ),
        check_vma=False,
    )
```

```python
from functools import partial

import jax
import jax.numpy as jnp
import numpy as np
from jax import lax
from jax.experimental import pallas as pl
from jax.experimental.pallas import tpu as pltpu
from jax.sharding import PartitionSpec as P

f32, bf16, i32 = jnp.float32, jnp.bfloat16, jnp.int32
ln_eps = 1e-05
DOCMAX = 800
FINE = 8
COARSE = 10
LANES = 128
NN = (((1,), (0,)), ((), ()))
NT = (((1,), (1,)), ((), ()))
TN = (((0,), (0,)), ((), ()))
VM = pl.BlockSpec(memory_space=pltpu.VMEM)
AN = pl.BlockSpec(memory_space=pl.ANY)
DMA = pltpu.SemaphoreType.DMA


def dot(a, b, dims=NN):
    return lax.dot_general(a, b, dims, preferred_element_type=f32)


def exact_dot(a, b, dims=NN):
    return lax.dot_general(a, b, dims, precision=lax.Precision.HIGHEST, preferred_element_type=f32)


def shape(dims, dtype=f32):
    return jax.ShapeDtypeStruct(dims, dtype)


def call(body, out, specs, scratch=(), name=None, mib=8, outs=None, us=0, keep=()):
    inputs, kept = len(specs), len(keep)

    def whole(*refs):
        body(*refs[:inputs], *refs[inputs + kept :])

    kernel = pl.pallas_call(
        whole,
        out_shape=out,
        in_specs=list(specs) + [AN] * kept,
        out_specs=outs if outs is not None else jax.tree.map(lambda _: VM, out),
        scratch_shapes=list(scratch),
        cost_estimate=pl.CostEstimate(flops=int(us * 1.15e9), bytes_accessed=1000, transcendentals=0),
        compiler_params=pltpu.CompilerParams(vmem_limit_bytes=mib * 2**20),
        name=name,
    )
    return lambda *args: kernel(*args, *keep)


def iota(dims, axis):
    return lax.broadcasted_iota(i32, dims, axis)


def cmul(ar, ai, br, bi):
    return ar * br - ai * bi, ar * bi + ai * br


def small_expm1(a):
    poly = jnp.full_like(a, 1.0)
    for k in range(9, 1, -1):
        poly = 1.0 + poly * a * (1.0 / k)
    return jnp.where(jnp.abs(a) < 0.5, a * poly, jnp.exp(a) - 1.0)


def state_terms(rate_log, freq, step_log, length):
    step = jnp.exp(step_log)
    a = -jnp.exp(rate_log) * step
    b = freq * step
    half = jnp.sin(0.5 * b)
    cos_b, sin_b, mag = jnp.cos(b), jnp.sin(b), jnp.exp(a)
    one_re = 2.0 * half * half - small_expm1(a) * cos_b
    one_im = -mag * sin_b
    far = jnp.exp(length * a)
    far_re, far_im = far * jnp.cos(length * b), far * jnp.sin(length * b)
    den_re, den_im = 1.0 - far_re, -far_im
    inv = 1.0 / (den_re * den_re + den_im * den_im)
    g_re = (one_re * den_re + one_im * den_im) * inv
    g_im = (one_im * den_re - one_re * den_im) * inv
    return a, b, mag * cos_b, mag * sin_b, one_re, one_im, far_re, far_im, den_re, den_im, inv, g_re, g_im


TERMS = 13


POWERS = (1, 2, 4) + tuple(8 * v for v in range(1, COARSE + 1))


def power_table(zr, zi):
    table = {1: (zr, zi)}
    for p in POWERS[1:]:
        at = p // 16 * 8 if p > 8 else p // 2
        table[p] = cmul(*table[at], *table[p - at])
    return [table[p] for p in POWERS]


def wide_row(ref, p, half, n):
    return jnp.broadcast_to(ref[2 * POWERS.index(p) + half, pl.ds(n, 1), :], (8, LANES))


def rows8(ref, n):
    at = iota((8, LANES), 0)
    total = None
    for p in (1, 2, 4):
        here = at & p > 0
        one = jnp.where(here, wide_row(ref, p, 0, n), 1.0), jnp.where(here, wide_row(ref, p, 1, n), 0.0)
        total = one if total is None else cmul(*total, *one)
    return total


def powers(ref, n):
    return [None] + [(wide_row(ref, 8 * v, 0, n), wide_row(ref, 8 * v, 1, n)) for v in range(1, COARSE + 1)]


def halves(x):
    hi = x.astype(bf16)
    return hi, (x - hi.astype(f32)).astype(bf16)


def stack3(ref, cols, x):
    height = x.shape[0]
    hi, lo = halves(x)
    ref[0:height, cols] = hi
    ref[height : 2 * height, cols] = lo
    ref[2 * height : 3 * height, cols] = hi


def signs(block, lanes):
    return jnp.where(iota((block, lanes), 0) & 1 > 0, -1.0, 1.0)


def dft_tables(block):
    k, j = np.arange(block)[:, None], np.arange(block)[None, :]
    theta = np.pi * (((2 * k + 1) * j) % (4 * block)) / (2 * block)
    full = np.concatenate([np.cos(theta), -np.sin(theta)], axis=0)
    high = full.astype(jnp.bfloat16)
    low = (full - high.astype(np.float64)).astype(jnp.bfloat16)
    return (jnp.asarray(np.concatenate([high, high, low], axis=1)),
            jnp.asarray(np.concatenate([high.T, high.T, low.T], axis=1)))


def moved(x, by):
    return x if by % LANES == 0 else pltpu.roll(x, by % LANES, 1)


def pack_kernel(sub, w_ref, step_ref, skip_ref, gain_ref, bias_ref, lam_ref, imag_ref, lb_ref, o_ref):
    own, per, cols = step_ref.shape[1], lam_ref.shape[1], lb_ref.shape[1]
    groups = LANES // sub
    height = w_ref.shape[0] // groups
    pick = (iota((own, LANES), 0) == lax.axis_index("seq") * sub + iota((own, LANES), 1) % sub).astype(f32)
    w = exact_dot(w_ref[...], pick)
    vec = exact_dot(jnp.concatenate([step_ref[...], skip_ref[...], gain_ref[...], bias_ref[...]] * 2, axis=0), pick)
    group = iota((1, LANES), 1) // sub
    main = jnp.zeros((height, LANES), f32)
    row = jnp.zeros((1, LANES), f32)
    for u in range(groups):
        main = jnp.where(group == u, w[u * height : (u + 1) * height], main)
        if u < 4:
            row = jnp.where(group == u, vec[u : u + 1], row)
    spot, lane = iota((per, LANES), 0), iota((per, LANES), 1)
    rates = exact_dot(jnp.broadcast_to(lam_ref[...], (8, per)), (lane == spot).astype(f32)) + exact_dot(
        jnp.broadcast_to(imag_ref[...], (8, per)), (lane == spot + per).astype(f32)
    )
    o_ref[...] = jnp.zeros(o_ref.shape, f32)
    o_ref[0, 0:height] = main
    o_ref[0, height : height + 1] = row
    o_ref[0, height + 1 : height + 2] = rates[0:1]
    o_ref[0, height + 2 : height + 3, 0:cols] = lb_ref[...]


def lag_kernel(sub, length, masks, n_parts, *refs):
    pieces, refs = refs[:n_parts], refs[n_parts:]
    f_ref, kh_ref, vec_ref, w_ref, term_ref, pow_ref, k_scr, z_scr, rhs_scr, kf_scr = refs
    slots = [piece.at[t] for piece in pieces for t in range(piece.shape[0])]
    ndp = len(slots)
    me = lax.axis_index("dp")
    n_w, lanes = w_ref.shape
    nstate = n_w // 2
    per = nstate // ndp
    groups = LANES // sub
    height = n_w // groups
    block = f_ref.shape[0] // 2
    group = iota((1, LANES), 1) // sub
    for u in range(groups):
        acc = jnp.zeros(slots[0].shape, f32)
        for t in range(ndp):
            i = me ^ masks[t]
            acc = jnp.where(group == i, pltpu.roll(slots[t][...], (i - u) * sub + LANES * ndp, 1), acc)
        w_ref[u * height : (u + 1) * height] = acc[0:height]
        if u < 4:
            vec_ref[u : u + 1] = acc[height : height + 1]
    vec_ref[4:8] = jnp.zeros((4, lanes), f32)
    rows = jnp.concatenate([slot[height + 1 : height + 2] for slot in slots], axis=0)
    source = jnp.zeros((nstate, ndp), i32)
    for t in range(ndp):
        source = jnp.where(iota((nstate, ndp), 1) == t, me ^ masks[t], source)
    spread = exact_dot((iota((nstate, ndp), 0) // per == source).astype(f32), rows)
    lane, state = iota((nstate, lanes), 1), iota((nstate, lanes), 0)
    lam = jnp.sum(jnp.where(lane == state % per, spread, 0.0), axis=1, keepdims=True)
    imag = jnp.sum(jnp.where(lane == state % per + per, spread, 0.0), axis=1, keepdims=True)
    terms = state_terms(lam, imag, vec_ref[0:1], float(length))
    for slot, value in enumerate(terms):
        term_ref[slot] = value
    z_scr[0], z_scr[1] = cmul(w_ref[0:nstate], w_ref[nstate:], terms[11], terms[12])
    for slot, pair in enumerate(power_table(terms[2], terms[3])):
        pow_ref[2 * slot], pow_ref[2 * slot + 1] = pair
    k_scr[...] = jnp.zeros_like(k_scr)

    def pair(m, _):
        ready = []
        for n in (2 * m, 2 * m + 1):
            fr, fi = rows8(pow_ref, n)
            cr = jnp.broadcast_to(z_scr[0, pl.ds(n, 1), :], (8, lanes))
            ci = jnp.broadcast_to(z_scr[1, pl.ds(n, 1), :], (8, lanes))
            ready.append([cmul(fr, fi, cr, ci), powers(pow_ref, n)])
        for u in range(DOCMAX // FINE // COARSE):
            for v in range(COARSE):
                at = (u * COARSE + v) * FINE
                total = k_scr[at : at + FINE]
                for (xr, xi), pows in ready:
                    total = total + (xr * pows[v][0] - xi * pows[v][1] if v else xr)
                k_scr[at : at + FINE] = total
            for one in ready:
                one[0] = cmul(*one[0], *one[1][COARSE])
        return 0

    lax.fori_loop(0, nstate // 2, pair, 0)
    k_scr[0:1] += vec_ref[1:2]
    parts = length // block
    for p in range(parts):
        stack3(rhs_scr, slice(p * lanes, (p + 1) * lanes), k_scr[p * block : (p + 1) * block])
    kf_scr[...] = dot(f_ref[...], rhs_scr[...])
    sign = signs(block, lanes)
    for p in range(parts):
        here, past = slice(p * lanes, (p + 1) * lanes), slice((p - 1) * lanes, p * lanes)
        re, im = kf_scr[:block, here], kf_scr[block:, here]
        if p:
            re = re - sign * kf_scr[block:, past]
            im = im + sign * kf_scr[:block, past]
        kh_ref[p, :block] = re * (1.0 / block)
        kh_ref[p, block:] = im * (1.0 / block)


def members(own, sub, c, width, wide):
    lane = iota((1, wide), 1)
    return (iota((width, wide), 0) == (lane // sub) * own + c * sub + lane % sub).astype(f32).astype(bf16)


STAT_ROWS = 16


def terms3(x):
    hi, rest = x.astype(bf16), x
    out = [hi]
    for _ in range(2):
        rest = rest - out[-1].astype(f32)
        out.append(rest.astype(bf16))
    return out


def spread_kernel(own, sub, x_any, *refs):
    *o_refs, x_ref, sems = refs
    count, block, width = x_ref.shape
    wide = o_refs[0].shape[-1]
    copies = [pltpu.make_async_copy(x_any.at[s], x_ref.at[s], sems.at[s]) for s in range(count)]
    for copy in copies:
        copy.start()
    places = [members(own, sub, lax.axis_index("seq") ^ d, width, wide) for d in range(len(o_refs))]
    eye = (iota((block, block), 0) == iota((block, block), 1)).astype(f32).astype(bf16)
    lane = iota((block, LANES), 1)
    for s in range(count):
        copies[s].wait()
        for o_ref, cols in zip(o_refs, places):
            o_ref[s, 0:block] = dot(x_ref[s], cols).astype(bf16)
        x = x_ref[s].astype(f32)
        mean = jnp.mean(x, axis=-1, keepdims=True)
        centre = x - mean
        inv = lax.rsqrt(jnp.mean(centre * centre, axis=-1, keepdims=True) + ln_eps)
        table = jnp.zeros((block, LANES), f32)
        for k, term in enumerate(terms3(mean) + terms3(inv)):
            table = jnp.where(lane == k, term.astype(f32), table)
        turned = dot(table.astype(bf16), eye, TN)
        both = jnp.concatenate([turned[0:8, 0:LANES], turned[0:8, LANES:]], axis=0).astype(bf16)
        for o_ref in o_refs:
            o_ref[s, block:] = both


def normal_inputs(piece_ref, s, block):
    stats = piece_ref[s, block:]
    spot, lane = iota((STAT_ROWS, 4 * LANES), 0), iota((STAT_ROWS, 4 * LANES), 1) // LANES
    first = lane // 2 * 8 + lane % 2 * 3
    pick = ((spot >= first) & (spot < first + 3)).astype(f32).astype(bf16)
    cols = dot(stats, pick, TN)
    parts = []
    for half in (0, 1):
        rows = piece_ref[s, half * LANES : (half + 1) * LANES].astype(f32)
        at = 2 * half * LANES
        parts.append((rows - cols[:, at : at + LANES]) * cols[:, at + LANES : at + 2 * LANES])
    return jnp.concatenate(parts, axis=0)


def ln_back_kernel(own, sub, g0, g1, g2, g3, x_ref, c_ref, o_ref):
    count, block, width = x_ref.shape
    wide = g0.shape[-1]
    tokens = count * block
    g = jnp.zeros((tokens, width), f32)
    for d, g_ref in enumerate((g0, g1, g2, g3)):
        cols = members(own, sub, lax.axis_index("seq") ^ d, width, wide)
        g = g + dot(g_ref[...].reshape(tokens, wide), cols, NT)
    x = x_ref[...].astype(f32).reshape(tokens, width)
    centre = x - jnp.mean(x, axis=-1, keepdims=True)
    inv = lax.rsqrt(jnp.mean(centre * centre, axis=-1, keepdims=True) + ln_eps)
    hat = centre * inv
    mean_g = jnp.mean(g, axis=-1, keepdims=True)
    mean_gx = jnp.mean(g * hat, axis=-1, keepdims=True)
    cot = c_ref[...].astype(f32).reshape(tokens, width)
    o_ref[...] = (cot + inv * (g - mean_g - hat * mean_gx)).astype(bf16).reshape(o_ref.shape)


def segments(len_ref, cut_ref, block, parts):
    count, docs = len_ref.shape
    last = parts + docs - 1
    for s in range(count):
        ends = []
        for d in range(docs - 1):
            ends.append(len_ref[s, d] + (ends[-1] if ends else 0))
        cut_ref[s, 0] = 0
        cut_ref[s, last] = parts * block
        for d, end in enumerate(ends):
            rank = 1 + d
            for k in range(1, parts):
                rank = rank + jnp.where(end > k * block, 1, 0)
            cut_ref[s, rank] = end
        for k in range(1, parts):
            rank = k
            for end in ends:
                rank = rank + jnp.where(end <= k * block, 1, 0)
            cut_ref[s, rank] = k * block


def document(len_ref, s, at):
    start, end, total = 0, 0, 0
    for d in range(len_ref.shape[1]):
        total = total + len_ref[s, d]
        start = jnp.where(total <= at, total, start)
    total = 0
    end = 1 << 30
    for d in range(len_ref.shape[1]):
        total = total + len_ref[s, d]
        end = jnp.minimum(end, jnp.where(total > at, total, 1 << 30))
    return start, end


def within(cut_ref, s, j, block, lanes):
    start, end = cut_ref[s, j], cut_ref[s, j + 1]
    b = start // block
    rows = b * block + iota((block, lanes), 0)
    return b, (rows >= start) & (rows < end)


def column(j, s, count, lanes):
    return pl.ds(pl.multiple_of((j * count + s) * lanes, lanes), lanes)


CHUNK = 64


def lengths_in(len_ref, len_scr, sem):
    copy = pltpu.make_async_copy(len_ref, len_scr, sem)
    copy.start()
    copy.wait()


def split_rows(y_scr, rows, cols, value, block, half):
    hi, lo = halves(value)
    for third, part in enumerate((hi, lo, hi)[: y_scr.shape[0] // (2 * block)]):
        at = (2 * third + half) * block
        y_scr[at + rows.start : at + rows.stop, cols] = part


def row_chunks(block):
    for r in range(0, block, CHUNK):
        yield slice(r, r + CHUNK), slice(block + r, block + r + CHUNK)


def conv_kernel(x0, x1, x2, x3, len_ref, vec_ref, kh_ref, f_ref, ft_ref,
                o0, o1, o2, o3, s_scr, x_scr, len_scr, cut_ref, rhs_scr, acc_scr, y_scr, out_scr, sem):
    count, parts, block, lanes = x_scr.shape
    me = lax.axis_index("seq")
    lengths_in(len_ref, len_scr, sem)
    for d, x_ref in enumerate((x0, x1, x2, x3)):
        for s in range(count):
            x_scr[s, me ^ d] = normal_inputs(x_ref, s, block)
    segments(len_scr, cut_ref, block, parts)
    gain, bias = vec_ref[2:3], vec_ref[3:4]
    items = cut_ref.shape[1] - 1
    for j in range(items):
        for s in range(count):
            b, keep = within(cut_ref, s, j, block, lanes)
            cols = slice((j * count + s) * lanes, (j * count + s + 1) * lanes)
            stack3(rhs_scr, cols, jnp.where(keep, x_scr[s, b] * gain + bias, 0.0))
        tile = slice(j * count * lanes, (j + 1) * count * lanes)
        s_scr[:, tile] = dot(f_ref[...], rhs_scr[:, tile])

    def own(j, _):
        for s in range(count):
            cols = column(j, s, count, lanes)
            for re, im in row_chunks(block):
                acc_scr[re, cols], acc_scr[im, cols] = cmul(
                    kh_ref[0, re], kh_ref[0, im], s_scr[re, cols], s_scr[im, cols]
                )
            start, _ = document(len_scr, s, cut_ref[s, j])
            b = cut_ref[s, j] // block
            first = j
            for i in range(items):
                first = first - jnp.where((i < j) & (cut_ref[s, i] >= start), 1, 0)

            def add(i, _):
                p = b - cut_ref[s, i] // block
                there = column(i, s, count, lanes)
                for re, im in row_chunks(block):
                    more = cmul(kh_ref[p, re], kh_ref[p, im], s_scr[re, there], s_scr[im, there])
                    acc_scr[re, cols] += more[0]
                    acc_scr[im, cols] += more[1]
                return 0

            lax.fori_loop(first, j, add, 0)
            for re, im in row_chunks(block):
                split_rows(y_scr, re, cols, acc_scr[re, cols], block, 0)
                split_rows(y_scr, re, cols, acc_scr[im, cols], block, 1)
        return 0

    lax.fori_loop(0, items, own, 0)
    acc_scr[0:block] = dot(ft_ref[:, 0 : y_scr.shape[0]], y_scr[...])
    for j in range(items):
        for s in range(count):
            b, keep = within(cut_ref, s, j, block, lanes)
            cols = slice((j * count + s) * lanes, (j * count + s + 1) * lanes)
            out_scr[s, b] = jnp.where(keep, acc_scr[0:block, cols], out_scr[s, b])
    for d, o_ref in enumerate((o0, o1, o2, o3)):
        for s in range(count):
            o_ref[s] = out_scr[s, me ^ d].astype(bf16)


def back_kernel(c0, c1, c2, c3, x_scr, len_ref, s_scr, vec_ref, kh_ref, f_ref, ft_ref,
                g0, g1, g2, g3, dkh_ref, dvec_ref,
                len_scr, cut_ref, v_scr, rhs_scr, sv_scr, acc_scr, y_scr, du_scr, sem):
    count, block, lanes = c0.shape
    parts = kh_ref.shape[0]
    me = lax.axis_index("seq")
    lengths_in(len_ref, len_scr, sem)
    for d, c_ref in enumerate((c0, c1, c2, c3)):
        for s in range(count):
            v_scr[s, me ^ d] = c_ref[s]
    dkh_ref[...] = jnp.zeros_like(dkh_ref)
    segments(len_scr, cut_ref, block, parts)
    items = cut_ref.shape[1] - 1
    for j in range(items):
        for s in range(count):
            b, keep = within(cut_ref, s, j, block, lanes)
            v = jnp.where(keep, v_scr[s, b].astype(f32), 0.0).astype(bf16)
            cols = slice((j * count + s) * lanes, (j * count + s + 1) * lanes)
            rhs_scr[:, cols] = v
        tile = slice(j * count * lanes, (j + 1) * count * lanes)
        sv_scr[:, tile] = dot(f_ref[:, 0:block], rhs_scr[:, tile])

    def own(j, _):
        for s in range(count):
            cols = column(j, s, count, lanes)
            for re, im in row_chunks(block):
                vr, vi, ur, ui = sv_scr[re, cols], sv_scr[im, cols], s_scr[re, cols], s_scr[im, cols]
                kr, ki = kh_ref[0, re], kh_ref[0, im]
                acc_scr[re, cols] = kr * vr + ki * vi
                acc_scr[im, cols] = kr * vi - ki * vr
                dkh_ref[0, re] += vr * ur + vi * ui
                dkh_ref[0, im] += vi * ur - vr * ui
            _, end = document(len_scr, s, cut_ref[s, j])
            b = cut_ref[s, j] // block
            last = j
            for i in range(items):
                last = last + jnp.where((i > j) & (cut_ref[s, i] < end), 1, 0)

            def add(i, _):
                p = cut_ref[s, i] // block - b
                there = column(i, s, count, lanes)
                for re, im in row_chunks(block):
                    vr, vi, ur, ui = sv_scr[re, there], sv_scr[im, there], s_scr[re, cols], s_scr[im, cols]
                    kr, ki = kh_ref[p, re], kh_ref[p, im]
                    acc_scr[re, cols] += kr * vr + ki * vi
                    acc_scr[im, cols] += kr * vi - ki * vr
                    dkh_ref[p, re] += vr * ur + vi * ui
                    dkh_ref[p, im] += vi * ur - vr * ui
                return 0

            lax.fori_loop(j + 1, last + 1, add, 0)
            for re, im in row_chunks(block):
                split_rows(y_scr, re, cols, acc_scr[re, cols], block, 0)
                split_rows(y_scr, re, cols, acc_scr[im, cols], block, 1)
        return 0

    lax.fori_loop(0, items, own, 0)
    acc_scr[0:block] = dot(ft_ref[:, 0 : y_scr.shape[0]], y_scr[...])
    for j in range(items):
        for s in range(count):
            b, keep = within(cut_ref, s, j, block, lanes)
            cols = slice((j * count + s) * lanes, (j * count + s + 1) * lanes)
            du_scr[s, b] = jnp.where(keep, acc_scr[0:block, cols], du_scr[s, b])
    gain = vec_ref[2:3]
    d_gain = jnp.zeros((8, lanes), f32)
    d_bias = jnp.zeros((8, lanes), f32)
    for d, g_ref in enumerate((g0, g1, g2, g3)):
        for s in range(count):
            for r in range(0, block, CHUNK):
                du = du_scr[s, me ^ d, r : r + CHUNK]
                d_bias += jnp.sum(du.reshape(CHUNK // 8, 8, lanes), axis=0)
                d_gain += jnp.sum((du * x_scr[s, me ^ d, r : r + CHUNK]).reshape(CHUNK // 8, 8, lanes), axis=0)
                g_ref[s, r : r + CHUNK] = (du * gain).astype(bf16)
    dvec_ref[0:1] = jnp.sum(d_gain, axis=0, keepdims=True)
    dvec_ref[1:2] = jnp.sum(d_bias, axis=0, keepdims=True)
    dvec_ref[2:3] = vec_ref[0:1]


def normal_cdf(v, bell):
    t = 1.0 / (1.0 + np.float32(0.3275911 / np.sqrt(2.0)) * jnp.abs(v))
    tail = t * (0.127414796 + t * (-0.142248368 + t * (0.7107068705 + t * (-0.7265760135 + t * 0.5307027145)))) * bell
    return jnp.where(v < 0.0, tail, 1.0 - tail)


def dense_kernel(q0, q1, q2, q3, x_any, c_any, w_ref, lb_ref,
                 out_ref, dlb_ref, d0, d1, d2, d3, stay_ref, send_ref,
                 x_ref, c_ref, act_ref, dpre_ref, slope_scr, pre_scr, dact_scr, sems):
    count, block, wide = q0.shape
    width = act_ref.shape[1]
    me = lax.axis_index("seq")
    copies = [pltpu.make_async_copy(x_any, x_ref, sems.at[0]), pltpu.make_async_copy(c_any, c_ref, sems.at[1])]
    for copy in copies:
        copy.start()

    def cols_of(d):
        return pl.ds(pl.multiple_of((me ^ d) * wide, wide), wide)

    def sequence(s, lb_sum):
        def slope(r, _):
            rows = pl.ds(pl.multiple_of(r * CHUNK, CHUNK), CHUNK)
            flat = pl.ds(pl.multiple_of(s * block + r * CHUNK, CHUNK), CHUNK)
            for d, q_ref in enumerate((q0, q1, q2, q3)):
                v = q_ref[s, rows].astype(f32)
                bell = jnp.exp(-0.5 * v * v)
                cdf = normal_cdf(v, bell)
                act_ref[flat, cols_of(d)] = (v * cdf).astype(bf16)
                slope_scr[rows, cols_of(d)] = cdf + v * (bell * np.float32(1.0 / np.sqrt(2.0 * np.pi)))
            return 0

        lax.fori_loop(0, block // CHUNK, slope, 0)
        whole = pl.ds(pl.multiple_of(s * block, block), block)
        pre_scr[...] = dot(act_ref[whole, :], w_ref[...])

        @pl.when(s == 0)
        def _():
            for copy in copies:
                copy.wait()

        def gate(r, total):
            rows = pl.ds(pl.multiple_of(r * 32, 32), 32)
            flat = pl.ds(pl.multiple_of(s * block + r * 32, 32), 32)
            first = pre_scr[rows, 0:width] + lb_ref[:, 0:width]
            sig = 1.0 / (1.0 + jnp.exp(-(pre_scr[rows, width:] + lb_ref[:, width:])))
            out_ref[s, rows] = (x_ref[s, rows].astype(f32) + first * sig).astype(bf16)
            d_first = c_ref[s, rows].astype(f32) * sig
            d_second = d_first * first * (1.0 - sig)
            d_pre = jnp.concatenate([d_first, d_second], axis=1).astype(bf16)
            dpre_ref[flat, :] = d_pre
            return total + jnp.sum(d_pre.astype(f32).reshape(4, 8, 2 * width), axis=0)

        lb_sum = lax.fori_loop(0, block // 32, gate, lb_sum)
        dact_scr[...] = dot(dpre_ref[whole, :], w_ref[...], NT)
        for d, o_ref in enumerate((d0, d1, d2, d3)):
            o_ref[s] = (dact_scr[:, cols_of(d)] * slope_scr[:, cols_of(d)]).astype(bf16)
        return lb_sum

    lb_sum = lax.fori_loop(0, count, sequence, jnp.zeros((8, 2 * width), f32))
    dlb_ref[...] = jnp.sum(lb_sum, axis=0, keepdims=True)
    for d in range(4):
        (send_ref if d & 1 else stay_ref)[d // 2] = dot(act_ref[:, cols_of(d)], dpre_ref[...], TN).astype(bf16)


def rows_kernel(sub, nseq, masks, shared_ref, *refs):
    *w_refs, o_ref, lb_ref = refs
    cols = w_refs[0].shape[-1]
    span = o_ref.shape[0] // nseq
    me = lax.axis_index("dp")
    bias_row = shared_ref.shape[1] - 8 + 2
    for t, mask in enumerate(masks):
        at = pl.ds(pl.multiple_of((me ^ mask) * cols, cols), cols)
        lb_ref[:, at] = shared_ref[t, bias_row : bias_row + 1, 0:cols]
    t = 0
    for w_ref in w_refs:
        for slot in range(w_ref.shape[0]):
            at = pl.ds(pl.multiple_of((me ^ masks[t]) * cols, cols), cols)
            t += 1
            for c in range(nseq):
                for i in range(span // sub):
                    o_ref[c * span + i * sub : c * span + (i + 1) * sub, at] = w_ref[
                        slot, (i * nseq + c) * sub : (i * nseq + c + 1) * sub
                    ]


def halve_kernel(mine_ref, other_ref, stay_ref, send_ref):
    for k in range(mine_ref.shape[0]):
        total = mine_ref[k].astype(f32) + other_ref[k].astype(f32)
        (send_ref if k & 1 else stay_ref)[k // 2] = total.astype(stay_ref.dtype)


def deal_kernel(mine_ref, other_ref, stay_ref, send_ref):
    part = stay_ref.shape[2]
    me = lax.axis_index("dp")
    for d in range(2 * stay_ref.shape[0]):
        cols = pl.ds(pl.multiple_of((me ^ d) * part, part), part)
        (send_ref if d & 1 else stay_ref)[d // 2] = mine_ref[0, :, cols].astype(f32) + other_ref[0, :, cols].astype(f32)


def merge_kernel(x_ref, mine_ref, other_ref, o_ref):
    span = -(-x_ref.shape[1] // 32) * 32
    total = x_ref[0]
    for i in range(1, x_ref.shape[0]):
        total = total + x_ref[i]
    total = jnp.concatenate([total, jnp.zeros((span - total.shape[0], LANES), f32)], axis=0)
    for k, term in enumerate(terms3(total)):
        o_ref[k * span : (k + 1) * span] = term
    o_ref[3 * span :] = (mine_ref[0] + other_ref[0]).astype(bf16)


PAIR = 2 * FINE


def power_kernel(pow_ref, o_ref):
    def some(g, _):
        rows = pl.ds(pl.multiple_of(g * 8, 8), 8)
        at = [2 * POWERS.index(PAIR * v) for v in range(1, COARSE // 2 + 1)]
        small = [(pow_ref[i, rows], pow_ref[i + 1, rows]) for i in at]
        x = jnp.ones((8, LANES), f32), jnp.zeros((8, LANES), f32)
        for u in range(DOCMAX // PAIR // (COARSE // 2)):
            for v in range(COARSE // 2):
                m = u * (COARSE // 2) + v
                o_ref[2 * m, rows], o_ref[2 * m + 1, rows] = cmul(*x, *small[v - 1]) if v else x
            x = cmul(*x, *small[-1])
        return 0

    lax.fori_loop(0, pow_ref.shape[1] // 8, some, 0)


CHAINS = 2


def state_grad_kernel(sub, length, w_ref, term_ref, pow_ref, far_ref, dkh_ref, dvec_ref, dlb_ref, ft_ref, o_ref,
                      dk_scr, f_scr, dw_scr, y_scr):
    ndp = o_ref.shape[0]
    n_w, lanes = w_ref.shape
    nstate = n_w // 2
    per = nstate // ndp
    groups = LANES // sub
    height = n_w // groups
    parts, twice, _ = dkh_ref.shape
    block = twice // 2
    sign = signs(block, lanes)
    for p in range(parts):
        re, im = dkh_ref[p, :block], dkh_ref[p, block:]
        if p + 1 < parts:
            re = re + sign * dkh_ref[p + 1, block:]
            im = im - sign * dkh_ref[p + 1, :block]
        stack3(y_scr, slice(p * lanes, (p + 1) * lanes), jnp.concatenate([re, im], axis=0))
    all_lags = dot(ft_ref[...], y_scr[...]) * (1.0 / block)
    for p in range(parts):
        dk_scr[p * block : (p + 1) * block] = all_lags[:, p * lanes : (p + 1) * lanes]
    at8 = iota((8, lanes), 0).astype(f32)

    def one(n, _):
        fr, fi = rows8(pow_ref, n)
        zero = jnp.zeros((8, lanes), f32)
        span = DOCMAX // PAIR // CHAINS
        sums = []
        for c in range(CHAINS):
            acc = [[zero] * 4, [zero] * 4]
            for m in range(c * span + span - 1, c * span - 1, -1):
                if m:
                    p_re = jnp.broadcast_to(far_ref[2 * m, pl.ds(n, 1), :], (8, lanes))
                    p_im = jnp.broadcast_to(far_ref[2 * m + 1, pl.ds(n, 1), :], (8, lanes))
                for h, one_acc in enumerate(acc):
                    at = m * PAIR + h * FINE
                    dk = dk_scr[at : at + FINE]
                    one_acc[0] = one_acc[0] + (dk * p_re if m else dk)
                    if m:
                        one_acc[1] = one_acc[1] + dk * p_im
                    if m > c * span:
                        one_acc[2], one_acc[3] = one_acc[2] + one_acc[0], one_acc[3] + one_acc[1]
            for one_acc in acc:
                one_acc[2], one_acc[3] = (one_acc[2 + k] + (c * span) * one_acc[k] for k in (0, 1))
            sums.append(acc)
        low, high = (
            [sum((acc[h][k] for acc in sums[1:]), sums[0][h][k]) for k in range(4)] for h in (0, 1)
        )
        for h, part in enumerate((low, high)):
            for k in (0, 1):
                part[2 + k] = PAIR * part[2 + k] + (at8 + float(h * FINE)) * part[k]
        shift = wide_row(pow_ref, FINE, 0, n), wide_row(pow_ref, FINE, 1, n)
        values = []
        for k in (0, 2):
            up = cmul(high[k], high[k + 1], *shift)
            values.append(cmul(low[k] + up[0], low[k + 1] + up[1], fr, fi))
        (s_re, s_im), (m_re, m_im) = values
        for slot, value in enumerate((s_re, s_im, m_re, m_im)):
            f_scr[slot, pl.ds(n, 1), :] = jnp.sum(value, axis=0, keepdims=True)
        return 0

    lax.fori_loop(0, nstate, one, 0, unroll=2)
    a, b, z_re, z_im, one_re, one_im, far_re, far_im, den_re, den_im, inv, g_re, g_im = (
        term_ref[slot] for slot in range(TERMS)
    )
    f0, f1 = (f_scr[0], f_scr[1]), (f_scr[2], f_scr[3])
    gf_re, gf_im = cmul(g_re, g_im, *f0)
    dw_scr[0:nstate] = gf_re
    dw_scr[nstate:] = -gf_im
    inv_one = 1.0 / (one_re * one_re + one_im * one_im)
    near_re, near_im = cmul(z_re, z_im, one_re * inv_one, -one_im * inv_one)
    far_re, far_im = cmul(far_re, far_im, den_re * inv, -den_im * inv)
    q_re, q_im = cmul(length * far_re - near_re, length * far_im - near_im, *f0)
    c_re, c_im = cmul(w_ref[0:nstate], w_ref[nstate:], g_re, g_im)
    y_re, y_im = cmul(c_re, c_im, q_re + f1[0], q_im + f1[1])
    by_a = a * y_re
    by_step = by_a - b * y_im
    step = jnp.exp(dvec_ref[2:3])
    by_imag = -step * y_im
    d_step = jnp.sum(by_step, axis=0, keepdims=True)
    lane, state = iota((nstate, lanes), 1), iota((nstate, lanes), 0)
    col_a = jnp.sum(by_a, axis=1, keepdims=True)
    col_b = jnp.sum(by_imag, axis=1, keepdims=True)
    grid = jnp.where(lane == state % per, col_a, jnp.where(lane == state % per + per, col_b, 0.0))
    rates = exact_dot((iota((ndp, nstate), 0) == iota((ndp, nstate), 1) // per).astype(f32), grid)
    vecs = (d_step, dk_scr[0:1], dvec_ref[0:1], dvec_ref[1:2])
    group = iota((1, LANES), 1) // sub
    cols = dlb_ref.shape[1] // ndp
    for i in range(ndp):
        main = jnp.zeros((height, LANES), f32)
        row = jnp.zeros((1, LANES), f32)
        for u in range(groups):
            main = jnp.where(group == u, moved(dw_scr[u * height : (u + 1) * height], (u - i) * sub), main)
            if u < 4:
                row = jnp.where(group == u, moved(jnp.broadcast_to(vecs[u], (8, LANES)), (u - i) * sub)[0:1], row)
        o_ref[i] = jnp.zeros(o_ref.shape[1:], f32)
        o_ref[i, 0:height] = main
        o_ref[i, height : height + 1] = row
        o_ref[i, height + 1 : height + 2] = rates[i : i + 1]
        o_ref[i, height + 2 : height + 3, 0:cols] = dlb_ref[:, i * cols : (i + 1) * cols]


def sum_kernel(x_ref, o_ref):
    total = x_ref[0].astype(f32)
    for i in range(1, x_ref.shape[0]):
        total = total + x_ref[i].astype(f32)
    o_ref[...] = total.astype(o_ref.dtype)


def last_kernel(sub, rows, *refs):
    *parts, w_ref, step_ref, skip_ref, gain_ref, bias_ref, lam_ref, imag_ref, lb_ref, dw_ref = refs
    n_w, own = w_ref.shape
    nseq = LANES * own // sub // LANES
    parts, dws = parts[:nseq], parts[nseq:]
    groups = LANES // sub
    height = n_w // groups
    per, cols = lam_ref.shape[1], lb_ref.shape[1]
    group = iota((1, LANES), 1) // sub
    me = lax.axis_index("seq")
    merged = not dws
    if merged:
        span = -(-rows // 32) * 32
        small = [sum(part[k * span : k * span + rows].astype(f32) for k in range(3)) for part in parts]
    else:
        small = [part[0:rows] for part in parts]
    for u in range(groups):
        acc = jnp.zeros((rows, LANES), f32)
        for d, value in enumerate(small):
            c = me ^ d
            acc = jnp.where(group == c, pltpu.roll(value, (c - u) * sub + LANES, 1), acc)
        w_ref[u * height : (u + 1) * height] = acc[0:height, 0:own]
        if u < 4:
            (step_ref, skip_ref, gain_ref, bias_ref)[u][...] = acc[height : height + 1, 0:own]
    total = sum(small[1:], small[0])
    lam_ref[...] = total[height + 1 : height + 2, 0:per]
    imag_ref[...] = pltpu.roll(total, LANES - per, 1)[height + 1 : height + 2, 0:per]
    lb_ref[...] = total[height + 2 : height + 3, 0:cols]
    for d in range(nseq):
        part_ref, first = (parts[d], 3 * span) if merged else (dws[d], 0)
        c = me ^ d
        for i in range((part_ref.shape[0] - first) // sub):
            at = pl.multiple_of((i * nseq + c) * sub, sub)
            dw_ref[pl.ds(at, sub)] = part_ref[first + i * sub : first + (i + 1) * sub].astype(f32)


def swap(x, axis, by):
    n = lax.axis_size(axis)
    return jax.tree.map(lambda v: lax.ppermute(v, axis, [(i, i ^ by) for i in range(n)]), x)


def trade(parts, axis):
    return [parts[0]] + [swap(parts[d], axis, d) for d in range(1, len(parts))]


def tie(*values):
    return lax.optimization_barrier(values)


def on_device(block_in, cotangent, ln_gain, ln_bias, lambda_log, lambda_imag, dss_weight, log_step, skip_gain,
              lin_weight, lin_bias, doc_lengths):
    ndp, nseq = lax.axis_size("dp"), lax.axis_size("seq")
    count, block, width = block_in.shape
    length = block * nseq
    own = ln_gain.shape[0]
    sub = own // nseq
    wide = width // nseq
    per = lambda_log.shape[0]
    nstate = per * ndp
    n_w = 2 * nstate
    cols = lin_weight.shape[1]
    tokens = count * block
    height = n_w * sub // LANES
    rows = height + 8
    steps = [1 << k for k in reversed(range(ndp.bit_length() - 1))]
    masks = [0]
    for step in steps:
        masks += [mask ^ step for mask in masks]

    def row(v):
        return v.reshape(1, -1)

    packed = call(partial(pack_kernel, sub), shape((1, rows, LANES)), [VM] * 8, name="pack", mib=60, us=2)(
        dss_weight.reshape(n_w, own), row(log_step), row(skip_gain), row(ln_gain), row(ln_bias),
        row(lambda_log), row(lambda_imag), row(lin_bias)
    )

    piece = shape((count, block, wide), bf16)
    shared, shared_parts = packed, [packed]
    w_slots = [lin_weight[None]]
    f_table, ft_table = dft_tables(block)
    w_more = hats = None
    for number, step in enumerate(steps):
        more = swap(shared, "dp", step)
        if number == 0:
            x_late, _ = tie(block_in, shared)
            hats = call(
                partial(spread_kernel, own, sub), [shape((count, block + STAT_ROWS, wide), bf16)] * nseq, [AN],
                scratch=[pltpu.VMEM((count, block, width), bf16), DMA((count,))], name="spread", us=2,
            )(x_late)
            more, *_ = tie(more, *hats)
        if number == 1:
            hats = trade(hats, "seq")
            more, _ = tie(more, hats[1])
        if number == 2:
            w_more = swap(w_slots[0], "dp", steps[0])
        shared_parts.append(more)
        if number < len(steps) - 1:
            shared = jnp.concatenate([shared, more], axis=0)

    spec = (nseq, 2 * block, wide)
    kh, vec, w_all, terms, pows = call(
        partial(lag_kernel, sub, length, masks, len(shared_parts)),
        [shape(spec), shape((8, wide)), shape((n_w, wide)), shape((TERMS, nstate, wide)),
         shape((2 * len(POWERS), nstate, wide))],
        [VM] * (len(shared_parts) + 1),
        scratch=[pltpu.VMEM((length, wide), f32), pltpu.VMEM((2, nstate, wide), f32),
                 pltpu.VMEM((3 * block, nseq * wide), bf16), pltpu.VMEM((2 * block, nseq * wide), f32)],
        name="lag_kernel", us=0, keep=[ft_table, block_in, cotangent],
    )(*shared_parts, f_table)

    kh, w_more = tie(kh, w_more)
    w_late = jnp.concatenate([w_slots[0], w_more], axis=0)
    ahead = steps[1:]
    if len(ahead) == 2:
        w_slots = [w_late, swap(w_late, "dp", ahead[0]), swap(w_late, "dp", ahead[1])]
    else:
        w_slots = [w_late]
        for step in ahead:
            w_slots = [jnp.concatenate(w_slots + [swap(slot, "dp", step) for slot in w_slots], axis=0)]

    blocks4 = (count, nseq, block, wide)
    items = nseq + doc_lengths.shape[1] - 1
    lens = pltpu.SMEM(doc_lengths.shape, i32)
    cuts = pltpu.SMEM((count, items + 1), i32)
    across = items * count * wide
    *convs, spectra_u, x_blocks = call(
        conv_kernel, [piece] * nseq + [shape((2 * block, across)), shape(blocks4)],
        [VM] * nseq + [AN] + [VM] * 4,
        scratch=[lens, cuts, pltpu.VMEM((3 * block, across), bf16), pltpu.VMEM((2 * block, across), f32),
                 pltpu.VMEM((6 * block, across), bf16), pltpu.VMEM(blocks4, f32), DMA],
        name="doc_conv", mib=20, us=7, keep=[w_all, terms, pows, block_in, cotangent],
    )(*hats, doc_lengths, vec, kh, f_table, ft_table)
    keep = [w_all, terms, pows, vec, kh, f_table, ft_table, spectra_u, x_blocks]
    if len(ahead) == 2:
        *convs, w_slots[1], w_slots[2] = tie(*convs, w_slots[1], w_slots[2])
    convs = trade(convs, "seq")
    if len(ahead) == 2:
        w_slots.append(swap(w_slots[1], "dp", ahead[1]))
    pows_late, _ = tie(pows, convs[1])
    far = call(power_kernel, shape((2 * DOCMAX // PAIR, nstate, wide)), [VM], name="state_powers", mib=16, us=1, keep=keep)(pows_late)
    convs[2], _ = tie(convs[2], far)
    keep.append(far)
    if cols % LANES == 0 and sub % 16 == 0:
        shared = jnp.concatenate([shared, shared_parts[-1]], axis=0)
        shared, convs[1] = tie(shared, convs[1])
        w_lin, bias_full = call(
            partial(rows_kernel, sub, nseq, masks), [shape((width, 2 * width), bf16), shape((1, 2 * width))],
            [VM] * (1 + len(w_slots)), name="linear_rows", us=1, keep=keep,
        )(shared, *w_slots)
    else:
        shared = jnp.concatenate([shared, shared_parts[-1]], axis=0)
        place = jnp.asarray([masks.index(i) for i in range(ndp)])[lax.axis_index("dp") ^ jnp.arange(ndp)]
        w_lin = jnp.take(jnp.concatenate(w_slots, axis=0), place, axis=0)
        w_lin = w_lin.reshape(ndp, ndp, nseq, sub, cols).transpose(2, 1, 3, 0, 4).reshape(width, 2 * width)
        bias_full = jnp.take(shared[:, height + 2, :cols], place, axis=0).reshape(1, 2 * width)

    group = shape((2, wide, 2 * width), bf16)
    block_out, d_lin_bias, *d_convs, stay, send = call(
        dense_kernel,
        [shape((count, block, width), bf16), shape((1, 2 * width))] + [piece] * nseq + [group] * 2,
        [VM] * nseq + [AN, AN, VM, VM],
        scratch=[pltpu.VMEM((count, block, width), bf16), pltpu.VMEM((count, block, width), bf16),
                 pltpu.VMEM((tokens, width), bf16), pltpu.VMEM((tokens, 2 * width), bf16),
                 pltpu.VMEM((block, width), f32), pltpu.VMEM((block, 2 * width), f32), pltpu.VMEM((block, width), f32), DMA((2,))],
        name="gated_linear", mib=16, us=5, keep=keep,
    )(*convs, block_in, cotangent, w_lin, bias_full)
    d_convs = trade(d_convs, "seq")

    staged = cols % LANES == 0
    if staged:
        stay, send = call(
            halve_kernel, [shape((1, wide, 2 * width), bf16)] * 2, [VM, VM], name="weight_half", keep=keep
        )(stay, swap(send, "seq", 1))
        d_convs[2], *_ = tie(d_convs[2], send)
        dw_other = swap(send, "seq", 2)
    else:
        full = jnp.stack([stay[0], send[0], stay[1], send[1]])
        full = full.reshape(nseq, wide, ndp, cols).transpose(2, 0, 1, 3)
        dw_own = jnp.sum(lax.all_to_all(full, "dp", 0, 0, tiled=True).astype(f32), axis=0)
        dw_own = sum(trade([dw_own[d] for d in range(nseq)], "seq"))

    out = call(
        back_kernel, [piece] * nseq + [shape(spec), shape((3, wide))],
        [VM] * (nseq + 1) + [AN] + [VM] * 5,
        scratch=[lens, cuts, pltpu.VMEM(blocks4, bf16), pltpu.VMEM((block, across), bf16),
                 pltpu.VMEM((2 * block, across), f32), pltpu.VMEM((2 * block, across), f32),
                 pltpu.VMEM((4 * block, across), bf16), pltpu.VMEM(blocks4, f32), DMA],
        name="doc_conv_grad", mib=24, us=8, keep=[w_all, terms, pows, far],
    )(*d_convs, x_blocks, doc_lengths, spectra_u, vec, kh, f_table, ft_table)
    g_own, dkh, d_norm = out[:nseq], out[nseq], out[nseq + 1]
    if staged:
        stay, send = call(
            deal_kernel, [shape((ndp // 2, wide, cols))] * 2, [VM, VM], name="weight_deal", us=1, keep=[w_all, terms, pows, far]
        )(stay, dw_other)
        dkh, *_ = tie(dkh, send)
        dw_other = swap(send, "dp", 1)

    small = call(
        partial(state_grad_kernel, sub, length), shape((ndp, rows, LANES)), [VM] * 8,
        scratch=[pltpu.VMEM((length, wide), f32), pltpu.VMEM((4, nstate, wide), f32), pltpu.VMEM((n_w, wide), f32),
                 pltpu.VMEM((6 * block, nseq * wide), bf16)],
        name="state_grad", mib=10, us=10,
    )(w_all, terms, pows, far, dkh, d_norm, d_lin_bias, ft_table)
    small, *g_own = tie(small, *g_own)
    if staged:
        small, dw_other = tie(small, dw_other)
    small = lax.all_to_all(small, "dp", 0, 0, tiled=True)
    gs = trade(g_own, "seq")
    if staged:
        step = 2
        while step < ndp:
            stay, send = call(
                halve_kernel, [shape((ndp // 2 // step, wide, cols))] * 2, [VM, VM], name="weight_half"
            )(stay, dw_other)
            dw_other = swap(send, "dp", step)
            step *= 2
    grad_in = call(
        partial(ln_back_kernel, own, sub), shape((count, block, width), bf16), [VM] * (nseq + 2),
        name="layer_norm_grad", mib=12,
    )(*gs, block_in, cotangent)
    if staged:
        merged = call(merge_kernel, shape((-(-rows // 32) * 96 + wide, cols), bf16), [VM] * 3, name="last_sums", us=0.5)(small, stay, dw_other)
        merged = trade([merged] * nseq, "seq")
        smalls, dws = merged, []
    else:
        small = call(sum_kernel, shape((rows, LANES)), [VM], name="small_sum", us=0.5)(small)
        smalls, dws = trade([small] * nseq, "seq"), trade([dw_own] * nseq, "seq")
    d_w, d_step, d_skip, d_gain, d_bias, d_lam, d_imag, d_lb, dw = call(
        partial(last_kernel, sub, rows),
        [shape((n_w, own))] + [shape((1, own))] * 4 + [shape((1, per))] * 2 + [shape((1, cols)), shape((width, cols))],
        [VM] * (len(smalls) + len(dws)), name="last", us=1,
    )(*smalls, *dws)
    return (
        block_out, grad_in, d_gain.reshape(own), d_bias.reshape(own), d_lam.reshape(per), d_imag.reshape(per),
        d_w.reshape(2, nstate, own), d_step.reshape(own), d_skip.reshape(own), dw, d_lb.reshape(cols),
    )


def solution(mesh):
    placed = (
        P("dp", "seq", None), P("dp", "seq", None), P("dp"), P("dp"), P("dp"), P("dp"),
        P(None, None, "dp"), P("dp"), P("dp"), P(None, "dp"), P("dp"), P("dp", None),
    )
    return jax.shard_map(
        on_device,
        mesh=mesh,
        in_specs=placed,
        out_specs=(
            P("dp", "seq", None), P("dp", "seq", None), P("dp"), P("dp"), P("dp"), P("dp"),
            P(None, None, "dp"), P("dp"), P("dp"), P(None, "dp"), P("dp"),
        ),
        check_vma=False,
    )
```

```python
from functools import partial

import jax
import jax.numpy as jnp
import numpy as np
from jax import lax
from jax.experimental import pallas as pl
from jax.experimental.pallas import tpu as pltpu
from jax.sharding import PartitionSpec as P

f32, bf16, i32 = jnp.float32, jnp.bfloat16, jnp.int32
ln_eps = 1e-05
DOCMAX = 800
FINE = 8
COARSE = 10
LANES = 128
NN = (((1,), (0,)), ((), ()))
NT = (((1,), (1,)), ((), ()))
TN = (((0,), (0,)), ((), ()))
VM = pl.BlockSpec(memory_space=pltpu.VMEM)
AN = pl.BlockSpec(memory_space=pl.ANY)
DMA = pltpu.SemaphoreType.DMA


def dot(a, b, dims=NN):
    return lax.dot_general(a, b, dims, preferred_element_type=f32)


def exact_dot(a, b, dims=NN):
    return lax.dot_general(a, b, dims, precision=lax.Precision.HIGHEST, preferred_element_type=f32)


def shape(dims, dtype=f32):
    return jax.ShapeDtypeStruct(dims, dtype)


def call(body, out, specs, scratch=(), name=None, mib=8, outs=None, us=0, keep=()):
    inputs, kept = len(specs), len(keep)

    def whole(*refs):
        body(*refs[:inputs], *refs[inputs + kept :])

    kernel = pl.pallas_call(
        whole,
        out_shape=out,
        in_specs=list(specs) + [AN] * kept,
        out_specs=outs if outs is not None else jax.tree.map(lambda _: VM, out),
        scratch_shapes=list(scratch),
        cost_estimate=pl.CostEstimate(flops=int(us * 1.15e9), bytes_accessed=1000, transcendentals=0),
        compiler_params=pltpu.CompilerParams(vmem_limit_bytes=mib * 2**20),
        name=name,
    )
    return lambda *args: kernel(*args, *keep)


def iota(dims, axis):
    return lax.broadcasted_iota(i32, dims, axis)


def cmul(ar, ai, br, bi):
    return ar * br - ai * bi, ar * bi + ai * br


def small_expm1(a):
    poly = jnp.full_like(a, 1.0)
    for k in range(9, 1, -1):
        poly = 1.0 + poly * a * (1.0 / k)
    return jnp.where(jnp.abs(a) < 0.5, a * poly, jnp.exp(a) - 1.0)


def state_terms(rate_log, freq, step_log, length):
    step = jnp.exp(step_log)
    a = -jnp.exp(rate_log) * step
    b = freq * step
    half, other = jnp.sin(0.5 * b), jnp.cos(0.5 * b)
    cos_b, sin_b, mag = 1.0 - 2.0 * half * half, 2.0 * half * other, jnp.exp(a)
    one_re = 2.0 * half * half - small_expm1(a) * cos_b
    one_im = -mag * sin_b
    far = jnp.exp(length * a)
    far_re, far_im = far * jnp.cos(length * b), far * jnp.sin(length * b)
    den_re, den_im = 1.0 - far_re, -far_im
    inv = 1.0 / (den_re * den_re + den_im * den_im)
    g_re = (one_re * den_re + one_im * den_im) * inv
    g_im = (one_im * den_re - one_re * den_im) * inv
    return a, b, mag * cos_b, mag * sin_b, one_re, one_im, far_re, far_im, den_re, den_im, inv, g_re, g_im


TERMS = 13


POWERS = (1, 2, 4) + tuple(8 * v for v in range(1, COARSE + 1))


def power_table(zr, zi):
    table = {1: (zr, zi)}
    for p in POWERS[1:]:
        at = p // 16 * 8 if p > 8 else p // 2
        table[p] = cmul(*table[at], *table[p - at])
    return [table[p] for p in POWERS]


def wide_row(ref, p, half, n):
    return jnp.broadcast_to(ref[2 * POWERS.index(p) + half, pl.ds(n, 1), :], (8, LANES))


def rows8(ref, n):
    at = iota((8, LANES), 0)
    total = None
    for p in (1, 2, 4):
        here = at & p > 0
        one = jnp.where(here, wide_row(ref, p, 0, n), 1.0), jnp.where(here, wide_row(ref, p, 1, n), 0.0)
        total = one if total is None else cmul(*total, *one)
    return total


def powers(ref, n):
    return [None] + [(wide_row(ref, 8 * v, 0, n), wide_row(ref, 8 * v, 1, n)) for v in range(1, COARSE + 1)]


def halves(x):
    hi = x.astype(bf16)
    return hi, (x - hi.astype(f32)).astype(bf16)


def stack3(ref, cols, x):
    height = x.shape[0]
    hi, lo = halves(x)
    ref[0:height, cols] = hi
    ref[height : 2 * height, cols] = lo
    ref[2 * height : 3 * height, cols] = hi


def signs(block, lanes):
    return jnp.where(iota((block, lanes), 0) & 1 > 0, -1.0, 1.0)


def dft_tables(block):
    k, j = np.arange(block)[:, None], np.arange(block)[None, :]
    theta = np.pi * (((2 * k + 1) * j) % (4 * block)) / (2 * block)
    full = np.concatenate([np.cos(theta), -np.sin(theta)], axis=0)
    high = full.astype(jnp.bfloat16)
    low = (full - high.astype(np.float64)).astype(jnp.bfloat16)
    return (jnp.asarray(np.concatenate([high, high, low], axis=1)),
            jnp.asarray(np.concatenate([high.T, high.T, low.T], axis=1)))


def moved(x, by):
    return x if by % LANES == 0 else pltpu.roll(x, by % LANES, 1)


def pack_kernel(sub, w_ref, step_ref, skip_ref, gain_ref, bias_ref, lam_ref, imag_ref, lb_ref, o_ref):
    own, per, cols = step_ref.shape[1], lam_ref.shape[1], lb_ref.shape[1]
    groups = LANES // sub
    height = w_ref.shape[0] // groups
    pick = (iota((own, LANES), 0) == lax.axis_index("seq") * sub + iota((own, LANES), 1) % sub).astype(f32)
    w = exact_dot(w_ref[...], pick)
    vec = exact_dot(jnp.concatenate([step_ref[...], skip_ref[...], gain_ref[...], bias_ref[...]] * 2, axis=0), pick)
    group = iota((1, LANES), 1) // sub
    main = jnp.zeros((height, LANES), f32)
    row = jnp.zeros((1, LANES), f32)
    for u in range(groups):
        main = jnp.where(group == u, w[u * height : (u + 1) * height], main)
        if u < 4:
            row = jnp.where(group == u, vec[u : u + 1], row)
    spot, lane = iota((per, LANES), 0), iota((per, LANES), 1)
    rates = exact_dot(jnp.broadcast_to(lam_ref[...], (8, per)), (lane == spot).astype(f32)) + exact_dot(
        jnp.broadcast_to(imag_ref[...], (8, per)), (lane == spot + per).astype(f32)
    )
    o_ref[...] = jnp.zeros(o_ref.shape, f32)
    o_ref[0, 0:height] = main
    o_ref[0, height : height + 1] = row
    o_ref[0, height + 1 : height + 2] = rates[0:1]
    o_ref[0, height + 2 : height + 3, 0:cols] = lb_ref[...]


def lag_kernel(sub, length, masks, n_parts, *refs):
    pieces, refs = refs[:n_parts], refs[n_parts:]
    f_ref, kh_ref, vec_ref, w_ref, term_ref, pow_ref, k_scr, z_scr, rhs_scr, kf_scr = refs
    slots = [piece.at[t] for piece in pieces for t in range(piece.shape[0])]
    ndp = len(slots)
    me = lax.axis_index("dp")
    n_w, lanes = w_ref.shape
    nstate = n_w // 2
    per = nstate // ndp
    groups = LANES // sub
    height = n_w // groups
    block = f_ref.shape[0] // 2
    group = iota((1, LANES), 1) // sub
    for u in range(groups):
        acc = jnp.zeros(slots[0].shape, f32)
        for t in range(ndp):
            i = me ^ masks[t]
            acc = jnp.where(group == i, pltpu.roll(slots[t][...], (i - u) * sub + LANES * ndp, 1), acc)
        w_ref[u * height : (u + 1) * height] = acc[0:height]
        if u < 4:
            vec_ref[u : u + 1] = acc[height : height + 1]
    vec_ref[4:8] = jnp.zeros((4, lanes), f32)
    rows = jnp.concatenate([slot[height + 1 : height + 2] for slot in slots], axis=0)
    source = jnp.zeros((nstate, ndp), i32)
    for t in range(ndp):
        source = jnp.where(iota((nstate, ndp), 1) == t, me ^ masks[t], source)
    spread = exact_dot((iota((nstate, ndp), 0) // per == source).astype(f32), rows)
    lane, state = iota((nstate, lanes), 1), iota((nstate, lanes), 0)
    lam = jnp.sum(jnp.where(lane == state % per, spread, 0.0), axis=1, keepdims=True)
    imag = jnp.sum(jnp.where(lane == state % per + per, spread, 0.0), axis=1, keepdims=True)
    terms = state_terms(lam, imag, vec_ref[0:1], float(length))
    for slot, value in enumerate(terms):
        term_ref[slot] = value
    z_scr[0], z_scr[1] = cmul(w_ref[0:nstate], w_ref[nstate:], terms[11], terms[12])
    for slot, pair in enumerate(power_table(terms[2], terms[3])):
        pow_ref[2 * slot], pow_ref[2 * slot + 1] = pair
    k_scr[...] = jnp.zeros_like(k_scr)

    def pair(m, _):
        ready = []
        for n in (2 * m, 2 * m + 1):
            fr, fi = rows8(pow_ref, n)
            cr = jnp.broadcast_to(z_scr[0, pl.ds(n, 1), :], (8, lanes))
            ci = jnp.broadcast_to(z_scr[1, pl.ds(n, 1), :], (8, lanes))
            ready.append([cmul(fr, fi, cr, ci), powers(pow_ref, n)])
        for u in range(DOCMAX // FINE // COARSE):
            for v in range(COARSE):
                at = (u * COARSE + v) * FINE
                total = k_scr[at : at + FINE]
                for (xr, xi), pows in ready:
                    total = total + (xr * pows[v][0] - xi * pows[v][1] if v else xr)
                k_scr[at : at + FINE] = total
            for one in ready:
                one[0] = cmul(*one[0], *one[1][COARSE])
        return 0

    lax.fori_loop(0, nstate // 2, pair, 0, unroll=2)
    k_scr[0:1] += vec_ref[1:2]
    parts = length // block
    for p in range(parts):
        stack3(rhs_scr, slice(p * lanes, (p + 1) * lanes), k_scr[p * block : (p + 1) * block])
    kf_scr[...] = dot(f_ref[...], rhs_scr[...])
    sign = signs(block, lanes)
    for p in range(parts):
        here, past = slice(p * lanes, (p + 1) * lanes), slice((p - 1) * lanes, p * lanes)
        re, im = kf_scr[:block, here], kf_scr[block:, here]
        if p:
            re = re - sign * kf_scr[block:, past]
            im = im + sign * kf_scr[:block, past]
        kh_ref[p, :block] = re * (1.0 / block)
        kh_ref[p, block:] = im * (1.0 / block)


def members(own, sub, c, width, wide):
    lane = iota((1, wide), 1)
    return (iota((width, wide), 0) == (lane // sub) * own + c * sub + lane % sub).astype(f32).astype(bf16)


STAT_ROWS = 16


def terms3(x):
    hi, rest = x.astype(bf16), x
    out = [hi]
    for _ in range(2):
        rest = rest - out[-1].astype(f32)
        out.append(rest.astype(bf16))
    return out


def spread_kernel(own, sub, x_any, *refs):
    *o_refs, x_ref, sems = refs
    count, block, width = x_ref.shape
    wide = o_refs[0].shape[-1]
    copies = [pltpu.make_async_copy(x_any.at[s], x_ref.at[s], sems.at[s]) for s in range(count)]
    for copy in copies:
        copy.start()
    places = [members(own, sub, lax.axis_index("seq") ^ d, width, wide) for d in range(len(o_refs))]
    eye = (iota((block, block), 0) == iota((block, block), 1)).astype(f32).astype(bf16)
    lane = iota((block, LANES), 1)
    for s in range(count):
        copies[s].wait()
        for o_ref, cols in zip(o_refs, places):
            o_ref[s, 0:block] = dot(x_ref[s], cols).astype(bf16)
        x = x_ref[s].astype(f32)
        mean = jnp.mean(x, axis=-1, keepdims=True)
        centre = x - mean
        inv = lax.rsqrt(jnp.mean(centre * centre, axis=-1, keepdims=True) + ln_eps)
        table = jnp.zeros((block, LANES), f32)
        for k, term in enumerate(terms3(mean) + terms3(inv)):
            table = jnp.where(lane == k, term.astype(f32), table)
        turned = dot(table.astype(bf16), eye, TN)
        both = jnp.concatenate([turned[0:8, 0:LANES], turned[0:8, LANES:]], axis=0).astype(bf16)
        for o_ref in o_refs:
            o_ref[s, block:] = both


def normal_inputs(piece_ref, s, block):
    stats = piece_ref[s, block:]
    spot, lane = iota((STAT_ROWS, 4 * LANES), 0), iota((STAT_ROWS, 4 * LANES), 1) // LANES
    first = lane // 2 * 8 + lane % 2 * 3
    pick = ((spot >= first) & (spot < first + 3)).astype(f32).astype(bf16)
    cols = dot(stats, pick, TN)
    parts = []
    for half in (0, 1):
        rows = piece_ref[s, half * LANES : (half + 1) * LANES].astype(f32)
        at = 2 * half * LANES
        parts.append((rows - cols[:, at : at + LANES]) * cols[:, at + LANES : at + 2 * LANES])
    return jnp.concatenate(parts, axis=0)


def ln_back_kernel(own, sub, g0, g1, g2, g3, x_ref, c_ref, o_ref):
    count, block, width = x_ref.shape
    wide = g0.shape[-1]
    tokens = count * block
    g = jnp.zeros((tokens, width), f32)
    for d, g_ref in enumerate((g0, g1, g2, g3)):
        cols = members(own, sub, lax.axis_index("seq") ^ d, width, wide)
        g = g + dot(g_ref[...].reshape(tokens, wide), cols, NT)
    x = x_ref[...].astype(f32).reshape(tokens, width)
    centre = x - jnp.mean(x, axis=-1, keepdims=True)
    inv = lax.rsqrt(jnp.mean(centre * centre, axis=-1, keepdims=True) + ln_eps)
    hat = centre * inv
    mean_g = jnp.mean(g, axis=-1, keepdims=True)
    mean_gx = jnp.mean(g * hat, axis=-1, keepdims=True)
    cot = c_ref[...].astype(f32).reshape(tokens, width)
    o_ref[...] = (cot + inv * (g - mean_g - hat * mean_gx)).astype(bf16).reshape(o_ref.shape)


def segments(len_ref, cut_ref, block, parts):
    count, docs = len_ref.shape
    last = parts + docs - 1
    for s in range(count):
        ends = []
        for d in range(docs - 1):
            ends.append(len_ref[s, d] + (ends[-1] if ends else 0))
        cut_ref[s, 0] = 0
        cut_ref[s, last] = parts * block
        for d, end in enumerate(ends):
            rank = 1 + d
            for k in range(1, parts):
                rank = rank + jnp.where(end > k * block, 1, 0)
            cut_ref[s, rank] = end
        for k in range(1, parts):
            rank = k
            for end in ends:
                rank = rank + jnp.where(end <= k * block, 1, 0)
            cut_ref[s, rank] = k * block


def document(len_ref, s, at):
    start, end, total = 0, 0, 0
    for d in range(len_ref.shape[1]):
        total = total + len_ref[s, d]
        start = jnp.where(total <= at, total, start)
    total = 0
    end = 1 << 30
    for d in range(len_ref.shape[1]):
        total = total + len_ref[s, d]
        end = jnp.minimum(end, jnp.where(total > at, total, 1 << 30))
    return start, end


def within(cut_ref, s, j, block, lanes):
    start, end = cut_ref[s, j], cut_ref[s, j + 1]
    b = start // block
    rows = b * block + iota((block, lanes), 0)
    return b, (rows >= start) & (rows < end)


def column(j, s, count, lanes):
    return pl.ds(pl.multiple_of((j * count + s) * lanes, lanes), lanes)


CHUNK = 64


def lengths_in(len_ref, len_scr, sem):
    copy = pltpu.make_async_copy(len_ref, len_scr, sem)
    copy.start()
    copy.wait()


def split_rows(y_scr, rows, cols, value, block, half):
    hi, lo = halves(value)
    for third, part in enumerate((hi, lo, hi)[: y_scr.shape[0] // (2 * block)]):
        at = (2 * third + half) * block
        y_scr[at + rows.start : at + rows.stop, cols] = part


def row_chunks(block):
    for r in range(0, block, CHUNK):
        yield slice(r, r + CHUNK), slice(block + r, block + r + CHUNK)


def conv_kernel(x0, x1, x2, x3, len_ref, vec_ref, kh_ref, f_ref, ft_ref,
                o0, o1, o2, o3, s_scr, x_scr, len_scr, cut_ref, rhs_scr, acc_scr, y_scr, out_scr, sem):
    count, parts, block, lanes = x_scr.shape
    me = lax.axis_index("seq")
    lengths_in(len_ref, len_scr, sem)
    for d, x_ref in enumerate((x0, x1, x2, x3)):
        for s in range(count):
            x_scr[s, me ^ d] = normal_inputs(x_ref, s, block)
    segments(len_scr, cut_ref, block, parts)
    gain, bias = vec_ref[2:3], vec_ref[3:4]
    items = cut_ref.shape[1] - 1
    for j in range(items):
        for s in range(count):
            b, keep = within(cut_ref, s, j, block, lanes)
            cols = slice((j * count + s) * lanes, (j * count + s + 1) * lanes)
            stack3(rhs_scr, cols, jnp.where(keep, x_scr[s, b] * gain + bias, 0.0))
        tile = slice(j * count * lanes, (j + 1) * count * lanes)
        s_scr[:, tile] = dot(f_ref[...], rhs_scr[:, tile])

    def own(j, _):
        for s in range(count):
            cols = column(j, s, count, lanes)
            for re, im in row_chunks(block):
                acc_scr[re, cols], acc_scr[im, cols] = cmul(
                    kh_ref[0, re], kh_ref[0, im], s_scr[re, cols], s_scr[im, cols]
                )
            start, _ = document(len_scr, s, cut_ref[s, j])
            b = cut_ref[s, j] // block
            first = j
            for i in range(items):
                first = first - jnp.where((i < j) & (cut_ref[s, i] >= start), 1, 0)

            def add(i, _):
                p = b - cut_ref[s, i] // block
                there = column(i, s, count, lanes)
                for re, im in row_chunks(block):
                    more = cmul(kh_ref[p, re], kh_ref[p, im], s_scr[re, there], s_scr[im, there])
                    acc_scr[re, cols] += more[0]
                    acc_scr[im, cols] += more[1]
                return 0

            lax.fori_loop(first, j, add, 0)
            for re, im in row_chunks(block):
                split_rows(y_scr, re, cols, acc_scr[re, cols], block, 0)
                split_rows(y_scr, re, cols, acc_scr[im, cols], block, 1)
        return 0

    lax.fori_loop(0, items, own, 0)
    acc_scr[0:block] = dot(ft_ref[:, 0 : y_scr.shape[0]], y_scr[...])
    for j in range(items):
        for s in range(count):
            b, keep = within(cut_ref, s, j, block, lanes)
            cols = slice((j * count + s) * lanes, (j * count + s + 1) * lanes)
            out_scr[s, b] = jnp.where(keep, acc_scr[0:block, cols], out_scr[s, b])
    for d, o_ref in enumerate((o0, o1, o2, o3)):
        for s in range(count):
            o_ref[s] = out_scr[s, me ^ d].astype(bf16)


def back_kernel(c0, c1, c2, c3, x_scr, len_ref, s_scr, vec_ref, kh_ref, f_ref, ft_ref,
                g0, g1, g2, g3, dkh_ref, dvec_ref,
                len_scr, cut_ref, v_scr, rhs_scr, sv_scr, acc_scr, y_scr, du_scr, sem):
    count, block, lanes = c0.shape
    parts = kh_ref.shape[0]
    me = lax.axis_index("seq")
    lengths_in(len_ref, len_scr, sem)
    for d, c_ref in enumerate((c0, c1, c2, c3)):
        for s in range(count):
            v_scr[s, me ^ d] = c_ref[s]
    dkh_ref[...] = jnp.zeros_like(dkh_ref)
    segments(len_scr, cut_ref, block, parts)
    items = cut_ref.shape[1] - 1
    for j in range(items):
        for s in range(count):
            b, keep = within(cut_ref, s, j, block, lanes)
            v = jnp.where(keep, v_scr[s, b].astype(f32), 0.0).astype(bf16)
            cols = slice((j * count + s) * lanes, (j * count + s + 1) * lanes)
            rhs_scr[:, cols] = v
        tile = slice(j * count * lanes, (j + 1) * count * lanes)
        sv_scr[:, tile] = dot(f_ref[:, 0:block], rhs_scr[:, tile])

    def own(j, _):
        for s in range(count):
            cols = column(j, s, count, lanes)
            for re, im in row_chunks(block):
                vr, vi, ur, ui = sv_scr[re, cols], sv_scr[im, cols], s_scr[re, cols], s_scr[im, cols]
                kr, ki = kh_ref[0, re], kh_ref[0, im]
                acc_scr[re, cols] = kr * vr + ki * vi
                acc_scr[im, cols] = kr * vi - ki * vr
                dkh_ref[0, re] += vr * ur + vi * ui
                dkh_ref[0, im] += vi * ur - vr * ui
            _, end = document(len_scr, s, cut_ref[s, j])
            b = cut_ref[s, j] // block
            last = j
            for i in range(items):
                last = last + jnp.where((i > j) & (cut_ref[s, i] < end), 1, 0)

            def add(i, _):
                p = cut_ref[s, i] // block - b
                there = column(i, s, count, lanes)
                for re, im in row_chunks(block):
                    vr, vi, ur, ui = sv_scr[re, there], sv_scr[im, there], s_scr[re, cols], s_scr[im, cols]
                    kr, ki = kh_ref[p, re], kh_ref[p, im]
                    acc_scr[re, cols] += kr * vr + ki * vi
                    acc_scr[im, cols] += kr * vi - ki * vr
                    dkh_ref[p, re] += vr * ur + vi * ui
                    dkh_ref[p, im] += vi * ur - vr * ui
                return 0

            lax.fori_loop(j + 1, last + 1, add, 0)
            for re, im in row_chunks(block):
                split_rows(y_scr, re, cols, acc_scr[re, cols], block, 0)
                split_rows(y_scr, re, cols, acc_scr[im, cols], block, 1)
        return 0

    lax.fori_loop(0, items, own, 0)
    acc_scr[0:block] = dot(ft_ref[:, 0 : y_scr.shape[0]], y_scr[...])
    for j in range(items):
        for s in range(count):
            b, keep = within(cut_ref, s, j, block, lanes)
            cols = slice((j * count + s) * lanes, (j * count + s + 1) * lanes)
            du_scr[s, b] = jnp.where(keep, acc_scr[0:block, cols], du_scr[s, b])
    gain = vec_ref[2:3]
    d_gain = jnp.zeros((8, lanes), f32)
    d_bias = jnp.zeros((8, lanes), f32)
    for d, g_ref in enumerate((g0, g1, g2, g3)):
        for s in range(count):
            for r in range(0, block, CHUNK):
                du = du_scr[s, me ^ d, r : r + CHUNK]
                d_bias += jnp.sum(du.reshape(CHUNK // 8, 8, lanes), axis=0)
                d_gain += jnp.sum((du * x_scr[s, me ^ d, r : r + CHUNK]).reshape(CHUNK // 8, 8, lanes), axis=0)
                g_ref[s, r : r + CHUNK] = (du * gain).astype(bf16)
    dvec_ref[0:1] = jnp.sum(d_gain, axis=0, keepdims=True)
    dvec_ref[1:2] = jnp.sum(d_bias, axis=0, keepdims=True)
    dvec_ref[2:3] = vec_ref[0:1]


def normal_cdf(v, bell):
    t = 1.0 / (1.0 + np.float32(0.3275911 / np.sqrt(2.0)) * jnp.abs(v))
    tail = t * (0.127414796 + t * (-0.142248368 + t * (0.7107068705 + t * (-0.7265760135 + t * 0.5307027145)))) * bell
    return jnp.where(v < 0.0, tail, 1.0 - tail)


def dense_kernel(q0, q1, q2, q3, x_any, c_any, w_ref, lb_ref,
                 out_ref, dlb_ref, d0, d1, d2, d3, stay_ref, send_ref,
                 x_ref, c_ref, act_ref, dpre_ref, slope_scr, pre_scr, dact_scr, sems):
    count, block, wide = q0.shape
    width = act_ref.shape[1]
    me = lax.axis_index("seq")
    copies = [pltpu.make_async_copy(x_any, x_ref, sems.at[0]), pltpu.make_async_copy(c_any, c_ref, sems.at[1])]
    for copy in copies:
        copy.start()

    def cols_of(d):
        return pl.ds(pl.multiple_of((me ^ d) * wide, wide), wide)

    def sequence(s, lb_sum):
        def slope(r, _):
            rows = pl.ds(pl.multiple_of(r * CHUNK, CHUNK), CHUNK)
            flat = pl.ds(pl.multiple_of(s * block + r * CHUNK, CHUNK), CHUNK)
            for d, q_ref in enumerate((q0, q1, q2, q3)):
                v = q_ref[s, rows].astype(f32)
                bell = jnp.exp(-0.5 * v * v)
                cdf = normal_cdf(v, bell)
                act_ref[flat, cols_of(d)] = (v * cdf).astype(bf16)
                slope_scr[rows, cols_of(d)] = cdf + v * (bell * np.float32(1.0 / np.sqrt(2.0 * np.pi)))
            return 0

        lax.fori_loop(0, block // CHUNK, slope, 0)
        whole = pl.ds(pl.multiple_of(s * block, block), block)
        pre_scr[...] = dot(act_ref[whole, :], w_ref[...])

        @pl.when(s == 0)
        def _():
            for copy in copies:
                copy.wait()

        def gate(r, total):
            rows = pl.ds(pl.multiple_of(r * 32, 32), 32)
            flat = pl.ds(pl.multiple_of(s * block + r * 32, 32), 32)
            first = pre_scr[rows, 0:width] + lb_ref[:, 0:width]
            sig = 1.0 / (1.0 + jnp.exp(-(pre_scr[rows, width:] + lb_ref[:, width:])))
            out_ref[s, rows] = (x_ref[s, rows].astype(f32) + first * sig).astype(bf16)
            d_first = c_ref[s, rows].astype(f32) * sig
            d_second = d_first * first * (1.0 - sig)
            d_pre = jnp.concatenate([d_first, d_second], axis=1).astype(bf16)
            dpre_ref[flat, :] = d_pre
            return total + jnp.sum(d_pre.astype(f32).reshape(4, 8, 2 * width), axis=0)

        lb_sum = lax.fori_loop(0, block // 32, gate, lb_sum)
        dact_scr[...] = dot(dpre_ref[whole, :], w_ref[...], NT)
        for d, o_ref in enumerate((d0, d1, d2, d3)):
            o_ref[s] = (dact_scr[:, cols_of(d)] * slope_scr[:, cols_of(d)]).astype(bf16)
        return lb_sum

    lb_sum = lax.fori_loop(0, count, sequence, jnp.zeros((8, 2 * width), f32))
    dlb_ref[...] = jnp.sum(lb_sum, axis=0, keepdims=True)
    for d in range(4):
        (send_ref if d & 1 else stay_ref)[d // 2] = dot(act_ref[:, cols_of(d)], dpre_ref[...], TN).astype(bf16)


def rows_kernel(sub, nseq, masks, shared_ref, *refs):
    *w_refs, o_ref, lb_ref = refs
    cols = w_refs[0].shape[-1]
    span = o_ref.shape[0] // nseq
    me = lax.axis_index("dp")
    bias_row = shared_ref.shape[1] - 8 + 2
    for t, mask in enumerate(masks):
        at = pl.ds(pl.multiple_of((me ^ mask) * cols, cols), cols)
        lb_ref[:, at] = shared_ref[t, bias_row : bias_row + 1, 0:cols]
    t = 0
    for w_ref in w_refs:
        for slot in range(w_ref.shape[0]):
            at = pl.ds(pl.multiple_of((me ^ masks[t]) * cols, cols), cols)
            t += 1
            for c in range(nseq):
                for i in range(span // sub):
                    o_ref[c * span + i * sub : c * span + (i + 1) * sub, at] = w_ref[
                        slot, (i * nseq + c) * sub : (i * nseq + c + 1) * sub
                    ]


def halve_kernel(mine_ref, other_ref, stay_ref, send_ref):
    for k in range(mine_ref.shape[0]):
        total = mine_ref[k].astype(f32) + other_ref[k].astype(f32)
        (send_ref if k & 1 else stay_ref)[k // 2] = total.astype(stay_ref.dtype)


def deal_kernel(mine_ref, other_ref, stay_ref, send_ref):
    part = stay_ref.shape[2]
    me = lax.axis_index("dp")
    for d in range(2 * stay_ref.shape[0]):
        cols = pl.ds(pl.multiple_of((me ^ d) * part, part), part)
        (send_ref if d & 1 else stay_ref)[d // 2] = mine_ref[0, :, cols].astype(f32) + other_ref[0, :, cols].astype(f32)


def merge_kernel(x_ref, mine_ref, other_ref, o_ref):
    span = -(-x_ref.shape[1] // 32) * 32
    total = x_ref[0]
    for i in range(1, x_ref.shape[0]):
        total = total + x_ref[i]
    total = jnp.concatenate([total, jnp.zeros((span - total.shape[0], LANES), f32)], axis=0)
    for k, term in enumerate(terms3(total)):
        o_ref[k * span : (k + 1) * span] = term
    o_ref[3 * span :] = (mine_ref[0] + other_ref[0]).astype(bf16)


PAIR = 2 * FINE


def power_kernel(pow_ref, o_ref):
    def some(g, _):
        rows = pl.ds(pl.multiple_of(g * 8, 8), 8)
        at = [2 * POWERS.index(PAIR * v) for v in range(1, COARSE // 2 + 1)]
        small = [(pow_ref[i, rows], pow_ref[i + 1, rows]) for i in at]
        x = jnp.ones((8, LANES), f32), jnp.zeros((8, LANES), f32)
        for u in range(DOCMAX // PAIR // (COARSE // 2)):
            for v in range(COARSE // 2):
                m = u * (COARSE // 2) + v
                o_ref[2 * m, rows], o_ref[2 * m + 1, rows] = cmul(*x, *small[v - 1]) if v else x
            x = cmul(*x, *small[-1])
        return 0

    lax.fori_loop(0, pow_ref.shape[1] // 8, some, 0)


CHAINS = 2


def state_grad_kernel(sub, length, w_ref, term_ref, pow_ref, far_ref, dkh_ref, dvec_ref, dlb_ref, ft_ref, o_ref,
                      dk_scr, f_scr, dw_scr, y_scr):
    ndp = o_ref.shape[0]
    n_w, lanes = w_ref.shape
    nstate = n_w // 2
    per = nstate // ndp
    groups = LANES // sub
    height = n_w // groups
    parts, twice, _ = dkh_ref.shape
    block = twice // 2
    sign = signs(block, lanes)
    for p in range(parts):
        re, im = dkh_ref[p, :block], dkh_ref[p, block:]
        if p + 1 < parts:
            re = re + sign * dkh_ref[p + 1, block:]
            im = im - sign * dkh_ref[p + 1, :block]
        stack3(y_scr, slice(p * lanes, (p + 1) * lanes), jnp.concatenate([re, im], axis=0))
    all_lags = dot(ft_ref[...], y_scr[...]) * (1.0 / block)
    for p in range(parts):
        dk_scr[p * block : (p + 1) * block] = all_lags[:, p * lanes : (p + 1) * lanes]
    at8 = iota((8, lanes), 0).astype(f32)

    def one(n, _):
        fr, fi = rows8(pow_ref, n)
        zero = jnp.zeros((8, lanes), f32)
        span = DOCMAX // PAIR // CHAINS
        sums = []
        for c in range(CHAINS):
            acc = [[zero] * 4, [zero] * 4]
            for m in range(c * span + span - 1, c * span - 1, -1):
                if m:
                    p_re = jnp.broadcast_to(far_ref[2 * m, pl.ds(n, 1), :], (8, lanes))
                    p_im = jnp.broadcast_to(far_ref[2 * m + 1, pl.ds(n, 1), :], (8, lanes))
                for h, one_acc in enumerate(acc):
                    at = m * PAIR + h * FINE
                    dk = dk_scr[at : at + FINE]
                    one_acc[0] = one_acc[0] + (dk * p_re if m else dk)
                    if m:
                        one_acc[1] = one_acc[1] + dk * p_im
                    if m > c * span:
                        one_acc[2], one_acc[3] = one_acc[2] + one_acc[0], one_acc[3] + one_acc[1]
            for one_acc in acc:
                one_acc[2], one_acc[3] = (one_acc[2 + k] + (c * span) * one_acc[k] for k in (0, 1))
            sums.append(acc)
        low, high = (
            [sum((acc[h][k] for acc in sums[1:]), sums[0][h][k]) for k in range(4)] for h in (0, 1)
        )
        for h, part in enumerate((low, high)):
            for k in (0, 1):
                part[2 + k] = PAIR * part[2 + k] + (at8 + float(h * FINE)) * part[k]
        shift = wide_row(pow_ref, FINE, 0, n), wide_row(pow_ref, FINE, 1, n)
        values = []
        for k in (0, 2):
            up = cmul(high[k], high[k + 1], *shift)
            values.append(cmul(low[k] + up[0], low[k + 1] + up[1], fr, fi))
        (s_re, s_im), (m_re, m_im) = values
        for slot, value in enumerate((s_re, s_im, m_re, m_im)):
            f_scr[slot, pl.ds(n, 1), :] = jnp.sum(value, axis=0, keepdims=True)
        return 0

    lax.fori_loop(0, nstate, one, 0, unroll=2)
    a, b, z_re, z_im, one_re, one_im, far_re, far_im, den_re, den_im, inv, g_re, g_im = (
        term_ref[slot] for slot in range(TERMS)
    )
    f0, f1 = (f_scr[0], f_scr[1]), (f_scr[2], f_scr[3])
    gf_re, gf_im = cmul(g_re, g_im, *f0)
    dw_scr[0:nstate] = gf_re
    dw_scr[nstate:] = -gf_im
    inv_one = 1.0 / (one_re * one_re + one_im * one_im)
    near_re, near_im = cmul(z_re, z_im, one_re * inv_one, -one_im * inv_one)
    far_re, far_im = cmul(far_re, far_im, den_re * inv, -den_im * inv)
    q_re, q_im = cmul(length * far_re - near_re, length * far_im - near_im, *f0)
    c_re, c_im = cmul(w_ref[0:nstate], w_ref[nstate:], g_re, g_im)
    y_re, y_im = cmul(c_re, c_im, q_re + f1[0], q_im + f1[1])
    by_a = a * y_re
    by_step = by_a - b * y_im
    step = jnp.exp(dvec_ref[2:3])
    by_imag = -step * y_im
    d_step = jnp.sum(by_step, axis=0, keepdims=True)
    lane, state = iota((nstate, lanes), 1), iota((nstate, lanes), 0)
    col_a = jnp.sum(by_a, axis=1, keepdims=True)
    col_b = jnp.sum(by_imag, axis=1, keepdims=True)
    grid = jnp.where(lane == state % per, col_a, jnp.where(lane == state % per + per, col_b, 0.0))
    rates = exact_dot((iota((ndp, nstate), 0) == iota((ndp, nstate), 1) // per).astype(f32), grid)
    vecs = (d_step, dk_scr[0:1], dvec_ref[0:1], dvec_ref[1:2])
    group = iota((1, LANES), 1) // sub
    cols = dlb_ref.shape[1] // ndp
    for i in range(ndp):
        main = jnp.zeros((height, LANES), f32)
        row = jnp.zeros((1, LANES), f32)
        for u in range(groups):
            main = jnp.where(group == u, moved(dw_scr[u * height : (u + 1) * height], (u - i) * sub), main)
            if u < 4:
                row = jnp.where(group == u, moved(jnp.broadcast_to(vecs[u], (8, LANES)), (u - i) * sub)[0:1], row)
        o_ref[i] = jnp.zeros(o_ref.shape[1:], f32)
        o_ref[i, 0:height] = main
        o_ref[i, height : height + 1] = row
        o_ref[i, height + 1 : height + 2] = rates[i : i + 1]
        o_ref[i, height + 2 : height + 3, 0:cols] = dlb_ref[:, i * cols : (i + 1) * cols]


def sum_kernel(x_ref, o_ref):
    total = x_ref[0].astype(f32)
    for i in range(1, x_ref.shape[0]):
        total = total + x_ref[i].astype(f32)
    o_ref[...] = total.astype(o_ref.dtype)


def last_kernel(sub, rows, *refs):
    *parts, w_ref, step_ref, skip_ref, gain_ref, bias_ref, lam_ref, imag_ref, lb_ref, dw_ref = refs
    n_w, own = w_ref.shape
    nseq = LANES * own // sub // LANES
    parts, dws = parts[:nseq], parts[nseq:]
    groups = LANES // sub
    height = n_w // groups
    per, cols = lam_ref.shape[1], lb_ref.shape[1]
    group = iota((1, LANES), 1) // sub
    me = lax.axis_index("seq")
    merged = not dws
    if merged:
        span = -(-rows // 32) * 32
        small = [sum(part[k * span : k * span + rows].astype(f32) for k in range(3)) for part in parts]
    else:
        small = [part[0:rows] for part in parts]
    for u in range(groups):
        acc = jnp.zeros((rows, LANES), f32)
        for d, value in enumerate(small):
            c = me ^ d
            acc = jnp.where(group == c, pltpu.roll(value, (c - u) * sub + LANES, 1), acc)
        w_ref[u * height : (u + 1) * height] = acc[0:height, 0:own]
        if u < 4:
            (step_ref, skip_ref, gain_ref, bias_ref)[u][...] = acc[height : height + 1, 0:own]
    total = sum(small[1:], small[0])
    lam_ref[...] = total[height + 1 : height + 2, 0:per]
    imag_ref[...] = pltpu.roll(total, LANES - per, 1)[height + 1 : height + 2, 0:per]
    lb_ref[...] = total[height + 2 : height + 3, 0:cols]
    for d in range(nseq):
        part_ref, first = (parts[d], 3 * span) if merged else (dws[d], 0)
        c = me ^ d
        for i in range((part_ref.shape[0] - first) // sub):
            at = pl.multiple_of((i * nseq + c) * sub, sub)
            dw_ref[pl.ds(at, sub)] = part_ref[first + i * sub : first + (i + 1) * sub].astype(f32)


def swap(x, axis, by):
    n = lax.axis_size(axis)
    return jax.tree.map(lambda v: lax.ppermute(v, axis, [(i, i ^ by) for i in range(n)]), x)


def trade(parts, axis):
    return [parts[0]] + [swap(parts[d], axis, d) for d in range(1, len(parts))]


def tie(*values):
    return lax.optimization_barrier(values)


def on_device(block_in, cotangent, ln_gain, ln_bias, lambda_log, lambda_imag, dss_weight, log_step, skip_gain,
              lin_weight, lin_bias, doc_lengths):
    ndp, nseq = lax.axis_size("dp"), lax.axis_size("seq")
    count, block, width = block_in.shape
    length = block * nseq
    own = ln_gain.shape[0]
    sub = own // nseq
    wide = width // nseq
    per = lambda_log.shape[0]
    nstate = per * ndp
    n_w = 2 * nstate
    cols = lin_weight.shape[1]
    tokens = count * block
    height = n_w * sub // LANES
    rows = height + 8
    steps = [1 << k for k in reversed(range(ndp.bit_length() - 1))]
    masks = [0]
    for step in steps:
        masks += [mask ^ step for mask in masks]

    def row(v):
        return v.reshape(1, -1)

    packed = call(partial(pack_kernel, sub), shape((1, rows, LANES)), [VM] * 8, name="pack", mib=60, us=2)(
        dss_weight.reshape(n_w, own), row(log_step), row(skip_gain), row(ln_gain), row(ln_bias),
        row(lambda_log), row(lambda_imag), row(lin_bias)
    )

    piece = shape((count, block, wide), bf16)
    shared, shared_parts = packed, [packed]
    w_slots = [lin_weight[None]]
    f_table, ft_table = dft_tables(block)
    w_more = hats = None
    for number, step in enumerate(steps):
        more = swap(shared, "dp", step)
        if number == 0:
            x_late, _ = tie(block_in, shared)
            hats = call(
                partial(spread_kernel, own, sub), [shape((count, block + STAT_ROWS, wide), bf16)] * nseq, [AN],
                scratch=[pltpu.VMEM((count, block, width), bf16), DMA((count,))], name="spread", us=2,
            )(x_late)
            more, *_ = tie(more, *hats)
        if number == 1:
            hats = trade(hats, "seq")
            more, _ = tie(more, hats[1])
        if number == 2:
            w_more = swap(w_slots[0], "dp", steps[0])
        shared_parts.append(more)
        if number < len(steps) - 1:
            shared = jnp.concatenate([shared, more], axis=0)

    spec = (nseq, 2 * block, wide)
    kh, vec, w_all, terms, pows = call(
        partial(lag_kernel, sub, length, masks, len(shared_parts)),
        [shape(spec), shape((8, wide)), shape((n_w, wide)), shape((TERMS, nstate, wide)),
         shape((2 * len(POWERS), nstate, wide))],
        [VM] * (len(shared_parts) + 1),
        scratch=[pltpu.VMEM((length, wide), f32), pltpu.VMEM((2, nstate, wide), f32),
                 pltpu.VMEM((3 * block, nseq * wide), bf16), pltpu.VMEM((2 * block, nseq * wide), f32)],
        name="lag_kernel", us=0, keep=[ft_table, block_in, cotangent],
    )(*shared_parts, f_table)

    kh, w_more = tie(kh, w_more)
    w_late = jnp.concatenate([w_slots[0], w_more], axis=0)
    ahead = steps[1:]
    if len(ahead) == 2:
        w_slots = [w_late, swap(w_late, "dp", ahead[0]), swap(w_late, "dp", ahead[1])]
    else:
        w_slots = [w_late]
        for step in ahead:
            w_slots = [jnp.concatenate(w_slots + [swap(slot, "dp", step) for slot in w_slots], axis=0)]

    blocks4 = (count, nseq, block, wide)
    items = nseq + doc_lengths.shape[1] - 1
    lens = pltpu.SMEM(doc_lengths.shape, i32)
    cuts = pltpu.SMEM((count, items + 1), i32)
    across = items * count * wide
    *convs, spectra_u, x_blocks = call(
        conv_kernel, [piece] * nseq + [shape((2 * block, across)), shape(blocks4)],
        [VM] * nseq + [AN] + [VM] * 4,
        scratch=[lens, cuts, pltpu.VMEM((3 * block, across), bf16), pltpu.VMEM((2 * block, across), f32),
                 pltpu.VMEM((6 * block, across), bf16), pltpu.VMEM(blocks4, f32), DMA],
        name="doc_conv", mib=20, us=7, keep=[w_all, terms, pows, block_in, cotangent],
    )(*hats, doc_lengths, vec, kh, f_table, ft_table)
    keep = [w_all, terms, pows, vec, kh, f_table, ft_table, spectra_u, x_blocks]
    if len(ahead) == 2:
        *convs, w_slots[1], w_slots[2] = tie(*convs, w_slots[1], w_slots[2])
    convs = trade(convs, "seq")
    if len(ahead) == 2:
        w_slots.append(swap(w_slots[1], "dp", ahead[1]))
    pows_late, _ = tie(pows, convs[1])
    far = call(power_kernel, shape((2 * DOCMAX // PAIR, nstate, wide)), [VM], name="state_powers", mib=16, us=1, keep=keep)(pows_late)
    convs[2], _ = tie(convs[2], far)
    keep.append(far)
    if cols % LANES == 0 and sub % 16 == 0:
        shared = jnp.concatenate([shared, shared_parts[-1]], axis=0)
        shared, convs[1] = tie(shared, convs[1])
        w_lin, bias_full = call(
            partial(rows_kernel, sub, nseq, masks), [shape((width, 2 * width), bf16), shape((1, 2 * width))],
            [VM] * (1 + len(w_slots)), name="linear_rows", us=1, keep=keep,
        )(shared, *w_slots)
    else:
        shared = jnp.concatenate([shared, shared_parts[-1]], axis=0)
        place = jnp.asarray([masks.index(i) for i in range(ndp)])[lax.axis_index("dp") ^ jnp.arange(ndp)]
        w_lin = jnp.take(jnp.concatenate(w_slots, axis=0), place, axis=0)
        w_lin = w_lin.reshape(ndp, ndp, nseq, sub, cols).transpose(2, 1, 3, 0, 4).reshape(width, 2 * width)
        bias_full = jnp.take(shared[:, height + 2, :cols], place, axis=0).reshape(1, 2 * width)

    group = shape((2, wide, 2 * width), bf16)
    block_out, d_lin_bias, *d_convs, stay, send = call(
        dense_kernel,
        [shape((count, block, width), bf16), shape((1, 2 * width))] + [piece] * nseq + [group] * 2,
        [VM] * nseq + [AN, AN, VM, VM],
        scratch=[pltpu.VMEM((count, block, width), bf16), pltpu.VMEM((count, block, width), bf16),
                 pltpu.VMEM((tokens, width), bf16), pltpu.VMEM((tokens, 2 * width), bf16),
                 pltpu.VMEM((block, width), f32), pltpu.VMEM((block, 2 * width), f32), pltpu.VMEM((block, width), f32), DMA((2,))],
        name="gated_linear", mib=16, us=5, keep=keep,
    )(*convs, block_in, cotangent, w_lin, bias_full)
    d_convs = trade(d_convs, "seq")

    staged = cols % LANES == 0
    if staged:
        stay, send = call(
            halve_kernel, [shape((1, wide, 2 * width), bf16)] * 2, [VM, VM], name="weight_half", keep=keep
        )(stay, swap(send, "seq", 1))
        d_convs[2], *_ = tie(d_convs[2], send)
        dw_other = swap(send, "seq", 2)
    else:
        full = jnp.stack([stay[0], send[0], stay[1], send[1]])
        full = full.reshape(nseq, wide, ndp, cols).transpose(2, 0, 1, 3)
        dw_own = jnp.sum(lax.all_to_all(full, "dp", 0, 0, tiled=True).astype(f32), axis=0)
        dw_own = sum(trade([dw_own[d] for d in range(nseq)], "seq"))

    out = call(
        back_kernel, [piece] * nseq + [shape(spec), shape((3, wide))],
        [VM] * (nseq + 1) + [AN] + [VM] * 5,
        scratch=[lens, cuts, pltpu.VMEM(blocks4, bf16), pltpu.VMEM((block, across), bf16),
                 pltpu.VMEM((2 * block, across), f32), pltpu.VMEM((2 * block, across), f32),
                 pltpu.VMEM((4 * block, across), bf16), pltpu.VMEM(blocks4, f32), DMA],
        name="doc_conv_grad", mib=24, us=8, keep=[w_all, terms, pows, far],
    )(*d_convs, x_blocks, doc_lengths, spectra_u, vec, kh, f_table, ft_table)
    g_own, dkh, d_norm = out[:nseq], out[nseq], out[nseq + 1]
    if staged:
        stay, send = call(
            deal_kernel, [shape((ndp // 2, wide, cols))] * 2, [VM, VM], name="weight_deal", us=1, keep=[w_all, terms, pows, far]
        )(stay, dw_other)
        dkh, *_ = tie(dkh, send)
        dw_other = swap(send, "dp", 1)

    small = call(
        partial(state_grad_kernel, sub, length), shape((ndp, rows, LANES)), [VM] * 8,
        scratch=[pltpu.VMEM((length, wide), f32), pltpu.VMEM((4, nstate, wide), f32), pltpu.VMEM((n_w, wide), f32),
                 pltpu.VMEM((6 * block, nseq * wide), bf16)],
        name="state_grad", mib=10, us=5,
    )(w_all, terms, pows, far, dkh, d_norm, d_lin_bias, ft_table)
    small, *g_own = tie(small, *g_own)
    if staged:
        small, dw_other = tie(small, dw_other)
    small = lax.all_to_all(small, "dp", 0, 0, tiled=True)
    gs = trade(g_own, "seq")
    if staged:
        step = 2
        while step < ndp:
            stay, send = call(
                halve_kernel, [shape((ndp // 2 // step, wide, cols))] * 2, [VM, VM], name="weight_half"
            )(stay, dw_other)
            dw_other = swap(send, "dp", step)
            step *= 2
    grad_in = call(
        partial(ln_back_kernel, own, sub), shape((count, block, width), bf16), [VM] * (nseq + 2),
        name="layer_norm_grad", mib=12,
    )(*gs, block_in, cotangent)
    if staged:
        merged = call(merge_kernel, shape((-(-rows // 32) * 96 + wide, cols), bf16), [VM] * 3, name="last_sums", us=0.5)(small, stay, dw_other)
        merged = trade([merged] * nseq, "seq")
        smalls, dws = merged, []
    else:
        small = call(sum_kernel, shape((rows, LANES)), [VM], name="small_sum", us=0.5)(small)
        smalls, dws = trade([small] * nseq, "seq"), trade([dw_own] * nseq, "seq")
    d_w, d_step, d_skip, d_gain, d_bias, d_lam, d_imag, d_lb, dw = call(
        partial(last_kernel, sub, rows),
        [shape((n_w, own))] + [shape((1, own))] * 4 + [shape((1, per))] * 2 + [shape((1, cols)), shape((width, cols))],
        [VM] * (len(smalls) + len(dws)), name="last", us=1,
    )(*smalls, *dws)
    return (
        block_out, grad_in, d_gain.reshape(own), d_bias.reshape(own), d_lam.reshape(per), d_imag.reshape(per),
        d_w.reshape(2, nstate, own), d_step.reshape(own), d_skip.reshape(own), dw, d_lb.reshape(cols),
    )


def solution(mesh):
    placed = (
        P("dp", "seq", None), P("dp", "seq", None), P("dp"), P("dp"), P("dp"), P("dp"),
        P(None, None, "dp"), P("dp"), P("dp"), P(None, "dp"), P("dp"), P("dp", None),
    )
    return jax.shard_map(
        on_device,
        mesh=mesh,
        in_specs=placed,
        out_specs=(
            P("dp", "seq", None), P("dp", "seq", None), P("dp"), P("dp"), P("dp"), P("dp"),
            P(None, None, "dp"), P("dp"), P("dp"), P(None, "dp"), P("dp"),
        ),
        check_vma=False,
    )
```
